1024 devices in a mesh: grp: 16 (over y, x), sub: 64 (over z, core).
Axes of the slice: x: 4, y: 4, z: 32, core: 2. Of those that a mesh axis runs over, the one named last changes fastest.
Arguments:
- populations: float32 [19, 128, 128, 384], P(None, 'sub', 'grp')
- heat_pops: float32 [7, 128, 128, 384], P(None, 'sub', 'grp')
- solid_frac: float32 [128, 128, 384], P('sub', 'grp'), may hold values from 0 to 0.5
- coupled_grid_point: int32 [16, 32768], P('grp', 'sub'), may hold values from 0 to 6143
- dest_index: int32 [16, 32768, 1], P('grp', 'sub'), may hold values from 0 to 63; in each aligned block of 512 rows (0 to 511, 512 to 1023, ..., all dimensions but the last counted through in order) at most 16 rows name the same one
- heat_coeff: float32 [16, 32768], P('grp', 'sub'), may hold values from 0.5 to 2
- slot_node: int32 [16, 65536], P('grp', 'sub'), may hold values from 0 to 1023
- node_diag: float32 [16, 512, 128], P('grp', 'sub'), may hold values from 2.5 to 5
- coupling: float32 [16, 512, 128, 128], P('grp', 'sub'), may hold values from 0 to 0.0078125
- block_pattern: int32 [16, 512], P('grp', 'sub'), may hold values from 0 to 7, as said below
- heat_source: float32 [16, 512, 128], P('grp', 'sub')
- solid_start: float32 [16, 512, 128], P('grp', 'sub'), may hold values from -6 to 6
Outputs:
- gas_hotness_after: float32 [128, 128, 384], P('sub', 'grp')
- gas_motion_amount: float32 [3, 128, 128, 384], P(None, 'sub', 'grp')
- solid_temp: float32 [16, 512, 128], P('grp', 'sub')
- fibre_surface_hotness: float32 [16, 32768], P('grp', 'sub')
The draws below stay inside these ranges and needn't reach their ends.
Inputs may be any that keep to these rules, and one draw needn't show every extreme that they name: `dest_index`: among one device's rows, no owner is named by more than 16 rows, a bound that some block reaches. `block_pattern`: on each device, block b's partner is (b + t) mod 8 for one shift t of 0 to 7 of that device, so every block is the partner of exactly one block.
All inputs are finite; a program needn't handle non-finite values.
Results may differ from the reference program's by a relative error of at most 0.0003.
Values sent between devices are 32-bit elements; how exact they have to be, the bound alone decides.
A program may use at most 64 MiB of HBM per device.

```python
import math
import jax
import jax.numpy as jnp
import numpy as np
from jax import lax

CX = 8
CY = 384
CZ = 2
NB = 8
CORE_MESH_PIECE = 128
ROWS_DEV = 512
STEPS = 2
ITERS = 2
LATERAL_BANDS = 16
SLABS = 64
NZ = 128
NX = 128
CAP = 16
COUPLED_ENTRIES = 32768
PIECES_PER_BAND = 512


flow_lift = np.array([0, 0, 0, 0, 0, 1, -1, 0, 0, 0, 0, 1, -1, -1, 1, 1, -1, -1, 1], dtype=np.float32)


lattice_share = np.array([1.0 / 3.0] + [1.0 / 18.0] * 6 + [1.0 / 36.0] * 12, dtype=np.float32)


thermal_share = np.array([0.25] + [0.125] * 6, dtype=np.float32)


def draw_populations(key, part):
    shape = (19, NZ, NX, CY)
    base = jax.random.uniform(key, shape, jnp.float32, 0.85, 1.15)
    lift = 0.15
    tilt = lift * jnp.asarray(flow_lift)[:, None, None, None]
    weights = jnp.asarray(lattice_share)[:, None, None, None]
    return (weights * (base + tilt)).astype(jnp.float32)


def draw_heat_pops(key, part):
    first = jax.random.fold_in(key, 11)
    second = jax.random.fold_in(key, 12)
    level = jax.random.uniform(first, (1, NZ, NX, CY), jnp.float32, 0.5, 1.5)
    rough = jax.random.uniform(second, (7, NZ, NX, CY), jnp.float32, 0.9, 1.1)
    return (jnp.asarray(thermal_share)[:, None, None, None] * level * rough).astype(jnp.float32)


def draw_heat_source(key, part):
    noise = jax.random.normal(key, (LATERAL_BANDS, PIECES_PER_BAND, CORE_MESH_PIECE), jnp.float32)
    device = jnp.arange(LATERAL_BANDS)[:, None] * SLABS + jnp.arange(PIECES_PER_BAND)[None, :] // NB
    frac = device.astype(jnp.float32) / (LATERAL_BANDS * SLABS - 1)
    scale = 3.0 ** frac
    return (scale[:, :, None] * noise).astype(jnp.float32)


def draw_block_pattern(key, part):
    shift = jax.random.randint(jax.random.fold_in(key, 21), (LATERAL_BANDS, SLABS, 1), 0, NB)
    blocks = jnp.arange(NB, dtype=jnp.int32)[None, None, :]
    return ((blocks + shift) % NB).reshape(LATERAL_BANDS, PIECES_PER_BAND).astype(jnp.int32)


def set_ends(values, own_key, smallest, largest):
    longest = values.shape.index(max(values.shape))
    spots = []
    for shift in (0, 1):
        where = [jax.random.randint(jax.random.fold_in(own_key, axis), (), 0, length) for axis, length in enumerate(values.shape)]
        where[longest] = (where[longest] + shift) % values.shape[longest]
        spots.append(tuple(where))
    return values.at[spots[0]].set(smallest).at[spots[1]].set(largest)


def shard_levels(rng, shape, shards, smallest, largest):
    loudness = 1.0
    for axis_at, shards_of in shards:
        draws = jax.random.uniform(jax.random.fold_in(jax.random.fold_in(rng, 6), axis_at), (shards_of,), jnp.float32, smallest / len(shards), largest / len(shards))
        loudness = loudness * jnp.repeat(jnp.exp(draws), shape[axis_at] // shards_of).reshape((-1,) + (1,) * (len(shape) - 1 - axis_at))
    return loudness


def routed_block(own_key, own, number, rows, count, top, bound, slope):
    sequence = jax.random.permutation(own_key, count)
    heavy_load, ordinary = shares(count, rows * top, bound, slope, True), shares(count, rows * top, bound, slope, False)
    places = jnp.arange(count)

    def named(lengths, offset_by):
        used = int((lengths > 0).sum())
        fixed = max(1, used // 4)
        shifted = fixed + (places - fixed + offset_by * (used - fixed)) % max(1, count - fixed)
        return jnp.zeros((count,), jnp.int32).at[sequence[jnp.where(places < fixed, places, shifted)]].set(jnp.asarray(lengths, jnp.int32))

    lengths = jnp.where(number % 4 == 0, named(heavy_load, number // 4), named(ordinary, number - number // 4 - 1))
    mixed = jax.random.permutation(jax.random.fold_in(own, 3), count)
    source_of, sink = mixed[0:count // 2 * 2:2], mixed[1:count // 2 * 2:2]
    slack = jnp.minimum(lengths[source_of] - 1, bound - lengths[sink]) // 2
    slack = jnp.where((source_of == sequence[0]) | (sink == sequence[0]) | (lengths[sink] == 0), 0, jnp.maximum(slack, 0))
    shifted = jax.random.randint(jax.random.fold_in(own, 4), (count // 2,), 0, 1 << 20) % (slack + 1)
    lengths = lengths.at[source_of].add(-shifted).at[sink].add(shifted)
    members = jnp.searchsorted(jnp.cumsum(lengths), jnp.arange(rows * top), side="right").astype(jnp.int32)
    listing = members.reshape(top, rows).T
    listing = listing[jax.random.permutation(jax.random.fold_in(own, 1), rows)]
    offset_by = jax.random.randint(jax.random.fold_in(own, 2), (rows, 1), 0, top)
    return jnp.take_along_axis(listing, (jnp.arange(top)[None, :] + offset_by) % top, axis=1)


def shares(amount, total, reach, slope, full):
    portions = [(1 << 20) // math.isqrt(standing ** slope) + 1 for standing in range(1, amount + 1)]
    largest = reach if full else min(reach, max(-(-total // amount), total * portions[0] // sum(portions)))
    least = 1 if total - largest >= amount - 1 else 0
    given, spare = [largest] + [least] * (amount - 1), total - largest - least * (amount - 1)
    while spare > 0:
        candidates = [i for i in range(1, amount) if given[i] < largest] or [i for i in range(1, amount) if given[i] < reach]
        whole, remaining = sum([portions[i] for i in candidates]), spare
        for i in candidates:
            extra = min(reach - given[i], max(1, remaining * portions[i] // whole), spare)
            given[i] = given[i] + extra
            spare = spare - extra
    return np.array(given)


def gaussian(rng, dims, width, most, pieces=(), kind=jnp.bfloat16):
    gain = shard_levels(rng, dims, pieces, -0.22, 0.18) if pieces else 1.0
    entries = jax.random.normal(rng, dims, jnp.float32) * width * gain
    return jnp.minimum(jnp.maximum(entries, -most), most).astype(kind)


def setup_inputs(seed: int = 0) -> dict:
    splits = jax.random.split(jax.random.key(seed), 13)
    populations = draw_populations(jax.random.fold_in(splits[12], 71), 0)
    heat_pops = draw_heat_pops(jax.random.fold_in(splits[12], 71), 0)
    solid_frac = jnp.clip(0.5 * jax.random.uniform(splits[2], (NZ, NX, CY), jnp.float32) ** shard_levels(splits[2], (NZ, NX, CY), ((0, 64), (1, 16)), -0.2, 0.2), 0.0, 0.5)
    coupled_grid_point = set_ends(jax.random.randint(splits[3], (LATERAL_BANDS, COUPLED_ENTRIES), 0, CZ * CX * CY), jax.random.fold_in(splits[3], 1), 0, (CZ * CX * CY) - 1).astype(jnp.int32)
    dest_index_keys = jax.random.split(jax.random.fold_in(splits[4], 1), LATERAL_BANDS * COUPLED_ENTRIES // ROWS_DEV)
    dest_index_turns = jax.random.permutation(jax.random.fold_in(splits[4], 3), LATERAL_BANDS * COUPLED_ENTRIES // ROWS_DEV)
    dest_index = jax.vmap(lambda own, number: routed_block(jax.random.fold_in(splits[4], 2), own, number, ROWS_DEV, SLABS, 1, CAP, 2))(dest_index_keys, dest_index_turns).reshape((LATERAL_BANDS, COUPLED_ENTRIES, 1))
    heat_coeff = jnp.clip(jnp.exp(math.log(2.0) - 1.3862944 * jax.random.uniform(splits[5], (LATERAL_BANDS, COUPLED_ENTRIES), jnp.float32) ** shard_levels(splits[5], (LATERAL_BANDS, COUPLED_ENTRIES), ((0, 16), (1, 64)), -0.2, 0.2)), 0.5, 2.0)
    slot_node = set_ends(jax.random.randint(splits[6], (LATERAL_BANDS, SLABS * SLABS * CAP), 0, NB * CORE_MESH_PIECE), jax.random.fold_in(splits[6], 1), 0, (NB * CORE_MESH_PIECE) - 1).astype(jnp.int32)
    node_diag = jnp.clip(2.5 + 2.5 * jax.random.uniform(splits[7], (LATERAL_BANDS, PIECES_PER_BAND, CORE_MESH_PIECE), jnp.float32) ** shard_levels(splits[7], (LATERAL_BANDS, PIECES_PER_BAND, CORE_MESH_PIECE), ((0, 16), (1, 64)), -0.2, 0.2), 2.5, 5.0)
    coupling = jnp.clip(0.0078125 * jax.random.uniform(splits[8], (LATERAL_BANDS, PIECES_PER_BAND, CORE_MESH_PIECE, CORE_MESH_PIECE), jnp.float32) ** shard_levels(splits[8], (LATERAL_BANDS, PIECES_PER_BAND, CORE_MESH_PIECE, CORE_MESH_PIECE), ((0, 16), (1, 64)), -0.2, 0.2), 0.0, 0.0078125)
    block_pattern = draw_block_pattern(jax.random.fold_in(splits[12], 71), 0)
    heat_source = draw_heat_source(jax.random.fold_in(splits[12], 71), 0)
    solid_start = gaussian(splits[11], (LATERAL_BANDS, PIECES_PER_BAND, CORE_MESH_PIECE), 1.0, 6.0, ((0, 16), (1, 64)), jnp.float32)
    return {"populations": populations, "heat_pops": heat_pops, "solid_frac": solid_frac, "coupled_grid_point": coupled_grid_point, "dest_index": dest_index, "heat_coeff": heat_coeff, "slot_node": slot_node, "node_diag": node_diag, "coupling": coupling, "block_pattern": block_pattern, "heat_source": heat_source, "solid_start": solid_start}


flow_velocity = np.array([[0, 0, 0], [1, 0, 0], [-1, 0, 0], [0, 1, 0], [0, -1, 0], [0, 0, 1], [0, 0, -1], [1, 1, 0], [-1, -1, 0], [1, -1, 0], [-1, 1, 0], [1, 0, 1], [-1, 0, -1], [1, 0, -1], [-1, 0, 1], [0, 1, 1], [0, -1, -1], [0, 1, -1], [0, -1, 1]], dtype=np.int32)
flow_weight = np.array([1.0 / 3.0] + [1.0 / 18.0] * 6 + [1.0 / 36.0] * 12)
flow_opposite = np.array([0, 2, 1, 4, 3, 6, 5, 8, 7, 10, 9, 12, 11, 14, 13, 16, 15, 18, 17], dtype=np.int32)
heat_velocity = flow_velocity[:7]
heat_weight = np.array([0.25] + [0.125] * 6)
tau_flow = 0.8
tau_heat = 0.7
highest = lax.Precision.HIGHEST


def flow_moments(flow):
    lattice = jnp.asarray(flow_velocity, flow.dtype)
    return jnp.tensordot(lattice, flow, axes=(0, 0), precision=highest)


def collide(flow, caloric_population, solidity):
    lattice = jnp.asarray(flow_velocity, flow.dtype)
    density = jnp.sum(flow, axis=0)
    velocity_field = flow_moments(flow) / density
    speed_square = jnp.sum(velocity_field * velocity_field, axis=0)
    projected = jnp.tensordot(lattice, velocity_field, axes=(1, 0), precision=highest)
    weights = jnp.asarray(flow_weight, flow.dtype)[:, None, None, None]
    balance = weights * density * (1.0 + 3.0 * projected + 4.5 * projected * projected - 1.5 * speed_square)
    flow_post = (1.0 - solidity) * (flow - (flow - balance) / tau_flow) + solidity * flow[flow_opposite]
    stream_hotness = jnp.sum(caloric_population, axis=0)
    heat_lattice = jnp.asarray(heat_velocity, flow.dtype)
    caloric_moment_reduce = jnp.tensordot(heat_lattice, velocity_field, axes=(1, 0), precision=highest)
    caloric_stencil_shares = jnp.asarray(heat_weight, flow.dtype)[:, None, None, None]
    conserved_power_ledger = caloric_stencil_shares * stream_hotness * (1.0 + 4.0 * caloric_moment_reduce)
    heat_post = caloric_population - (caloric_population - conserved_power_ledger) / tau_heat
    return flow_post, heat_post


def collide_all(flow, caloric_population, solidity):
    def layer_block(slab, carry):
        flow_out, heat_out = carry
        start = (slab * CZ).astype(jnp.int32)
        flow_part = lax.dynamic_slice_in_dim(flow, start, CZ, 1)
        heat_part = lax.dynamic_slice_in_dim(caloric_population, start, CZ, 1)
        solid_part = lax.dynamic_slice_in_dim(solidity, start, CZ, 0)
        flow_post, heat_post = collide(flow_part, heat_part, solid_part)
        flow_out = lax.dynamic_update_slice_in_dim(flow_out, flow_post, start, 1)
        heat_out = lax.dynamic_update_slice_in_dim(heat_out, heat_post, start, 1)
        return flow_out, heat_out

    return lax.fori_loop(0, SLABS, layer_block, (jnp.zeros_like(flow), jnp.zeros_like(caloric_population)))


def stream_all(post, velocity):
    lanes = []
    for lane in range(post.shape[0]):
        step_x, step_y, step_z = velocity[lane]
        lanes.append(jnp.roll(post[lane], (int(step_z), int(step_x), int(step_y)), axis=(0, 1, 2)))
    return jnp.stack(lanes)


def apply_solid(vector, diagonal, coupling, picker):
    partner = jnp.einsum('csbd,csdk->csbk', picker, vector, precision=highest)
    forward = jnp.einsum('csbij,csbj->csbi', coupling, partner, precision=highest)
    backward_terms = jnp.einsum('csbji,csbj->csbi', coupling, vector, precision=highest)
    backward = jnp.einsum('csbd,csbk->csdk', picker, backward_terms, precision=highest)
    return diagonal * vector - forward - backward


def reference(populations, heat_pops, solid_frac, coupled_grid_point, dest_index, heat_coeff, slot_node, node_diag, coupling, block_pattern, heat_source, solid_start):
    flow = populations
    caloric_population = heat_pops
    for step in range(STEPS):
        flow_post, heat_post = collide_all(flow, caloric_population, solid_frac)
        flow = stream_all(flow_post, flow_velocity)
        caloric_population = stream_all(heat_post, heat_velocity)
    gas_hotness_after = jnp.sum(caloric_population, axis=0)
    gas_motion_amount = flow_moments(flow)
    band_identifiers = jnp.arange(LATERAL_BANDS, dtype=jnp.int32)[:, None, None]
    plate_identifiers = jnp.arange(SLABS, dtype=jnp.int32)[None, :, None]
    temp_rows = gas_hotness_after.reshape(SLABS, CZ, LATERAL_BANDS, CX, CY).transpose(2, 0, 1, 3, 4).reshape(LATERAL_BANDS, SLABS, CZ * CX * CY)
    voxels = coupled_grid_point.reshape(LATERAL_BANDS, SLABS, ROWS_DEV).astype(jnp.int32)
    coupling_conductivities = heat_coeff.reshape(LATERAL_BANDS, SLABS, ROWS_DEV)
    interface_flux_rows = coupling_conductivities * jnp.take_along_axis(temp_rows, voxels, axis=2)
    aimed_entry = dest_index.reshape(LATERAL_BANDS, SLABS, ROWS_DEV).astype(jnp.int32)
    member = (aimed_entry[..., None] == jnp.arange(SLABS, dtype=jnp.int32)).astype(jnp.int32)
    current_place = jnp.sum((jnp.cumsum(member, axis=2) - member) * member, axis=3).astype(jnp.int32)
    opening_ordinal = aimed_entry * CAP + current_place
    send_flux = jnp.zeros((LATERAL_BANDS, SLABS, SLABS * CAP), interface_flux_rows.dtype).at[band_identifiers, plate_identifiers, opening_ordinal].set(interface_flux_rows)
    send_coeff = jnp.zeros((LATERAL_BANDS, SLABS, SLABS * CAP), coupling_conductivities.dtype).at[band_identifiers, plate_identifiers, opening_ordinal].set(coupling_conductivities)
    recv_flux = send_flux.reshape(LATERAL_BANDS, SLABS, SLABS, CAP).transpose(0, 2, 1, 3).reshape(LATERAL_BANDS, SLABS, SLABS * CAP)
    recv_coeff = send_coeff.reshape(LATERAL_BANDS, SLABS, SLABS, CAP).transpose(0, 2, 1, 3).reshape(LATERAL_BANDS, SLABS, SLABS * CAP)
    node_index = slot_node.reshape(LATERAL_BANDS, SLABS, SLABS * CAP).astype(jnp.int32)
    added_source = jnp.zeros((LATERAL_BANDS, SLABS, NB * CORE_MESH_PIECE), recv_flux.dtype).at[band_identifiers, plate_identifiers, node_index].add(recv_flux)
    added_diag = jnp.zeros((LATERAL_BANDS, SLABS, NB * CORE_MESH_PIECE), recv_coeff.dtype).at[band_identifiers, plate_identifiers, node_index].add(recv_coeff)
    shape4 = (LATERAL_BANDS, SLABS, NB, CORE_MESH_PIECE)
    diagonal = node_diag.reshape(shape4) + added_diag.reshape(shape4)
    right_side = heat_source.reshape(shape4) + added_source.reshape(shape4)
    blocks = coupling.reshape(LATERAL_BANDS, SLABS, NB, CORE_MESH_PIECE, CORE_MESH_PIECE)
    pattern = block_pattern.reshape(LATERAL_BANDS, SLABS, NB).astype(jnp.int32)
    picker = (pattern[..., None] == jnp.arange(NB, dtype=jnp.int32)).astype(node_diag.dtype)
    conduction_approximant = solid_start.reshape(shape4)
    residual = right_side - apply_solid(conduction_approximant, diagonal, blocks, picker)
    direction = residual
    norm_now = jnp.sum(residual * residual)
    for step in range(ITERS):
        image = apply_solid(direction, diagonal, blocks, picker)
        step_size = norm_now / jnp.sum(direction * image)
        conduction_approximant = conduction_approximant + step_size * direction
        residual = residual - step_size * image
        norm_next = jnp.sum(residual * residual)
        direction = residual + (norm_next / norm_now) * direction
        norm_now = norm_next
    opening_hotness = jnp.take_along_axis(conduction_approximant.reshape(LATERAL_BANDS, SLABS, NB * CORE_MESH_PIECE), node_index, axis=2).reshape(LATERAL_BANDS, SLABS, SLABS, CAP)
    fibre_surface_hotness = opening_hotness[band_identifiers, aimed_entry, plate_identifiers, current_place]
    return gas_hotness_after, gas_motion_amount, conduction_approximant.reshape(LATERAL_BANDS, PIECES_PER_BAND, CORE_MESH_PIECE), fibre_surface_hotness.reshape(LATERAL_BANDS, COUPLED_ENTRIES)
```

```python
import functools

import jax
import jax.numpy as jnp
import numpy as np
from jax import lax
from jax.experimental import pallas as pl
from jax.experimental.pallas import tpu as pltpu
from jax.sharding import PartitionSpec as P

MESH = pl.DeviceIdType.MESH
F32 = jnp.float32
BF16 = jnp.bfloat16
I32 = jnp.int32

STEPS = 2
CY = 384
CAP = 16
SHIFT = 4.0

FLOW = [
    (0, 0, 0),
    (1, 0, 0),
    (-1, 0, 0),
    (0, 1, 0),
    (0, -1, 0),
    (0, 0, 1),
    (0, 0, -1),
    (1, 1, 0),
    (-1, -1, 0),
    (1, -1, 0),
    (-1, 1, 0),
    (1, 0, 1),
    (-1, 0, -1),
    (1, 0, -1),
    (-1, 0, 1),
    (0, 1, 1),
    (0, -1, -1),
    (0, 1, -1),
    (0, -1, 1),
]
EVERY = FLOW + FLOW[:7]
WEIGHT = [1.0 / 3.0] + [1.0 / 18.0] * 6 + [1.0 / 36.0] * 12
HEAT_WEIGHT = [0.25] + [0.125] * 6
TAU_FLOW = 0.8
TAU_HEAT = 0.7

X_UP = [i for i, e in enumerate(EVERY) if e[0] == 1]
X_DOWN = [i for i, e in enumerate(EVERY) if e[0] == -1]
Z_UP = [i for i, e in enumerate(EVERY) if e[2] == 1]
Z_DOWN = [i for i, e in enumerate(EVERY) if e[2] == -1]
EDGES = [
    next(i for i, e in enumerate(FLOW) if e == (1, 0, 1)),
    next(i for i, e in enumerate(FLOW) if e == (-1, 0, 1)),
    next(i for i, e in enumerate(FLOW) if e == (1, 0, -1)),
    next(i for i, e in enumerate(FLOW) if e == (-1, 0, -1)),
]


def dot(a, b, dims):
    return lax.dot_general(a, b, (dims, ((), ())), preferred_element_type=F32)


def parts3(v):
    a = v.astype(BF16).astype(F32)
    rest = v - a
    b = rest.astype(BF16).astype(F32)
    return a, b, rest - b


def iota(shape, dim):
    return lax.broadcasted_iota(I32, shape, dim)


def total(v):
    return jnp.sum(jnp.sum(v, axis=1, keepdims=True), axis=0, keepdims=True)


def kernel(
    groups,
    bands,
    pops_ref,
    heat_ref,
    solid_ref,
    voxel_ref,
    dest_ref,
    coeff_ref,
    slot_ref,
    diag_ref,
    coup_ref,
    pat_ref,
    source_ref,
    start_ref,
    temp_out,
    motion_out,
    solid_out,
    rows_out,
    cur,
    post,
    zs,
    zr,
    xs,
    xr,
    er,
    chop,
    cthop,
    lohot,
    mask,
    place,
    dhot,
    lo_vox,
    ecode,
    fcode,
    send1,
    recv1,
    send2,
    recv2,
    back1,
    rback1,
    back2,
    rback2,
    tot,
    rtot,
    halo_send,
    halo_recv,
    sems_send,
    sems_recv,
    grp_send,
    grp_recv,
):
    subs = groups * 8
    gi = lax.axis_index("grp")
    si = lax.axis_index("sub")
    g = si // 8
    j = si % 8
    g_up = lax.rem(gi + 1, bands)
    g_dn = lax.rem(gi + bands - 1, bands)
    s_up = lax.rem(si + 1, subs)
    s_dn = lax.rem(si + subs - 1, subs)

    barrier = pltpu.get_barrier_semaphore()

    def greet(a, b):
        pl.semaphore_signal(barrier, inc=1, device_id=(a, b), device_id_type=MESH)

    for a, b in (
        (gi, s_up),
        (gi, s_dn),
        (g_up, si),
        (g_dn, si),
        (g_up, s_up),
        (g_up, s_dn),
        (g_dn, s_up),
        (g_dn, s_dn),
    ):
        greet(a, b)

    def greet_strip(i, carry):
        greet(gi, lax.rem(g + i, groups) * 8 + j)
        greet(gi, g * 8 + lax.rem(j + i, 8))
        return carry

    lax.fori_loop(1, 8, greet_strip, 0)

    def greet_bands(i, carry):
        greet(lax.rem(gi + i, bands), si)
        return carry

    lax.fori_loop(1, bands, greet_bands, 0)

    cur[0:19] = pops_ref[...]
    cur[19:26] = heat_ref[...]
    xs[:, :, 8:16] = jnp.zeros((STEPS, 2, 8, CY), F32)

    for b in range(8):
        block = coup_ref[0, b]
        high = block.astype(BF16).astype(F32)
        low = block - high
        rows = pl.ds(b * 128, 128)
        chop[rows, 0:128] = high.astype(BF16)
        chop[rows, 128:256] = low.astype(BF16)
        cthop[rows, 0:128] = high.T.astype(BF16)
        cthop[rows, 128:256] = low.T.astype(BF16)

    wide = 16 * 128
    a_of = iota((128, wide), 0)
    c_of = iota((128, wide), 1)
    k_of = c_of // 128
    lane_of = c_of % 128
    p_of = lane_of // 32
    t_of = (lane_of // 8) % 4
    ecode[...] = jnp.where(
        (a_of == p_of * 32 + t_of * 16 + k_of) & (p_of < 3) & (t_of < 2), 1.0, 0.0
    ).astype(BF16)
    spread = jnp.where(a_of == k_of, 1.0, 0.0).astype(BF16)
    c_of = iota((wide, 128), 0)
    l_of = iota((wide, 128), 1)
    k_of = c_of // 128
    lane_of = c_of % 128
    p_of = lane_of // 32
    t_of = (lane_of // 8) % 4
    fcode[...] = jnp.where((l_of == t_of * 16 + k_of) & (p_of < 3) & (t_of < 3), 1.0, 0.0).astype(
        BF16
    )

    slots = slot_ref[...]
    rolled = [slots] + [pltpu.roll(slots, 128 - 16 * a, 1) for a in range(1, 8)]
    slots = jnp.concatenate(rolled, axis=0)
    slot_hi = (slots // 128).astype(F32).astype(BF16)
    slot_lo = (slots % 128).astype(F32).astype(BF16)
    hi_all = dot(slot_hi, spread, ((1,), (0,)))
    lo_all = dot(slot_lo, spread, ((1,), (0,)))
    lane = iota((64, 128), 1)
    for k in range(16):
        cols = slice(k * 128, (k + 1) * 128)
        rows = pl.ds(k * 64, 64)
        lohot[rows, :] = jnp.where(lo_all[:, cols] == lane.astype(F32), 1.0, 0.0).astype(BF16)
        mask[rows, :] = jnp.where(hi_all[:, cols] == (lane % 8).astype(F32), 1.0, 0.0)

    dest = dest_ref[...]
    dest_hot = jnp.where(iota((64, 512), 0) == dest, 1.0, 0.0)
    dhot[...] = dest_hot.astype(BF16)
    ahead = jnp.where(iota((512, 512), 0) < iota((512, 512), 1), 1.0, 0.0).astype(BF16)
    counts = dot(dest_hot.astype(BF16), ahead, ((1,), (0,)))
    at = jnp.sum(dest_hot * counts, axis=0, keepdims=True)
    place[...] = jnp.where((iota((128, 512), 0) % 16).astype(F32) == at, 1.0, 0.0)

    voxel = voxel_ref[...]
    lo_vox[...] = jnp.where(iota((128, 512), 0) == voxel % 128, 1.0, 0.0).astype(BF16)
    over = voxel // 128
    layer_x = over // 3
    vox_row = (over - layer_x * 3) * 16 + layer_x

    sub8 = iota((8, 128), 0)
    pat = [pat_ref[0, b] for b in range(8)]
    pat_col = jnp.zeros((8, 128), I32)
    for b in range(8):
        pat_col = jnp.where(sub8 == b, pat[b], pat_col)

    def block_dot(v, table):
        high = v.astype(BF16).astype(F32)
        low = v - high
        left = jnp.concatenate([jnp.where(sub8 == b, high, 0.0) for b in range(8)], axis=1)
        right = jnp.concatenate([jnp.where(sub8 == b, low, 0.0) for b in range(8)], axis=1)
        both = jnp.concatenate([left, right], axis=0).astype(BF16)
        out = dot(both, table[...], ((1,), (0,)))
        return out[0:8, 0:128] + out[8:16, 0:128] + out[0:8, 128:256]

    def off_diagonal(v):
        partner = jnp.zeros((8, 128), F32)
        for k in range(8):
            partner = jnp.where(pat_col == k, v[k : k + 1, :], partner)
        forward = block_dot(partner, cthop)
        terms = block_dot(v, chop)
        backward = jnp.zeros((8, 128), F32)
        for b in range(8):
            backward = backward + jnp.where(sub8 == pat[b], terms[b : b + 1, :], 0.0)
        return forward + backward

    x0 = start_ref[0]
    fixed = source_ref[0] + off_diagonal(x0)
    diag = diag_ref[0]

    def collide(step):
        for z in range(2):
            for c in range(3):
                cols = slice(c * 128, (c + 1) * 128)
                f = [cur[i, z, :, cols] for i in range(19)]
                heat = [cur[19 + i, z, :, cols] for i in range(7)]
                solid = solid_ref[z, :, cols]
                rho = functools.reduce(jnp.add, f)
                m = []
                for d in range(3):
                    pos = [f[i] for i in range(19) if FLOW[i][d] == 1]
                    neg = [f[i] for i in range(19) if FLOW[i][d] == -1]
                    m.append(functools.reduce(jnp.add, pos) - functools.reduce(jnp.add, neg))
                u = [v / rho for v in m]
                flat = 1.0 - 1.5 * (u[0] * u[0] + u[1] * u[1] + u[2] * u[2])
                fluid = 1.0 - solid
                keep = fluid * (1.0 - 1.0 / TAU_FLOW)
                gain = fluid * rho * (1.0 / TAU_FLOW)
                out = [None] * 26
                out[0] = (keep + solid) * f[0] + gain * WEIGHT[0] * flat
                for i in range(1, 19, 2):
                    along = None
                    for d in range(3):
                        if FLOW[i][d] == 1:
                            along = u[d] if along is None else along + u[d]
                        elif FLOW[i][d] == -1:
                            along = -u[d] if along is None else along - u[d]
                    even = flat + 4.5 * along * along
                    odd = 3.0 * along
                    scale = gain * WEIGHT[i]
                    out[i] = keep * f[i] + solid * f[i + 1] + scale * (even + odd)
                    out[i + 1] = keep * f[i + 1] + solid * f[i] + scale * (even - odd)
                hot = functools.reduce(jnp.add, heat)
                for i in range(7):
                    share = hot * (HEAT_WEIGHT[i] / TAU_HEAT)
                    if i > 0:
                        d = [abs(v) for v in FLOW[i]].index(1)
                        sign = FLOW[i][d]
                        share = share * (1.0 + (4.0 * sign) * u[d])
                    out[19 + i] = (1.0 - 1.0 / TAU_HEAT) * heat[i] + share
                for i in range(26):
                    ez = EVERY[i][2]
                    post[i, z, :, cols] = out[i]
                    if ez == 1 and z == 1:
                        zs[step, 0, Z_UP.index(i), :, cols] = out[i]
                    if ez == -1 and z == 0:
                        zs[step, 1, Z_DOWN.index(i), :, cols] = out[i]
                    if EVERY[i][0] == 1:
                        r = X_UP.index(i) * 2 + z
                        xs[step, 0, r : r + 1, cols] = out[i][7:8, :]
                    if EVERY[i][0] == -1:
                        r = X_DOWN.index(i) * 2 + z
                        xs[step, 1, r : r + 1, cols] = out[i][0:1, :]

    def halo(step):
        made = []

        def put(n, src, dst, a, b):
            made.append(
                pltpu.make_async_remote_copy(
                    src_ref=src,
                    dst_ref=dst,
                    send_sem=halo_send.at[step, n],
                    recv_sem=halo_recv.at[step, n],
                    device_id=(a, b),
                    device_id_type=MESH,
                )
            )

        put(0, zs.at[step, 0, Z_UP.index(EDGES[0])], er.at[step, 0], g_up, s_up)
        put(1, zs.at[step, 0, Z_UP.index(EDGES[1])], er.at[step, 1], g_dn, s_up)
        put(2, zs.at[step, 1, Z_DOWN.index(EDGES[2])], er.at[step, 2], g_up, s_dn)
        put(3, zs.at[step, 1, Z_DOWN.index(EDGES[3])], er.at[step, 3], g_dn, s_dn)
        put(4, xs.at[step, 0], xr.at[step, 0], g_up, si)
        put(5, xs.at[step, 1], xr.at[step, 1], g_dn, si)
        put(6, zs.at[step, 0], zr.at[step, 0], gi, s_up)
        put(7, zs.at[step, 1], zr.at[step, 1], gi, s_dn)
        return made

    edge8 = iota((8, CY), 0)

    def stream(step):
        for i in range(26):
            ex, ey, ez = EVERY[i]
            for z in range(2):
                edge = None
                if ez == 0 or (ez == 1 and z == 1) or (ez == -1 and z == 0):
                    source = z - ez
                    piece = post[i, source]
                    if ex == 1:
                        r = X_UP.index(i) * 2 + source
                        edge = xr[step, 0, r : r + 1, :]
                    if ex == -1:
                        r = X_DOWN.index(i) * 2 + source
                        edge = xr[step, 1, r : r + 1, :]
                else:
                    if ez == 1:
                        piece = zr[step, 0, Z_UP.index(i)]
                    else:
                        piece = zr[step, 1, Z_DOWN.index(i)]
                    if ex == 1:
                        edge = er[step, EDGES.index(i), 7:8, :]
                    if ex == -1:
                        edge = er[step, EDGES.index(i), 0:1, :]
                if ex == 1:
                    piece = jnp.where(edge8 == 0, edge, pltpu.roll(piece, 1, 0))
                if ex == -1:
                    piece = jnp.where(edge8 == 7, edge, pltpu.roll(piece, 7, 0))
                if ey == 1:
                    piece = pltpu.roll(piece, 1, 1)
                if ey == -1:
                    piece = pltpu.roll(piece, CY - 1, 1)
                cur[i, z] = piece

    collide(0)
    pl.semaphore_wait(barrier, 8 + 14 + bands - 1)

    for step in range(STEPS):
        if step > 0:
            collide(step)
        made = halo(step)
        for c in made:
            c.start()
        for c in made:
            c.wait_recv()
        stream(step)

    hot_rows = []
    for z in range(2):
        hot = functools.reduce(jnp.add, [cur[19 + i, z] for i in range(7)])
        temp_out[z] = hot
        hot_rows.append(hot)
        for d in range(3):
            pos = [cur[i, z] for i in range(19) if FLOW[i][d] == 1]
            neg = [cur[i, z] for i in range(19) if FLOW[i][d] == -1]
            motion_out[d, z] = functools.reduce(jnp.add, pos) - functools.reduce(jnp.add, neg)

    table = jnp.concatenate(
        [hot_rows[z][:, c * 128 : (c + 1) * 128] for c in range(3) for z in range(2)], axis=0
    )
    picked = dot(
        jnp.concatenate(parts3(table), axis=0).astype(BF16), lo_vox[...], ((1,), (0,))
    )
    picked = picked[0:48] + picked[48:96] + picked[96:144]
    seen = jnp.sum(jnp.where(iota((48, 512), 0) == vox_row, picked, 0.0), axis=0, keepdims=True)
    coeff = coeff_ref[...]
    flux = coeff * seen
    placed = place[0:16, :]
    laid = []
    for pair in zip(parts3(flux), parts3(coeff)):
        laid.append(placed * pair[0])
        laid.append(placed * pair[1])
    laid.append(jnp.zeros((32, 512), F32))
    laid = jnp.concatenate(laid, axis=0).astype(BF16)
    sent = dot(dhot[...], laid, ((1,), (1,)))
    send1[...] = sent + pltpu.roll(sent, 96, 1) + pltpu.roll(sent, 64, 1)

    def tile(ref, n):
        return ref.at[pl.ds(pl.multiple_of(n * 8, 8), 8), :]

    def across(kind, src, dst):
        def copy(i):
            to = lax.rem(g + i, groups)
            return pltpu.make_async_remote_copy(
                src_ref=tile(src, to),
                dst_ref=tile(dst, g),
                send_sem=sems_send.at[kind, to],
                recv_sem=sems_recv.at[kind, g],
                device_id=(gi, to * 8 + j),
                device_id_type=MESH,
            )

        return copy, g, groups

    def within(kind, src, dst):
        def copy(i):
            to = lax.rem(j + i, 8)
            return pltpu.make_async_remote_copy(
                src_ref=tile(src, to),
                dst_ref=tile(dst, j),
                send_sem=sems_send.at[kind, to],
                recv_sem=sems_recv.at[kind, j],
                device_id=(gi, g * 8 + to),
                device_id_type=MESH,
            )

        return copy, j, 8

    def start_all(stage):
        copy, me, count = stage

        def go(i, carry):
            copy(i).start()
            return carry

        lax.fori_loop(1, count, go, 0)

    def finish(kind, stage, src, dst):
        copy, me, count = stage
        own = pl.ds(pl.multiple_of(me * 8, 8), 8)
        dst[own, :] = src[own, :]

        def take(i, carry):
            peer = lax.rem(me + i, count)
            pltpu.make_async_copy(
                tile(src, peer), tile(dst, peer), sems_recv.at[kind, peer]
            ).wait()
            return carry

        lax.fori_loop(1, count, take, 0)

    def turn(src, n):
        return src[pl.ds(n, 8, stride=8), :]

    stage0 = across(0, send1, recv1)
    start_all(stage0)
    finish(0, stage0, send1, recv1)
    for n in range(8):
        send2[n * 8 : (n + 1) * 8, :] = turn(recv1, n)
    stage1 = within(1, send2, recv2)
    start_all(stage1)
    finish(1, stage1, send2, recv2)

    got = recv2[...]
    in_flux = jnp.where(lane < 32, got, 0.0)
    p0, p1, p2 = parts3(in_flux)
    coded = (p0 + pltpu.roll(p1, 32, 1) + pltpu.roll(p2, 64, 1)).astype(BF16)
    values = dot(coded, ecode[...], ((1,), (0,)))
    values = jnp.concatenate([values[:, k * 128 : (k + 1) * 128] for k in range(16)], axis=0)
    values = (values * mask[...]).astype(BF16)
    summed = dot(values, lohot[...], ((0,), (0,)))
    add_source = summed[0:8] + summed[32:40] + summed[64:72]
    add_diag = summed[8:16] + summed[40:48] + summed[72:80]

    diag = diag + add_diag
    r0 = fixed + add_source - diag * x0
    w1 = (diag - SHIFT) * r0 - off_diagonal(r0)
    w2 = (diag - SHIFT) * w1 - off_diagonal(w1)
    sums = [total(r0 * r0), total(r0 * w1), total(w1 * w1), total(w1 * w2)]

    held = jnp.concatenate([x0, r0, w1, jnp.zeros((8, 128), F32)], axis=0)
    held = jnp.concatenate(list(parts3(held)) + [jnp.zeros((32, 128), F32)], axis=0).astype(BF16)
    found = dot(lohot[...], held, ((1,), (1,)))
    found = (found * mask[...]).astype(BF16)
    found = jnp.concatenate([found[k * 64 : (k + 1) * 64, :] for k in range(16)], axis=1)
    found = dot(found, fcode[...], ((1,), (0,)))
    for n in range(4):
        found = jnp.where(lane == 48 + n, sums[n], found)
    back1[...] = found

    stage2 = within(2, back1, rback1)
    start_all(stage2)
    finish(2, stage2, back1, rback1)
    lane8 = iota((8, 128), 1)
    is_sum = (lane8 >= 48) & (lane8 < 52)
    group_sum = functools.reduce(jnp.add, [rback1[n * 8 : (n + 1) * 8, :] for n in range(8)])
    for n in range(8):
        back2[n * 8 : (n + 1) * 8, :] = jnp.where(is_sum, group_sum, turn(rback1, n))
    stage3 = across(3, back2, rback2)
    start_all(stage3)
    finish(3, stage3, back2, rback2)
    tot[...] = functools.reduce(jnp.add, [rback2[n * 8 : (n + 1) * 8, :] for n in range(8)])

    def band_copy(i):
        to = lax.rem(gi + i, bands)
        return pltpu.make_async_remote_copy(
            src_ref=tot,
            dst_ref=rtot.at[gi],
            send_sem=grp_send.at[to],
            recv_sem=grp_recv.at[gi],
            device_id=(to, si),
            device_id_type=MESH,
        )

    def band_go(i, carry):
        band_copy(i).start()
        return carry

    lax.fori_loop(1, bands, band_go, 0)

    back = jnp.where(lane < 48, rback2[...], 0.0)
    rows = functools.reduce(
        jnp.add, [dot(p.astype(BF16), dhot[...], ((0,), (0,))) for p in parts3(back)]
    )
    rows = rows * place[...]
    row_x0 = jnp.sum(rows[0:16], axis=0, keepdims=True)
    row_r0 = jnp.sum(rows[16:32], axis=0, keepdims=True)
    row_w1 = jnp.sum(rows[32:48], axis=0, keepdims=True)

    rtot[gi] = tot[...]

    def band_take(i, carry):
        peer = lax.rem(gi + i, bands)
        pltpu.make_async_copy(tot, rtot.at[peer], grp_recv.at[peer]).wait()
        return carry

    lax.fori_loop(1, bands, band_take, 0)
    whole = functools.reduce(jnp.add, [rtot[n] for n in range(bands)])

    def lane_value(n):
        return total(jnp.where((lane8 == 48 + n) & (sub8 == 0), whole, 0.0))

    n0, n1, n2, n3 = [lane_value(n) for n in range(4)]
    delta = n1 / n0
    second = n2 / n0
    spread_of = second - delta * delta
    theta = SHIFT + delta
    third = n3 / n0 - 3.0 * delta * second + 2.0 * delta * delta * delta
    wide_enough = spread_of > 1e-7 * theta * theta
    spread_of = jnp.maximum(spread_of, 0.0)
    skew = jnp.where(wide_enough, third / jnp.where(wide_enough, spread_of, 1.0), 0.0)
    step0 = 1.0 / theta
    growth = spread_of / (theta * theta)
    step1 = 1.0 / (theta + skew - spread_of / theta)
    by_r0 = step0 + step1 * (growth + step0 * delta)
    by_w1 = -step1 * step0
    solid_out[0] = x0 + by_r0 * r0 + by_w1 * w1
    rows_out[...] = row_x0 + by_r0 * row_r0 + by_w1 * row_w1

    for step in range(STEPS):
        for c in halo(step):
            c.wait_send()
    for stage in (stage0, stage1, stage2, stage3):
        copy, me, count = stage

        def left(i, carry):
            copy(i).wait_send()
            return carry

        lax.fori_loop(1, count, left, 0)

    def band_left(i, carry):
        band_copy(i).wait_send()
        return carry

    lax.fori_loop(1, bands, band_left, 0)


def solution(mesh):
    bands = mesh.shape["grp"]
    subs = mesh.shape["sub"]
    groups = subs // 8

    def body(
        populations,
        heat_pops,
        solid_frac,
        coupled_grid_point,
        dest_index,
        heat_coeff,
        slot_node,
        node_diag,
        coupling,
        block_pattern,
        heat_source,
        solid_start,
    ):
        vmem = pl.BlockSpec(memory_space=pltpu.VMEM)
        smem = pl.BlockSpec(memory_space=pltpu.SMEM)
        dma = pltpu.SemaphoreType.DMA
        return pl.pallas_call(
            functools.partial(kernel, groups, bands),
            out_shape=(
                jax.ShapeDtypeStruct((2, 8, CY), F32),
                jax.ShapeDtypeStruct((3, 2, 8, CY), F32),
                jax.ShapeDtypeStruct((1, 8, 128), F32),
                jax.ShapeDtypeStruct((1, 512), F32),
            ),
            in_specs=[vmem] * 9 + [smem] + [vmem] * 2,
            out_specs=(vmem,) * 4,
            scratch_shapes=[
                pltpu.VMEM((26, 2, 8, CY), F32),
                pltpu.VMEM((26, 2, 8, CY), F32),
                pltpu.VMEM((STEPS, 2, 6, 8, CY), F32),
                pltpu.VMEM((STEPS, 2, 6, 8, CY), F32),
                pltpu.VMEM((STEPS, 2, 16, CY), F32),
                pltpu.VMEM((STEPS, 2, 16, CY), F32),
                pltpu.VMEM((STEPS, 4, 8, CY), F32),
                pltpu.VMEM((1024, 256), BF16),
                pltpu.VMEM((1024, 256), BF16),
                pltpu.VMEM((1024, 128), BF16),
                pltpu.VMEM((1024, 128), F32),
                pltpu.VMEM((128, 512), F32),
                pltpu.VMEM((64, 512), BF16),
                pltpu.VMEM((128, 512), BF16),
                pltpu.VMEM((128, 2048), BF16),
                pltpu.VMEM((2048, 128), BF16),
                *[pltpu.VMEM((64, 128), F32)] * 8,
                pltpu.VMEM((8, 128), F32),
                pltpu.VMEM((bands, 8, 128), F32),
                dma((STEPS, 8)),
                dma((STEPS, 8)),
                dma((4, 8)),
                dma((4, 8)),
                dma((bands,)),
                dma((bands,)),
            ],
            compiler_params=pltpu.CompilerParams(collective_id=0, has_side_effects=True),
            name="coupled_step",
        )(
            populations,
            heat_pops,
            solid_frac,
            coupled_grid_point,
            dest_index[..., 0],
            heat_coeff,
            slot_node.reshape(8, 128),
            node_diag,
            coupling,
            block_pattern,
            heat_source,
            solid_start,
        )

    band = P("grp", "sub")
    block = P("grp", "sub", None)
    return jax.shard_map(
        body,
        mesh=mesh,
        in_specs=(
            P(None, "sub", "grp", None),
            P(None, "sub", "grp", None),
            P("sub", "grp", None),
            band,
            block,
            band,
            band,
            block,
            P("grp", "sub", None, None),
            band,
            block,
            block,
        ),
        out_specs=(P("sub", "grp", None), P(None, "sub", "grp", None), block, band),
        check_vma=False,
    )
```

```python
import functools

import jax
import jax.numpy as jnp
import numpy as np
from jax import lax
from jax.experimental import pallas as pl
from jax.experimental.pallas import tpu as pltpu
from jax.sharding import PartitionSpec as P

MESH = pl.DeviceIdType.MESH
F32 = jnp.float32
BF16 = jnp.bfloat16
I32 = jnp.int32

STEPS = 2
CY = 384
CAP = 16
SHIFT = 4.0

FLOW = [
    (0, 0, 0),
    (1, 0, 0),
    (-1, 0, 0),
    (0, 1, 0),
    (0, -1, 0),
    (0, 0, 1),
    (0, 0, -1),
    (1, 1, 0),
    (-1, -1, 0),
    (1, -1, 0),
    (-1, 1, 0),
    (1, 0, 1),
    (-1, 0, -1),
    (1, 0, -1),
    (-1, 0, 1),
    (0, 1, 1),
    (0, -1, -1),
    (0, 1, -1),
    (0, -1, 1),
]
EVERY = FLOW + FLOW[:7]
WEIGHT = [1.0 / 3.0] + [1.0 / 18.0] * 6 + [1.0 / 36.0] * 12
HEAT_WEIGHT = [0.25] + [0.125] * 6
TAU_FLOW = 0.8
TAU_HEAT = 0.7

X_UP = [i for i, e in enumerate(EVERY) if e[0] == 1]
X_DOWN = [i for i, e in enumerate(EVERY) if e[0] == -1]
Z_UP = [i for i, e in enumerate(EVERY) if e[2] == 1]
Z_DOWN = [i for i, e in enumerate(EVERY) if e[2] == -1]
EDGES = [
    next(i for i, e in enumerate(FLOW) if e == (1, 0, 1)),
    next(i for i, e in enumerate(FLOW) if e == (-1, 0, 1)),
    next(i for i, e in enumerate(FLOW) if e == (1, 0, -1)),
    next(i for i, e in enumerate(FLOW) if e == (-1, 0, -1)),
]


def dot(a, b, dims):
    return lax.dot_general(a, b, (dims, ((), ())), preferred_element_type=F32)


def parts3(v):
    a = v.astype(BF16).astype(F32)
    rest = v - a
    b = rest.astype(BF16).astype(F32)
    return a, b, rest - b


def iota(shape, dim):
    return lax.broadcasted_iota(I32, shape, dim)


def total(v):
    return jnp.sum(jnp.sum(v, axis=1, keepdims=True), axis=0, keepdims=True)


def kernel(
    groups,
    bands,
    pops_ref,
    heat_ref,
    solid_ref,
    voxel_ref,
    dest_ref,
    coeff_ref,
    slot_ref,
    diag_ref,
    coup_ref,
    pat_ref,
    source_ref,
    start_ref,
    temp_out,
    motion_out,
    solid_out,
    rows_out,
    cur,
    post,
    zs,
    zr,
    xs,
    xr,
    er,
    chop,
    cthop,
    lohot,
    mask,
    place,
    dhot,
    lo_vox,
    ecode,
    fcode,
    laid_out,
    rel_r,
    rel_l,
    ring_r,
    ring_l,
    recv1,
    send2,
    recv2,
    back1,
    rback1,
    back2,
    rback2,
    tot,
    rtot,
    halo_send,
    halo_recv,
    sems_send,
    sems_recv,
    grp_send,
    grp_recv,
    ready,
    ring_send,
    ring_recv,
):
    subs = groups * 8
    gi = lax.axis_index("grp")
    si = lax.axis_index("sub")
    g = si // 8
    j = si % 8
    g_up = lax.rem(gi + 1, bands)
    g_dn = lax.rem(gi + bands - 1, bands)
    s_up = lax.rem(si + 1, subs)
    s_dn = lax.rem(si + subs - 1, subs)

    barrier = pltpu.get_barrier_semaphore()

    def greet(a, b):
        pl.semaphore_signal(barrier, inc=1, device_id=(a, b), device_id_type=MESH)

    for a, b in (
        (gi, s_up),
        (gi, s_dn),
        (g_up, si),
        (g_dn, si),
        (g_up, s_up),
        (g_up, s_dn),
        (g_dn, s_up),
        (g_dn, s_dn),
    ):
        greet(a, b)

    def tell(n):
        d = 1 << n
        for a, b in (
            (gi, lax.rem(si + d, subs)),
            (gi, lax.rem(si + subs - d, subs)),
            (lax.rem(gi + d, bands), si),
            (lax.rem(gi + bands - d, bands), si),
        ):
            pl.semaphore_signal(ready.at[n], inc=1, device_id=(a, b), device_id_type=MESH)

    def hear(n):
        pl.semaphore_wait(ready.at[n], 4)

    sub8 = iota((8, 128), 0)
    lane = iota((64, 128), 1)
    xs[:, :, 8:16] = jnp.zeros((STEPS, 2, 8, CY), F32)

    def slot_tables():
        a_of = iota((128, 2048), 0)
        spread = jnp.where(a_of == iota((128, 2048), 1) // 128, 1.0, 0.0).astype(BF16)
        slots = slot_ref[...]
        rolled = [slots] + [pltpu.roll(slots, 128 - 16 * a, 1) for a in range(1, 8)]
        slots = jnp.concatenate(rolled, axis=0)
        slot_hi = (slots // 128).astype(F32).astype(BF16)
        slot_lo = (slots % 128).astype(F32).astype(BF16)
        hi_all = dot(slot_hi, spread, ((1,), (0,)))
        lo_all = dot(slot_lo, spread, ((1,), (0,)))
        for k in range(16):
            cols = slice(k * 128, (k + 1) * 128)
            rows = pl.ds(k * 64, 64)
            lohot[rows, :] = jnp.where(lo_all[:, cols] == lane.astype(F32), 1.0, 0.0).astype(BF16)
            mask[rows, :] = jnp.where(hi_all[:, cols] == (lane % 8).astype(F32), 1.0, 0.0)

    def row_tables():
        dest = dest_ref[...]
        dest_hot = jnp.where(iota((64, 512), 0) == dest, 1.0, 0.0)
        dhot[...] = dest_hot.astype(BF16)
        ahead = jnp.where(iota((512, 512), 0) < iota((512, 512), 1), 1.0, 0.0).astype(BF16)
        counts = dot(dest_hot.astype(BF16), ahead, ((1,), (0,)))
        at = jnp.sum(dest_hot * counts, axis=0, keepdims=True)
        place[...] = jnp.where((iota((128, 512), 0) % 16).astype(F32) == at, 1.0, 0.0)

    def code_tables():
        wide = 16 * 128
        a_of = iota((128, wide), 0)
        c_of = iota((128, wide), 1)
        k_of = c_of // 128
        lane_of = c_of % 128
        p_of = lane_of // 32
        t_of = (lane_of // 8) % 4
        ecode[...] = jnp.where(
            (a_of == p_of * 32 + t_of * 16 + k_of) & (p_of < 3) & (t_of < 2), 1.0, 0.0
        ).astype(BF16)
        c_of = iota((wide, 128), 0)
        l_of = iota((wide, 128), 1)
        k_of = c_of // 128
        lane_of = c_of % 128
        p_of = lane_of // 32
        t_of = (lane_of // 8) % 4
        fcode[...] = jnp.where((l_of == t_of * 16 + k_of) & (p_of < 3) & (t_of < 3), 1.0, 0.0).astype(
            BF16
        )

    def coupling_tables():
        for b in range(8):
            block = coup_ref[0, b]
            high = block.astype(BF16).astype(F32)
            low = block - high
            rows = pl.ds(b * 128, 128)
            chop[rows, 0:128] = high.astype(BF16)
            chop[rows, 128:256] = low.astype(BF16)
            cthop[rows, 0:128] = high.T.astype(BF16)
            cthop[rows, 128:256] = low.T.astype(BF16)

    voxel = voxel_ref[...]
    lo_vox[...] = jnp.where(iota((128, 512), 0) == voxel % 128, 1.0, 0.0).astype(BF16)
    over = voxel // 128
    layer_x = over // 3
    vox_row = (over - layer_x * 3) * 16 + layer_x

    pat = [pat_ref[0, b] for b in range(8)]
    pat_col = jnp.zeros((8, 128), I32)
    for b in range(8):
        pat_col = jnp.where(sub8 == b, pat[b], pat_col)

    def block_dot(v, table):
        high = v.astype(BF16).astype(F32)
        low = v - high
        left = jnp.concatenate([jnp.where(sub8 == b, high, 0.0) for b in range(8)], axis=1)
        right = jnp.concatenate([jnp.where(sub8 == b, low, 0.0) for b in range(8)], axis=1)
        both = jnp.concatenate([left, right], axis=0).astype(BF16)
        out = dot(both, table[...], ((1,), (0,)))
        return out[0:8, 0:128] + out[8:16, 0:128] + out[0:8, 128:256]

    def off_diagonal(v):
        partner = jnp.zeros((8, 128), F32)
        for k in range(8):
            partner = jnp.where(pat_col == k, v[k : k + 1, :], partner)
        forward = block_dot(partner, cthop)
        terms = block_dot(v, chop)
        backward = jnp.zeros((8, 128), F32)
        for b in range(8):
            backward = backward + jnp.where(sub8 == pat[b], terms[b : b + 1, :], 0.0)
        return forward + backward

    def collide(step):
        for z in range(2):
            for c in range(3):
                cols = slice(c * 128, (c + 1) * 128)
                if step == 0:
                    f = [pops_ref[i, z, :, cols] for i in range(19)]
                    heat = [heat_ref[i, z, :, cols] for i in range(7)]
                else:
                    f = [cur[i, z, :, cols] for i in range(19)]
                    heat = [cur[19 + i, z, :, cols] for i in range(7)]
                solid = solid_ref[z, :, cols]
                rho = functools.reduce(jnp.add, f)
                m = []
                for d in range(3):
                    pos = [f[i] for i in range(19) if FLOW[i][d] == 1]
                    neg = [f[i] for i in range(19) if FLOW[i][d] == -1]
                    m.append(functools.reduce(jnp.add, pos) - functools.reduce(jnp.add, neg))
                u = [v / rho for v in m]
                flat = 1.0 - 1.5 * (u[0] * u[0] + u[1] * u[1] + u[2] * u[2])
                fluid = 1.0 - solid
                keep = fluid * (1.0 - 1.0 / TAU_FLOW)
                gain = fluid * rho * (1.0 / TAU_FLOW)
                out = [None] * 26
                out[0] = (keep + solid) * f[0] + gain * WEIGHT[0] * flat
                for i in range(1, 19, 2):
                    along = None
                    for d in range(3):
                        if FLOW[i][d] == 1:
                            along = u[d] if along is None else along + u[d]
                        elif FLOW[i][d] == -1:
                            along = -u[d] if along is None else along - u[d]
                    even = flat + 4.5 * along * along
                    odd = 3.0 * along
                    scale = gain * WEIGHT[i]
                    out[i] = keep * f[i] + solid * f[i + 1] + scale * (even + odd)
                    out[i + 1] = keep * f[i + 1] + solid * f[i] + scale * (even - odd)
                hot = functools.reduce(jnp.add, heat)
                for i in range(7):
                    share = hot * (HEAT_WEIGHT[i] / TAU_HEAT)
                    if i > 0:
                        d = [abs(v) for v in FLOW[i]].index(1)
                        sign = FLOW[i][d]
                        share = share * (1.0 + (4.0 * sign) * u[d])
                    out[19 + i] = (1.0 - 1.0 / TAU_HEAT) * heat[i] + share
                for i in range(26):
                    ez = EVERY[i][2]
                    post[i, z, :, cols] = out[i]
                    if ez == 1 and z == 1:
                        zs[step, 0, Z_UP.index(i), :, cols] = out[i]
                    if ez == -1 and z == 0:
                        zs[step, 1, Z_DOWN.index(i), :, cols] = out[i]
                    if EVERY[i][0] == 1:
                        r = X_UP.index(i) * 2 + z
                        xs[step, 0, r : r + 1, cols] = out[i][7:8, :]
                    if EVERY[i][0] == -1:
                        r = X_DOWN.index(i) * 2 + z
                        xs[step, 1, r : r + 1, cols] = out[i][0:1, :]

    def halo(step):
        made = []

        def put(n, src, dst, a, b):
            made.append(
                pltpu.make_async_remote_copy(
                    src_ref=src,
                    dst_ref=dst,
                    send_sem=halo_send.at[step, n],
                    recv_sem=halo_recv.at[step, n],
                    device_id=(a, b),
                    device_id_type=MESH,
                )
            )

        put(0, zs.at[step, 0, Z_UP.index(EDGES[0])], er.at[step, 0], g_up, s_up)
        put(1, zs.at[step, 0, Z_UP.index(EDGES[1])], er.at[step, 1], g_dn, s_up)
        put(2, zs.at[step, 1, Z_DOWN.index(EDGES[2])], er.at[step, 2], g_up, s_dn)
        put(3, zs.at[step, 1, Z_DOWN.index(EDGES[3])], er.at[step, 3], g_dn, s_dn)
        put(4, xs.at[step, 0], xr.at[step, 0], g_up, si)
        put(5, xs.at[step, 1], xr.at[step, 1], g_dn, si)
        put(6, zs.at[step, 0], zr.at[step, 0], gi, s_up)
        put(7, zs.at[step, 1], zr.at[step, 1], gi, s_dn)
        return made

    edge8 = iota((8, CY), 0)

    def stream(step, arrived):
        for i in range(26):
            ex, ey, ez = EVERY[i]
            for z in range(2):
                edge = None
                inside = ez == 0 or z == (1 if ez == 1 else 0)
                if arrived == (inside and ex == 0):
                    continue
                if ez == 0 or (ez == 1 and z == 1) or (ez == -1 and z == 0):
                    source = z - ez
                    piece = post[i, source]
                    if ex == 1:
                        r = X_UP.index(i) * 2 + source
                        edge = xr[step, 0, r : r + 1, :]
                    if ex == -1:
                        r = X_DOWN.index(i) * 2 + source
                        edge = xr[step, 1, r : r + 1, :]
                else:
                    if ez == 1:
                        piece = zr[step, 0, Z_UP.index(i)]
                    else:
                        piece = zr[step, 1, Z_DOWN.index(i)]
                    if ex == 1:
                        edge = er[step, EDGES.index(i), 7:8, :]
                    if ex == -1:
                        edge = er[step, EDGES.index(i), 0:1, :]
                if ex == 1:
                    piece = jnp.where(edge8 == 0, edge, pltpu.roll(piece, 1, 0))
                if ex == -1:
                    piece = jnp.where(edge8 == 7, edge, pltpu.roll(piece, 7, 0))
                if ey == 1:
                    piece = pltpu.roll(piece, 1, 1)
                if ey == -1:
                    piece = pltpu.roll(piece, CY - 1, 1)
                cur[i, z] = piece

    collide(0)
    pl.semaphore_wait(barrier, 8)
    made = halo(0)
    for c in made:
        c.start()
    tell(0)
    stream(0, False)
    slot_tables()
    hear(0)
    tell(1)
    row_tables()
    for c in made:
        c.wait_recv()
    stream(0, True)
    collide(1)
    made = halo(1)
    for c in made:
        c.start()
    hear(1)
    tell(2)
    stream(1, False)
    coupling_tables()
    code_tables()
    x0 = start_ref[0]
    fixed = source_ref[0] + off_diagonal(x0)
    diag = diag_ref[0]

    for c in made:
        c.wait_recv()
    stream(1, True)
    hear(2)

    hot_rows = []
    for z in range(2):
        hot = functools.reduce(jnp.add, [cur[19 + i, z] for i in range(7)])
        temp_out[z] = hot
        hot_rows.append(hot)
        for d in range(3):
            pos = [cur[i, z] for i in range(19) if FLOW[i][d] == 1]
            neg = [cur[i, z] for i in range(19) if FLOW[i][d] == -1]
            motion_out[d, z] = functools.reduce(jnp.add, pos) - functools.reduce(jnp.add, neg)

    table = jnp.concatenate(
        [hot_rows[z][:, c * 128 : (c + 1) * 128] for c in range(3) for z in range(2)], axis=0
    )
    picked = dot(
        jnp.concatenate(parts3(table), axis=0).astype(BF16), lo_vox[...], ((1,), (0,))
    )
    picked = picked[0:48] + picked[48:96] + picked[96:144]
    seen = jnp.sum(jnp.where(iota((48, 512), 0) == vox_row, picked, 0.0), axis=0, keepdims=True)
    coeff = coeff_ref[...]
    flux = coeff * seen
    placed = place[0:16, :]
    laid = []
    for pair in zip(parts3(flux), parts3(coeff)):
        laid.append(placed * pair[0])
        laid.append(placed * pair[1])
    laid.append(jnp.zeros((32, 512), F32))
    laid = jnp.concatenate(laid, axis=0).astype(BF16)
    sent = dot(dhot[...], laid, ((1,), (1,)))
    sent = sent + pltpu.roll(sent, 96, 1) + pltpu.roll(sent, 64, 1)
    laid_out[...] = sent

    def tile(ref, n):
        return ref.at[pl.ds(pl.multiple_of(n * 8, 8), 8), :]

    def across(kind, src, dst):
        def copy(i):
            to = lax.rem(g + i, groups)
            return pltpu.make_async_remote_copy(
                src_ref=tile(src, to),
                dst_ref=tile(dst, g),
                send_sem=sems_send.at[kind, to],
                recv_sem=sems_recv.at[kind, g],
                device_id=(gi, to * 8 + j),
                device_id_type=MESH,
            )

        return copy, g, groups

    def within(kind, src, dst):
        def copy(i):
            to = lax.rem(j + i, 8)
            return pltpu.make_async_remote_copy(
                src_ref=tile(src, to),
                dst_ref=tile(dst, j),
                send_sem=sems_send.at[kind, to],
                recv_sem=sems_recv.at[kind, j],
                device_id=(gi, g * 8 + to),
                device_id_type=MESH,
            )

        return copy, j, 8

    def start_all(stage):
        copy, me, count = stage

        def go(i, carry):
            copy(i).start()
            return carry

        lax.fori_loop(1, count, go, 0)

    def finish(kind, stage, src, dst):
        copy, me, count = stage
        own = pl.ds(pl.multiple_of(me * 8, 8), 8)
        dst[own, :] = src[own, :]

        def take(i, carry):
            peer = lax.rem(me + i, count)
            pltpu.make_async_copy(
                tile(src, peer), tile(dst, peer), sems_recv.at[kind, peer]
            ).wait()
            return carry

        lax.fori_loop(1, count, take, 0)

    def turn(src, n):
        return src[pl.ds(n, 8, stride=8), :]

    def group_rows(d):
        return pl.ds(pl.multiple_of(lax.rem(g + groups + d, groups) * 8, 8), 8)

    for d in range(1, 5):
        rel_r[(d - 1) * 8 : d * 8, :] = laid_out[group_rows(d), :]
    for d in range(1, 4):
        rel_l[(d - 1) * 8 : d * 8, :] = laid_out[group_rows(-d), :]
    recv1[group_rows(0), :] = laid_out[group_rows(0), :]

    def ring_copy(way, s):
        if way == 0:
            first, buffer, starts, most = rel_r, ring_r, (0, 32, 56, 72), 4
            to = lax.rem(g + 1, groups)
        else:
            first, buffer, starts, most = rel_l, ring_l, (0, 24, 40), 3
            to = lax.rem(g + groups - 1, groups)
        size = (most - s) * 8
        if s == 0:
            src = first.at[0:size, :]
        else:
            src = buffer.at[starts[s - 1] + 8 : starts[s - 1] + 8 + size, :]
        return pltpu.make_async_remote_copy(
            src_ref=src,
            dst_ref=buffer.at[starts[s] : starts[s] + size, :],
            send_sem=ring_send.at[way, s],
            recv_sem=ring_recv.at[way, s],
            device_id=(gi, to * 8 + j),
            device_id_type=MESH,
        )

    ring_copy(0, 0).start()
    ring_copy(1, 0).start()
    for s in range(4):
        ring_copy(0, s).wait_recv()
        if s < 3:
            ring_copy(0, s + 1).start()
            ring_copy(1, s).wait_recv()
            if s < 2:
                ring_copy(1, s + 1).start()
            at_l = (0, 24, 40)[s]
            recv1[group_rows(s + 1), :] = ring_l[at_l : at_l + 8, :]
        at_r = (0, 32, 56, 72)[s]
        recv1[group_rows(-1 - s), :] = ring_r[at_r : at_r + 8, :]
    for n in range(8):
        send2[n * 8 : (n + 1) * 8, :] = turn(recv1, n)
    stage1 = within(1, send2, recv2)
    start_all(stage1)
    finish(1, stage1, send2, recv2)

    got = recv2[...]
    in_flux = jnp.where(lane < 32, got, 0.0)
    p0, p1, p2 = parts3(in_flux)
    coded = (p0 + pltpu.roll(p1, 32, 1) + pltpu.roll(p2, 64, 1)).astype(BF16)
    values = dot(coded, ecode[...], ((1,), (0,)))
    values = jnp.concatenate([values[:, k * 128 : (k + 1) * 128] for k in range(16)], axis=0)
    values = (values * mask[...]).astype(BF16)
    summed = dot(values, lohot[...], ((0,), (0,)))
    add_source = summed[0:8] + summed[32:40] + summed[64:72]
    add_diag = summed[8:16] + summed[40:48] + summed[72:80]

    diag = diag + add_diag
    r0 = fixed + add_source - diag * x0
    w1 = (diag - SHIFT) * r0 - off_diagonal(r0)
    w2 = (diag - SHIFT) * w1 - off_diagonal(w1)
    sums = [total(r0 * r0), total(r0 * w1), total(w1 * w1), total(w1 * w2)]

    held = jnp.concatenate([x0, r0, w1, jnp.zeros((8, 128), F32)], axis=0)
    held = jnp.concatenate(list(parts3(held)) + [jnp.zeros((32, 128), F32)], axis=0).astype(BF16)
    found = dot(lohot[...], held, ((1,), (1,)))
    found = (found * mask[...]).astype(BF16)
    found = jnp.concatenate([found[k * 64 : (k + 1) * 64, :] for k in range(16)], axis=1)
    found = dot(found, fcode[...], ((1,), (0,)))
    for n in range(4):
        found = jnp.where(lane == 48 + n, sums[n], found)
    back1[...] = found

    stage2 = within(2, back1, rback1)
    start_all(stage2)
    finish(2, stage2, back1, rback1)
    lane8 = iota((8, 128), 1)
    is_sum = (lane8 >= 48) & (lane8 < 52)
    group_sum = functools.reduce(jnp.add, [rback1[n * 8 : (n + 1) * 8, :] for n in range(8)])
    for n in range(8):
        back2[n * 8 : (n + 1) * 8, :] = jnp.where(is_sum, group_sum, turn(rback1, n))
    stage3 = across(3, back2, rback2)
    start_all(stage3)
    finish(3, stage3, back2, rback2)
    tot[...] = functools.reduce(jnp.add, [rback2[n * 8 : (n + 1) * 8, :] for n in range(8)])

    def band_copy(i):
        to = lax.rem(gi + i, bands)
        return pltpu.make_async_remote_copy(
            src_ref=tot,
            dst_ref=rtot.at[gi],
            send_sem=grp_send.at[to],
            recv_sem=grp_recv.at[gi],
            device_id=(to, si),
            device_id_type=MESH,
        )

    def band_go(i, carry):
        band_copy(i).start()
        return carry

    lax.fori_loop(1, bands, band_go, 0)

    back = jnp.where(lane < 48, rback2[...], 0.0)
    rows = functools.reduce(
        jnp.add, [dot(p.astype(BF16), dhot[...], ((0,), (0,))) for p in parts3(back)]
    )
    rows = rows * place[...]
    row_x0 = jnp.sum(rows[0:16], axis=0, keepdims=True)
    row_r0 = jnp.sum(rows[16:32], axis=0, keepdims=True)
    row_w1 = jnp.sum(rows[32:48], axis=0, keepdims=True)

    rtot[gi] = tot[...]

    def band_take(i, carry):
        peer = lax.rem(gi + i, bands)
        pltpu.make_async_copy(tot, rtot.at[peer], grp_recv.at[peer]).wait()
        return carry

    lax.fori_loop(1, bands, band_take, 0)
    whole = functools.reduce(jnp.add, [rtot[n] for n in range(bands)])

    def lane_value(n):
        return total(jnp.where((lane8 == 48 + n) & (sub8 == 0), whole, 0.0))

    n0, n1, n2, n3 = [lane_value(n) for n in range(4)]
    delta = n1 / n0
    second = n2 / n0
    spread_of = second - delta * delta
    theta = SHIFT + delta
    third = n3 / n0 - 3.0 * delta * second + 2.0 * delta * delta * delta
    wide_enough = spread_of > 1e-7 * theta * theta
    spread_of = jnp.maximum(spread_of, 0.0)
    skew = jnp.where(wide_enough, third / jnp.where(wide_enough, spread_of, 1.0), 0.0)
    step0 = 1.0 / theta
    growth = spread_of / (theta * theta)
    step1 = 1.0 / (theta + skew - spread_of / theta)
    by_r0 = step0 + step1 * (growth + step0 * delta)
    by_w1 = -step1 * step0
    solid_out[0] = x0 + by_r0 * r0 + by_w1 * w1
    rows_out[...] = row_x0 + by_r0 * row_r0 + by_w1 * row_w1

    for step in range(STEPS):
        for c in halo(step):
            c.wait_send()
    for way, s in [(0, 0), (0, 1), (0, 2), (0, 3), (1, 0), (1, 1), (1, 2)]:
        ring_copy(way, s).wait_send()
    for stage in (stage1, stage2, stage3):
        copy, me, count = stage

        def left(i, carry):
            copy(i).wait_send()
            return carry

        lax.fori_loop(1, count, left, 0)

    def band_left(i, carry):
        band_copy(i).wait_send()
        return carry

    lax.fori_loop(1, bands, band_left, 0)


def publish(*refs):
    for source, target in zip(refs[:4], refs[4:]):
        target[...] = source[...]


def solution(mesh):
    bands = mesh.shape["grp"]
    subs = mesh.shape["sub"]
    groups = subs // 8

    def body(
        populations,
        heat_pops,
        solid_frac,
        coupled_grid_point,
        dest_index,
        heat_coeff,
        slot_node,
        node_diag,
        coupling,
        block_pattern,
        heat_source,
        solid_start,
    ):
        vmem = pl.BlockSpec(memory_space=pltpu.VMEM)
        smem = pl.BlockSpec(memory_space=pltpu.SMEM)
        dma = pltpu.SemaphoreType.DMA
        shapes = (
                jax.ShapeDtypeStruct((2, 8, CY), F32),
                jax.ShapeDtypeStruct((3, 2, 8, CY), F32),
                jax.ShapeDtypeStruct((1, 8, 128), F32),
                jax.ShapeDtypeStruct((1, 512), F32),
            )
        made = pl.pallas_call(
            functools.partial(kernel, groups, bands),
            out_shape=shapes,
            in_specs=[vmem] * 9 + [smem] + [vmem] * 2,
            out_specs=(vmem,) * 4,
            scratch_shapes=[
                pltpu.VMEM((26, 2, 8, CY), F32),
                pltpu.VMEM((26, 2, 8, CY), F32),
                pltpu.VMEM((STEPS, 2, 6, 8, CY), F32),
                pltpu.VMEM((STEPS, 2, 6, 8, CY), F32),
                pltpu.VMEM((STEPS, 2, 16, CY), F32),
                pltpu.VMEM((STEPS, 2, 16, CY), F32),
                pltpu.VMEM((STEPS, 4, 8, CY), F32),
                pltpu.VMEM((1024, 256), BF16),
                pltpu.VMEM((1024, 256), BF16),
                pltpu.VMEM((1024, 128), BF16),
                pltpu.VMEM((1024, 128), F32),
                pltpu.VMEM((128, 512), F32),
                pltpu.VMEM((64, 512), BF16),
                pltpu.VMEM((128, 512), BF16),
                pltpu.VMEM((128, 2048), BF16),
                pltpu.VMEM((2048, 128), BF16),
                pltpu.VMEM((64, 128), F32),
                pltpu.VMEM((32, 128), F32),
                pltpu.VMEM((24, 128), F32),
                pltpu.VMEM((80, 128), F32),
                pltpu.VMEM((48, 128), F32),
                *[pltpu.VMEM((64, 128), F32)] * 7,
                pltpu.VMEM((8, 128), F32),
                pltpu.VMEM((bands, 8, 128), F32),
                dma((STEPS, 8)),
                dma((STEPS, 8)),
                dma((4, 8)),
                dma((4, 8)),
                dma((bands,)),
                dma((bands,)),
                pltpu.SemaphoreType.REGULAR((3,)),
                dma((2, 4)),
                dma((2, 4)),
            ],
            compiler_params=pltpu.CompilerParams(collective_id=0, has_side_effects=True),
            name="coupled_step",
        )(
            populations,
            heat_pops,
            solid_frac,
            coupled_grid_point,
            dest_index[..., 0],
            heat_coeff,
            slot_node.reshape(8, 128),
            node_diag,
            coupling,
            block_pattern,
            heat_source,
            solid_start,
        )
        return pl.pallas_call(
            publish,
            out_shape=shapes,
            in_specs=[vmem] * 4,
            out_specs=(vmem,) * 4,
            name="publish",
        )(*made)

    band = P("grp", "sub")
    block = P("grp", "sub", None)
    return jax.shard_map(
        body,
        mesh=mesh,
        in_specs=(
            P(None, "sub", "grp", None),
            P(None, "sub", "grp", None),
            P("sub", "grp", None),
            band,
            block,
            band,
            band,
            block,
            P("grp", "sub", None, None),
            band,
            block,
            block,
        ),
        out_specs=(P("sub", "grp", None), P(None, "sub", "grp", None), block, band),
        check_vma=False,
    )
```

```python
import functools

import jax
import jax.numpy as jnp
import numpy as np
from jax import lax
from jax.experimental import pallas as pl
from jax.experimental.pallas import tpu as pltpu
from jax.sharding import PartitionSpec as P

MESH = pl.DeviceIdType.MESH
F32 = jnp.float32
BF16 = jnp.bfloat16
I32 = jnp.int32

STEPS = 2
CY = 384
CAP = 16
SHIFT = 4.0

FLOW = [
    (0, 0, 0),
    (1, 0, 0),
    (-1, 0, 0),
    (0, 1, 0),
    (0, -1, 0),
    (0, 0, 1),
    (0, 0, -1),
    (1, 1, 0),
    (-1, -1, 0),
    (1, -1, 0),
    (-1, 1, 0),
    (1, 0, 1),
    (-1, 0, -1),
    (1, 0, -1),
    (-1, 0, 1),
    (0, 1, 1),
    (0, -1, -1),
    (0, 1, -1),
    (0, -1, 1),
]
EVERY = FLOW + FLOW[:7]
WEIGHT = [1.0 / 3.0] + [1.0 / 18.0] * 6 + [1.0 / 36.0] * 12
HEAT_WEIGHT = [0.25] + [0.125] * 6
TAU_FLOW = 0.8
TAU_HEAT = 0.7

X_UP = [i for i, e in enumerate(EVERY) if e[0] == 1]
X_DOWN = [i for i, e in enumerate(EVERY) if e[0] == -1]
Z_UP = [i for i, e in enumerate(EVERY) if e[2] == 1]
Z_DOWN = [i for i, e in enumerate(EVERY) if e[2] == -1]
EDGES = [
    next(i for i, e in enumerate(FLOW) if e == (1, 0, 1)),
    next(i for i, e in enumerate(FLOW) if e == (-1, 0, 1)),
    next(i for i, e in enumerate(FLOW) if e == (1, 0, -1)),
    next(i for i, e in enumerate(FLOW) if e == (-1, 0, -1)),
]


def dot(a, b, dims):
    return lax.dot_general(a, b, (dims, ((), ())), preferred_element_type=F32)


def parts3(v):
    a = v.astype(BF16).astype(F32)
    rest = v - a
    b = rest.astype(BF16).astype(F32)
    return a, b, rest - b


def iota(shape, dim):
    return lax.broadcasted_iota(I32, shape, dim)


def total(v):
    return jnp.sum(jnp.sum(v, axis=1, keepdims=True), axis=0, keepdims=True)


def kernel(
    groups,
    bands,
    pops_ref,
    heat_ref,
    solid_ref,
    voxel_ref,
    dest_ref,
    coeff_ref,
    slot_ref,
    diag_ref,
    coup_ref,
    pat_ref,
    source_ref,
    start_ref,
    temp_out,
    motion_out,
    solid_out,
    rows_out,
    cur,
    post,
    zs,
    zr,
    xs,
    xr,
    er,
    chop,
    cthop,
    lohot,
    mask,
    place,
    dhot,
    lo_vox,
    ecode,
    fcode,
    laid_out,
    landed,
    returned,
    received,
    tot,
    rtot,
    halo_send,
    halo_recv,
    strip_send,
    strip_recv,
    band_send,
    band_recv,
    ready,
):
    subs = groups * 8
    gi = lax.axis_index("grp")
    si = lax.axis_index("sub")
    g = si // 8
    j = si % 8
    g_up = lax.rem(gi + 1, bands)
    g_dn = lax.rem(gi + bands - 1, bands)
    s_up = lax.rem(si + 1, subs)
    s_dn = lax.rem(si + subs - 1, subs)

    barrier = pltpu.get_barrier_semaphore()

    def greet(a, b):
        pl.semaphore_signal(barrier, inc=1, device_id=(a, b), device_id_type=MESH)

    for a, b in (
        (gi, s_up),
        (gi, s_dn),
        (g_up, si),
        (g_dn, si),
        (g_up, s_up),
        (g_up, s_dn),
        (g_dn, s_up),
        (g_dn, s_dn),
    ):
        greet(a, b)

    def tell(n):
        d = 1 << n
        to = [(gi, lax.rem(si + d, subs)), (gi, lax.rem(si + subs - d, subs))]
        if 2 * d < bands:
            to += [(lax.rem(gi + d, bands), si), (lax.rem(gi + bands - d, bands), si)]
        for a, b in to:
            pl.semaphore_signal(ready.at[n], inc=1, device_id=(a, b), device_id_type=MESH)

    def hear(n):
        pl.semaphore_wait(ready.at[n], 4 if 2 << n < bands else 2)

    sub8 = iota((8, 128), 0)
    lane = iota((64, 128), 1)
    xs[:, :, 8:16] = jnp.zeros((STEPS, 2, 8, CY), F32)

    def slot_tables():
        a_of = iota((128, 2048), 0)
        spread = jnp.where(a_of == iota((128, 2048), 1) // 128, 1.0, 0.0).astype(BF16)
        slots = slot_ref[...]
        rolled = [slots] + [pltpu.roll(slots, 128 - 16 * a, 1) for a in range(1, 8)]
        slots = jnp.concatenate(rolled, axis=0)
        slot_hi = (slots // 128).astype(F32).astype(BF16)
        slot_lo = (slots % 128).astype(F32).astype(BF16)
        hi_all = dot(slot_hi, spread, ((1,), (0,)))
        lo_all = dot(slot_lo, spread, ((1,), (0,)))
        for k in range(16):
            cols = slice(k * 128, (k + 1) * 128)
            rows = pl.ds(k * 64, 64)
            lohot[rows, :] = jnp.where(lo_all[:, cols] == lane.astype(F32), 1.0, 0.0).astype(BF16)
            mask[rows, :] = jnp.where(hi_all[:, cols] == (lane % 8).astype(F32), 1.0, 0.0)

    def row_tables():
        dest = dest_ref[...]
        dest_hot = jnp.where(iota((64, 512), 0) == dest, 1.0, 0.0)
        dhot[...] = dest_hot.astype(BF16)
        ahead = jnp.where(iota((512, 512), 0) < iota((512, 512), 1), 1.0, 0.0).astype(BF16)
        counts = dot(dest_hot.astype(BF16), ahead, ((1,), (0,)))
        at = jnp.sum(dest_hot * counts, axis=0, keepdims=True)
        place[...] = jnp.where((iota((128, 512), 0) % 16).astype(F32) == at, 1.0, 0.0)

    def code_tables():
        wide = 16 * 128
        a_of = iota((128, wide), 0)
        c_of = iota((128, wide), 1)
        k_of = c_of // 128
        lane_of = c_of % 128
        p_of = lane_of // 32
        t_of = (lane_of // 8) % 4
        ecode[...] = jnp.where(
            (a_of == p_of * 32 + t_of * 16 + k_of) & (p_of < 3) & (t_of < 2), 1.0, 0.0
        ).astype(BF16)
        c_of = iota((wide, 128), 0)
        l_of = iota((wide, 128), 1)
        k_of = c_of // 128
        lane_of = c_of % 128
        p_of = lane_of // 32
        t_of = (lane_of // 8) % 4
        fcode[...] = jnp.where((l_of == t_of * 16 + k_of) & (p_of < 3) & (t_of < 3), 1.0, 0.0).astype(
            BF16
        )

    def coupling_tables():
        for b in range(8):
            block = coup_ref[0, b]
            high = block.astype(BF16).astype(F32)
            low = block - high
            rows = pl.ds(b * 128, 128)
            chop[rows, 0:128] = high.astype(BF16)
            chop[rows, 128:256] = low.astype(BF16)
            cthop[rows, 0:128] = high.T.astype(BF16)
            cthop[rows, 128:256] = low.T.astype(BF16)

    voxel = voxel_ref[...]
    lo_vox[...] = jnp.where(iota((128, 512), 0) == voxel % 128, 1.0, 0.0).astype(BF16)
    over = voxel // 128
    layer_x = over // 3
    vox_row = (over - layer_x * 3) * 16 + layer_x

    pat = [pat_ref[0, b] for b in range(8)]
    pat_col = jnp.zeros((8, 128), I32)
    for b in range(8):
        pat_col = jnp.where(sub8 == b, pat[b], pat_col)

    def block_dot(v, table):
        high = v.astype(BF16).astype(F32)
        low = v - high
        left = jnp.concatenate([jnp.where(sub8 == b, high, 0.0) for b in range(8)], axis=1)
        right = jnp.concatenate([jnp.where(sub8 == b, low, 0.0) for b in range(8)], axis=1)
        both = jnp.concatenate([left, right], axis=0).astype(BF16)
        out = dot(both, table[...], ((1,), (0,)))
        return out[0:8, 0:128] + out[8:16, 0:128] + out[0:8, 128:256]

    def off_diagonal(v):
        partner = jnp.zeros((8, 128), F32)
        for k in range(8):
            partner = jnp.where(pat_col == k, v[k : k + 1, :], partner)
        forward = block_dot(partner, cthop)
        terms = block_dot(v, chop)
        backward = jnp.zeros((8, 128), F32)
        for b in range(8):
            backward = backward + jnp.where(sub8 == pat[b], terms[b : b + 1, :], 0.0)
        return forward + backward

    def collide(step):
        for z in range(2):
            for c in range(3):
                cols = slice(c * 128, (c + 1) * 128)
                if step == 0:
                    f = [pops_ref[i, z, :, cols] for i in range(19)]
                    heat = [heat_ref[i, z, :, cols] for i in range(7)]
                else:
                    f = [cur[i, z, :, cols] for i in range(19)]
                    heat = [cur[19 + i, z, :, cols] for i in range(7)]
                solid = solid_ref[z, :, cols]
                rho = functools.reduce(jnp.add, f)
                m = []
                for d in range(3):
                    pos = [f[i] for i in range(19) if FLOW[i][d] == 1]
                    neg = [f[i] for i in range(19) if FLOW[i][d] == -1]
                    m.append(functools.reduce(jnp.add, pos) - functools.reduce(jnp.add, neg))
                u = [v / rho for v in m]
                flat = 1.0 - 1.5 * (u[0] * u[0] + u[1] * u[1] + u[2] * u[2])
                fluid = 1.0 - solid
                keep = fluid * (1.0 - 1.0 / TAU_FLOW)
                gain = fluid * rho * (1.0 / TAU_FLOW)
                out = [None] * 26
                out[0] = (keep + solid) * f[0] + gain * WEIGHT[0] * flat
                for i in range(1, 19, 2):
                    along = None
                    for d in range(3):
                        if FLOW[i][d] == 1:
                            along = u[d] if along is None else along + u[d]
                        elif FLOW[i][d] == -1:
                            along = -u[d] if along is None else along - u[d]
                    even = flat + 4.5 * along * along
                    odd = 3.0 * along
                    scale = gain * WEIGHT[i]
                    out[i] = keep * f[i] + solid * f[i + 1] + scale * (even + odd)
                    out[i + 1] = keep * f[i + 1] + solid * f[i] + scale * (even - odd)
                hot = functools.reduce(jnp.add, heat)
                for i in range(7):
                    share = hot * (HEAT_WEIGHT[i] / TAU_HEAT)
                    if i > 0:
                        d = [abs(v) for v in FLOW[i]].index(1)
                        sign = FLOW[i][d]
                        share = share * (1.0 + (4.0 * sign) * u[d])
                    out[19 + i] = (1.0 - 1.0 / TAU_HEAT) * heat[i] + share
                for i in range(26):
                    ez = EVERY[i][2]
                    post[i, z, :, cols] = out[i]
                    if ez == 1 and z == 1:
                        zs[step, 0, Z_UP.index(i), :, cols] = out[i]
                    if ez == -1 and z == 0:
                        zs[step, 1, Z_DOWN.index(i), :, cols] = out[i]
                    if EVERY[i][0] == 1:
                        r = X_UP.index(i) * 2 + z
                        xs[step, 0, r : r + 1, cols] = out[i][7:8, :]
                    if EVERY[i][0] == -1:
                        r = X_DOWN.index(i) * 2 + z
                        xs[step, 1, r : r + 1, cols] = out[i][0:1, :]

    def halo(step):
        made = []

        def put(n, src, dst, a, b):
            made.append(
                pltpu.make_async_remote_copy(
                    src_ref=src,
                    dst_ref=dst,
                    send_sem=halo_send.at[step, n],
                    recv_sem=halo_recv.at[step, n],
                    device_id=(a, b),
                    device_id_type=MESH,
                )
            )

        put(0, zs.at[step, 0, Z_UP.index(EDGES[0])], er.at[step, 0], g_up, s_up)
        put(1, zs.at[step, 0, Z_UP.index(EDGES[1])], er.at[step, 1], g_dn, s_up)
        put(2, zs.at[step, 1, Z_DOWN.index(EDGES[2])], er.at[step, 2], g_up, s_dn)
        put(3, zs.at[step, 1, Z_DOWN.index(EDGES[3])], er.at[step, 3], g_dn, s_dn)
        put(4, xs.at[step, 0], xr.at[step, 0], g_up, si)
        put(5, xs.at[step, 1], xr.at[step, 1], g_dn, si)
        put(6, zs.at[step, 0], zr.at[step, 0], gi, s_up)
        put(7, zs.at[step, 1], zr.at[step, 1], gi, s_dn)
        return made

    edge8 = iota((8, CY), 0)

    def stream(step, arrived):
        for i in range(26):
            ex, ey, ez = EVERY[i]
            for z in range(2):
                edge = None
                inside = ez == 0 or z == (1 if ez == 1 else 0)
                if arrived == (inside and ex == 0):
                    continue
                if ez == 0 or (ez == 1 and z == 1) or (ez == -1 and z == 0):
                    source = z - ez
                    piece = post[i, source]
                    if ex == 1:
                        r = X_UP.index(i) * 2 + source
                        edge = xr[step, 0, r : r + 1, :]
                    if ex == -1:
                        r = X_DOWN.index(i) * 2 + source
                        edge = xr[step, 1, r : r + 1, :]
                else:
                    if ez == 1:
                        piece = zr[step, 0, Z_UP.index(i)]
                    else:
                        piece = zr[step, 1, Z_DOWN.index(i)]
                    if ex == 1:
                        edge = er[step, EDGES.index(i), 7:8, :]
                    if ex == -1:
                        edge = er[step, EDGES.index(i), 0:1, :]
                if ex == 1:
                    piece = jnp.where(edge8 == 0, edge, pltpu.roll(piece, 1, 0))
                if ex == -1:
                    piece = jnp.where(edge8 == 7, edge, pltpu.roll(piece, 7, 0))
                if ey == 1:
                    piece = pltpu.roll(piece, 1, 1)
                if ey == -1:
                    piece = pltpu.roll(piece, CY - 1, 1)
                cur[i, z] = piece

    collide(0)
    pl.semaphore_wait(barrier, 8)
    made = halo(0)
    for c in made:
        c.start()
    tell(0)
    stream(0, False)
    slot_tables()
    hear(0)
    tell(1)
    row_tables()
    hear(1)
    tell(2)
    coupling_tables()
    hear(2)
    tell(3)
    code_tables()
    for c in made:
        c.wait_recv()
    stream(0, True)
    collide(1)
    made = halo(1)
    for c in made:
        c.start()
    hear(3)
    tell(4)
    stream(1, False)
    x0 = start_ref[0]
    fixed = source_ref[0] + off_diagonal(x0)
    diag = diag_ref[0]
    for c in made:
        c.wait_recv()
    stream(1, True)

    hot_rows = []
    for z in range(2):
        hot = functools.reduce(jnp.add, [cur[19 + i, z] for i in range(7)])
        temp_out[z] = hot
        hot_rows.append(hot)
        for d in range(3):
            pos = [cur[i, z] for i in range(19) if FLOW[i][d] == 1]
            neg = [cur[i, z] for i in range(19) if FLOW[i][d] == -1]
            motion_out[d, z] = functools.reduce(jnp.add, pos) - functools.reduce(jnp.add, neg)

    table = jnp.concatenate(
        [hot_rows[z][:, c * 128 : (c + 1) * 128] for c in range(3) for z in range(2)], axis=0
    )
    picked = dot(
        jnp.concatenate(parts3(table), axis=0).astype(BF16), lo_vox[...], ((1,), (0,))
    )
    picked = picked[0:48] + picked[48:96] + picked[96:144]
    seen = jnp.sum(jnp.where(iota((48, 512), 0) == vox_row, picked, 0.0), axis=0, keepdims=True)
    coeff = coeff_ref[...]
    flux = coeff * seen
    placed = place[0:16, :]
    laid = []
    for pair in zip(parts3(flux), parts3(coeff)):
        laid.append(placed * pair[0])
        laid.append(placed * pair[1])
    laid.append(jnp.zeros((32, 512), F32))
    laid = jnp.concatenate(laid, axis=0).astype(BF16)
    sent = dot(dhot[...], laid, ((1,), (1,)))
    sent = sent + pltpu.roll(sent, 96, 1) + pltpu.roll(sent, 64, 1)
    laid_out[...] = sent.reshape(64, 1, 128)

    def strip_copy(way, i):
        d = subs // 2 + (1 - 2 * (i % 2)) * ((i + 1) // 2)
        to = lax.rem(si + d, subs)
        if way == 0:
            src, dst = laid_out.at[to], landed.at[j * groups + g]
        else:
            src, dst = returned.at[(to % 8) * groups + to // 8], received.at[si]
        return pltpu.make_async_remote_copy(
            src_ref=src,
            dst_ref=dst,
            send_sem=strip_send.at[way],
            recv_sem=strip_recv.at[way],
            device_id=(gi, to),
            device_id_type=MESH,
        )

    def strip_start(way):
        def go(i, carry):
            strip_copy(way, i).start()
            return carry

        lax.fori_loop(0, subs - 1, go, 0)

    def strip_all(way, sem):
        src, dst = (laid_out, landed) if way == 0 else (returned, received)
        rest = pl.ds(0, subs - 1)
        return pltpu.make_async_copy(src.at[rest], dst.at[rest], sem.at[way])

    hear(4)
    strip_start(0)
    landed[j * groups + g] = laid_out[si]
    strip_all(0, strip_recv).wait()

    got = landed[...].reshape(64, 128)
    in_flux = jnp.where(lane < 32, got, 0.0)
    p0, p1, p2 = parts3(in_flux)
    coded = (p0 + pltpu.roll(p1, 32, 1) + pltpu.roll(p2, 64, 1)).astype(BF16)
    values = dot(coded, ecode[...], ((1,), (0,)))
    values = jnp.concatenate([values[:, k * 128 : (k + 1) * 128] for k in range(16)], axis=0)
    values = (values * mask[...]).astype(BF16)
    summed = dot(values, lohot[...], ((0,), (0,)))
    add_source = summed[0:8] + summed[32:40] + summed[64:72]
    add_diag = summed[8:16] + summed[40:48] + summed[72:80]

    diag = diag + add_diag
    r0 = fixed + add_source - diag * x0
    w1 = (diag - SHIFT) * r0 - off_diagonal(r0)
    w2 = (diag - SHIFT) * w1 - off_diagonal(w1)
    sums = [total(r0 * r0), total(r0 * w1), total(w1 * w1), total(w1 * w2)]

    held = jnp.concatenate([x0, r0, w1, jnp.zeros((8, 128), F32)], axis=0)
    held = jnp.concatenate(list(parts3(held)) + [jnp.zeros((32, 128), F32)], axis=0).astype(BF16)
    found = dot(lohot[...], held, ((1,), (1,)))
    found = (found * mask[...]).astype(BF16)
    found = jnp.concatenate([found[k * 64 : (k + 1) * 64, :] for k in range(16)], axis=1)
    found = dot(found, fcode[...], ((1,), (0,)))
    for n in range(4):
        found = jnp.where(lane == 48 + n, sums[n], found)
    returned[...] = found.reshape(64, 1, 128)
    strip_start(1)
    received[si] = returned[j * groups + g]
    strip_all(1, strip_recv).wait()
    back = received[...].reshape(64, 128)
    tot[...] = jnp.sum(back, axis=0, keepdims=True)

    def band_copy(i):
        return pltpu.make_async_remote_copy(
            src_ref=tot,
            dst_ref=rtot.at[gi],
            send_sem=band_send,
            recv_sem=band_recv,
            device_id=(lax.rem(gi + i, bands), si),
            device_id_type=MESH,
        )

    def band_go(i, carry):
        band_copy(i).start()
        return carry

    lax.fori_loop(1, bands, band_go, 0)

    def band_all(sem):
        rest = pl.ds(0, bands - 1)
        return pltpu.make_async_copy(laid_out.at[rest], rtot.at[rest], sem)

    back = jnp.where(lane < 48, back, 0.0)
    rows = functools.reduce(
        jnp.add, [dot(p.astype(BF16), dhot[...], ((0,), (0,))) for p in parts3(back)]
    )
    rows = rows * place[...]
    row_x0 = jnp.sum(rows[0:16], axis=0, keepdims=True)
    row_r0 = jnp.sum(rows[16:32], axis=0, keepdims=True)
    row_w1 = jnp.sum(rows[32:48], axis=0, keepdims=True)

    rtot[gi] = tot[...]

    band_all(band_recv).wait()
    lane1 = iota((1, 128), 1)
    whole = functools.reduce(jnp.add, [rtot[n] for n in range(bands)])

    def lane_value(n):
        return jnp.sum(jnp.where(lane1 == 48 + n, whole, 0.0), axis=1, keepdims=True)

    n0, n1, n2, n3 = [lane_value(n) for n in range(4)]
    delta = n1 / n0
    second = n2 / n0
    spread_of = second - delta * delta
    theta = SHIFT + delta
    third = n3 / n0 - 3.0 * delta * second + 2.0 * delta * delta * delta
    wide_enough = spread_of > 1e-7 * theta * theta
    spread_of = jnp.maximum(spread_of, 0.0)
    skew = jnp.where(wide_enough, third / jnp.where(wide_enough, spread_of, 1.0), 0.0)
    step0 = 1.0 / theta
    growth = spread_of / (theta * theta)
    step1 = 1.0 / (theta + skew - spread_of / theta)
    by_r0 = step0 + step1 * (growth + step0 * delta)
    by_w1 = -step1 * step0
    solid_out[0] = x0 + by_r0 * r0 + by_w1 * w1
    rows_out[...] = row_x0 + by_r0 * row_r0 + by_w1 * row_w1

    for step in range(STEPS):
        for c in halo(step):
            c.wait_send()
    strip_all(0, strip_send).wait()
    strip_all(1, strip_send).wait()
    band_all(band_send).wait()


def publish(*refs):
    for source, target in zip(refs[:4], refs[4:]):
        target[...] = source[...]


def solution(mesh):
    bands = mesh.shape["grp"]
    subs = mesh.shape["sub"]
    groups = subs // 8

    def body(
        populations,
        heat_pops,
        solid_frac,
        coupled_grid_point,
        dest_index,
        heat_coeff,
        slot_node,
        node_diag,
        coupling,
        block_pattern,
        heat_source,
        solid_start,
    ):
        vmem = pl.BlockSpec(memory_space=pltpu.VMEM)
        smem = pl.BlockSpec(memory_space=pltpu.SMEM)
        dma = pltpu.SemaphoreType.DMA
        shapes = (
                jax.ShapeDtypeStruct((2, 8, CY), F32),
                jax.ShapeDtypeStruct((3, 2, 8, CY), F32),
                jax.ShapeDtypeStruct((1, 8, 128), F32),
                jax.ShapeDtypeStruct((1, 512), F32),
            )
        made = pl.pallas_call(
            functools.partial(kernel, groups, bands),
            out_shape=shapes,
            in_specs=[vmem] * 9 + [smem] + [vmem] * 2,
            out_specs=(vmem,) * 4,
            scratch_shapes=[
                pltpu.VMEM((26, 2, 8, CY), F32),
                pltpu.VMEM((26, 2, 8, CY), F32),
                pltpu.VMEM((STEPS, 2, 6, 8, CY), F32),
                pltpu.VMEM((STEPS, 2, 6, 8, CY), F32),
                pltpu.VMEM((STEPS, 2, 16, CY), F32),
                pltpu.VMEM((STEPS, 2, 16, CY), F32),
                pltpu.VMEM((STEPS, 4, 8, CY), F32),
                pltpu.VMEM((1024, 256), BF16),
                pltpu.VMEM((1024, 256), BF16),
                pltpu.VMEM((1024, 128), BF16),
                pltpu.VMEM((1024, 128), F32),
                pltpu.VMEM((128, 512), F32),
                pltpu.VMEM((64, 512), BF16),
                pltpu.VMEM((128, 512), BF16),
                pltpu.VMEM((128, 2048), BF16),
                pltpu.VMEM((2048, 128), BF16),
                *[pltpu.VMEM((64, 1, 128), F32)] * 4,
                pltpu.VMEM((1, 128), F32),
                pltpu.VMEM((bands, 1, 128), F32),
                dma((STEPS, 8)),
                dma((STEPS, 8)),
                dma((2,)),
                dma((2,)),
                dma,
                dma,
                pltpu.SemaphoreType.REGULAR((5,)),
            ],
            compiler_params=pltpu.CompilerParams(collective_id=0, has_side_effects=True),
            name="coupled_step",
        )(
            populations,
            heat_pops,
            solid_frac,
            coupled_grid_point,
            dest_index[..., 0],
            heat_coeff,
            slot_node.reshape(8, 128),
            node_diag,
            coupling,
            block_pattern,
            heat_source,
            solid_start,
        )
        return pl.pallas_call(
            publish,
            out_shape=shapes,
            in_specs=[vmem] * 4,
            out_specs=(vmem,) * 4,
            name="publish",
        )(*made)

    band = P("grp", "sub")
    block = P("grp", "sub", None)
    return jax.shard_map(
        body,
        mesh=mesh,
        in_specs=(
            P(None, "sub", "grp", None),
            P(None, "sub", "grp", None),
            P("sub", "grp", None),
            band,
            block,
            band,
            band,
            block,
            P("grp", "sub", None, None),
            band,
            block,
            block,
        ),
        out_specs=(P("sub", "grp", None), P(None, "sub", "grp", None), block, band),
        check_vma=False,
    )
```

```python
import functools

import jax
import jax.numpy as jnp
import numpy as np
from jax import lax
from jax.experimental import pallas as pl
from jax.experimental.pallas import tpu as pltpu
from jax.sharding import PartitionSpec as P

MESH = pl.DeviceIdType.MESH
F32 = jnp.float32
BF16 = jnp.bfloat16
I32 = jnp.int32

STEPS = 2
CY = 384
CAP = 16
SHIFT = 4.0

FLOW = [
    (0, 0, 0),
    (1, 0, 0),
    (-1, 0, 0),
    (0, 1, 0),
    (0, -1, 0),
    (0, 0, 1),
    (0, 0, -1),
    (1, 1, 0),
    (-1, -1, 0),
    (1, -1, 0),
    (-1, 1, 0),
    (1, 0, 1),
    (-1, 0, -1),
    (1, 0, -1),
    (-1, 0, 1),
    (0, 1, 1),
    (0, -1, -1),
    (0, 1, -1),
    (0, -1, 1),
]
EVERY = FLOW + FLOW[:7]
WEIGHT = [1.0 / 3.0] + [1.0 / 18.0] * 6 + [1.0 / 36.0] * 12
HEAT_WEIGHT = [0.25] + [0.125] * 6
TAU_FLOW = 0.8
TAU_HEAT = 0.7

X_UP = [i for i, e in enumerate(EVERY) if e[0] == 1]
X_DOWN = [i for i, e in enumerate(EVERY) if e[0] == -1]
Z_UP = [i for i, e in enumerate(EVERY) if e[2] == 1]
Z_DOWN = [i for i, e in enumerate(EVERY) if e[2] == -1]
EDGES = [
    next(i for i, e in enumerate(FLOW) if e == (1, 0, 1)),
    next(i for i, e in enumerate(FLOW) if e == (-1, 0, 1)),
    next(i for i, e in enumerate(FLOW) if e == (1, 0, -1)),
    next(i for i, e in enumerate(FLOW) if e == (-1, 0, -1)),
]


def dot(a, b, dims):
    return lax.dot_general(a, b, (dims, ((), ())), preferred_element_type=F32)


def parts3(v):
    a = v.astype(BF16).astype(F32)
    rest = v - a
    b = rest.astype(BF16).astype(F32)
    return a, b, rest - b


def iota(shape, dim):
    return lax.broadcasted_iota(I32, shape, dim)


def total(v):
    return jnp.sum(jnp.sum(v, axis=1, keepdims=True), axis=0, keepdims=True)


def kernel(
    groups,
    bands,
    pops_ref,
    heat_ref,
    solid_ref,
    voxel_ref,
    dest_ref,
    coeff_ref,
    slot_ref,
    diag_ref,
    coup_ref,
    pat_ref,
    source_ref,
    start_ref,
    temp_out,
    motion_out,
    solid_out,
    rows_out,
    cur,
    post,
    zs,
    zr,
    xs,
    xr,
    er,
    chop,
    cthop,
    lohot,
    mask,
    place,
    dhot,
    lo_vox,
    ecode,
    fcode,
    laid_out,
    block_out,
    block_in,
    landed,
    returned,
    received,
    tot,
    rtot,
    halo_send,
    halo_recv,
    strip_send,
    strip_recv,
    band_send,
    band_recv,
    block_send,
    block_recv,
    ready,
):
    subs = groups * 8
    gi = lax.axis_index("grp")
    si = lax.axis_index("sub")
    g = si // 8
    j = si % 8
    g_up = lax.rem(gi + 1, bands)
    g_dn = lax.rem(gi + bands - 1, bands)
    s_up = lax.rem(si + 1, subs)
    s_dn = lax.rem(si + subs - 1, subs)

    barrier = pltpu.get_barrier_semaphore()

    def greet(a, b):
        pl.semaphore_signal(barrier, inc=1, device_id=(a, b), device_id_type=MESH)

    for a, b in (
        (gi, s_up),
        (gi, s_dn),
        (g_up, si),
        (g_dn, si),
        (g_up, s_up),
        (g_up, s_dn),
        (g_dn, s_up),
        (g_dn, s_dn),
    ):
        greet(a, b)

    def tell(n):
        d = 1 << n
        to = [(gi, lax.rem(si + d, subs)), (gi, lax.rem(si + subs - d, subs))]
        if 2 * d < bands:
            to += [(lax.rem(gi + d, bands), si), (lax.rem(gi + bands - d, bands), si)]
        for a, b in to:
            pl.semaphore_signal(ready.at[n], inc=1, device_id=(a, b), device_id_type=MESH)

    def hear(n):
        pl.semaphore_wait(ready.at[n], 4 if 2 << n < bands else 2)

    sub8 = iota((8, 128), 0)
    lane = iota((64, 128), 1)
    xs[:, :, 8:16] = jnp.zeros((STEPS, 2, 8, CY), F32)

    def slot_tables():
        a_of = iota((128, 2048), 0)
        spread = jnp.where(a_of == iota((128, 2048), 1) // 128, 1.0, 0.0).astype(BF16)
        slots = slot_ref[...]
        rolled = [slots] + [pltpu.roll(slots, 128 - 16 * a, 1) for a in range(1, 8)]
        slots = jnp.concatenate(rolled, axis=0)
        slot_hi = (slots // 128).astype(F32).astype(BF16)
        slot_lo = (slots % 128).astype(F32).astype(BF16)
        hi_all = dot(slot_hi, spread, ((1,), (0,)))
        lo_all = dot(slot_lo, spread, ((1,), (0,)))
        for k in range(16):
            cols = slice(k * 128, (k + 1) * 128)
            rows = pl.ds(k * 64, 64)
            lohot[rows, :] = jnp.where(lo_all[:, cols] == lane.astype(F32), 1.0, 0.0).astype(BF16)
            mask[rows, :] = jnp.where(hi_all[:, cols] == (lane % 8).astype(F32), 1.0, 0.0)

    def row_tables():
        dest = dest_ref[...]
        dest_hot = jnp.where(iota((64, 512), 0) == dest, 1.0, 0.0)
        dhot[...] = dest_hot.astype(BF16)
        ahead = jnp.where(iota((512, 512), 0) < iota((512, 512), 1), 1.0, 0.0).astype(BF16)
        counts = dot(dest_hot.astype(BF16), ahead, ((1,), (0,)))
        at = jnp.sum(dest_hot * counts, axis=0, keepdims=True)
        place[...] = jnp.where((iota((128, 512), 0) % 16).astype(F32) == at, 1.0, 0.0)

    def code_tables():
        wide = 16 * 128
        a_of = iota((128, wide), 0)
        c_of = iota((128, wide), 1)
        k_of = c_of // 128
        lane_of = c_of % 128
        p_of = lane_of // 32
        t_of = (lane_of // 8) % 4
        ecode[...] = jnp.where(
            (a_of == p_of * 32 + t_of * 16 + k_of) & (p_of < 3) & (t_of < 2), 1.0, 0.0
        ).astype(BF16)
        c_of = iota((wide, 128), 0)
        l_of = iota((wide, 128), 1)
        k_of = c_of // 128
        lane_of = c_of % 128
        p_of = lane_of // 32
        t_of = (lane_of // 8) % 4
        fcode[...] = jnp.where((l_of == t_of * 16 + k_of) & (p_of < 3) & (t_of < 3), 1.0, 0.0).astype(
            BF16
        )

    def coupling_tables():
        for b in range(8):
            block = coup_ref[0, b]
            high = block.astype(BF16).astype(F32)
            low = block - high
            rows = pl.ds(b * 128, 128)
            chop[rows, 0:128] = high.astype(BF16)
            chop[rows, 128:256] = low.astype(BF16)
            cthop[rows, 0:128] = high.T.astype(BF16)
            cthop[rows, 128:256] = low.T.astype(BF16)

    voxel = voxel_ref[...]
    lo_vox[...] = jnp.where(iota((128, 512), 0) == voxel % 128, 1.0, 0.0).astype(BF16)
    over = voxel // 128
    layer_x = over // 3
    vox_row = (over - layer_x * 3) * 16 + layer_x

    pat = [pat_ref[0, b] for b in range(8)]
    pat_col = jnp.zeros((8, 128), I32)
    for b in range(8):
        pat_col = jnp.where(sub8 == b, pat[b], pat_col)

    def block_dot(v, table):
        high = v.astype(BF16).astype(F32)
        low = v - high
        left = jnp.concatenate([jnp.where(sub8 == b, high, 0.0) for b in range(8)], axis=1)
        right = jnp.concatenate([jnp.where(sub8 == b, low, 0.0) for b in range(8)], axis=1)
        both = jnp.concatenate([left, right], axis=0).astype(BF16)
        out = dot(both, table[...], ((1,), (0,)))
        return out[0:8, 0:128] + out[8:16, 0:128] + out[0:8, 128:256]

    def off_diagonal(v):
        partner = jnp.zeros((8, 128), F32)
        for k in range(8):
            partner = jnp.where(pat_col == k, v[k : k + 1, :], partner)
        forward = block_dot(partner, cthop)
        terms = block_dot(v, chop)
        backward = jnp.zeros((8, 128), F32)
        for b in range(8):
            backward = backward + jnp.where(sub8 == pat[b], terms[b : b + 1, :], 0.0)
        return forward + backward

    def collide(step):
        for z in range(2):
            for c in range(3):
                cols = slice(c * 128, (c + 1) * 128)
                if step == 0:
                    f = [pops_ref[i, z, :, cols] for i in range(19)]
                    heat = [heat_ref[i, z, :, cols] for i in range(7)]
                else:
                    f = [cur[i, z, :, cols] for i in range(19)]
                    heat = [cur[19 + i, z, :, cols] for i in range(7)]
                solid = solid_ref[z, :, cols]
                rho = functools.reduce(jnp.add, f)
                m = []
                for d in range(3):
                    pos = [f[i] for i in range(19) if FLOW[i][d] == 1]
                    neg = [f[i] for i in range(19) if FLOW[i][d] == -1]
                    m.append(functools.reduce(jnp.add, pos) - functools.reduce(jnp.add, neg))
                u = [v / rho for v in m]
                flat = 1.0 - 1.5 * (u[0] * u[0] + u[1] * u[1] + u[2] * u[2])
                fluid = 1.0 - solid
                keep = fluid * (1.0 - 1.0 / TAU_FLOW)
                gain = fluid * rho * (1.0 / TAU_FLOW)
                out = [None] * 26
                out[0] = (keep + solid) * f[0] + gain * WEIGHT[0] * flat
                for i in range(1, 19, 2):
                    along = None
                    for d in range(3):
                        if FLOW[i][d] == 1:
                            along = u[d] if along is None else along + u[d]
                        elif FLOW[i][d] == -1:
                            along = -u[d] if along is None else along - u[d]
                    even = flat + 4.5 * along * along
                    odd = 3.0 * along
                    scale = gain * WEIGHT[i]
                    out[i] = keep * f[i] + solid * f[i + 1] + scale * (even + odd)
                    out[i + 1] = keep * f[i + 1] + solid * f[i] + scale * (even - odd)
                hot = functools.reduce(jnp.add, heat)
                for i in range(7):
                    share = hot * (HEAT_WEIGHT[i] / TAU_HEAT)
                    if i > 0:
                        d = [abs(v) for v in FLOW[i]].index(1)
                        sign = FLOW[i][d]
                        share = share * (1.0 + (4.0 * sign) * u[d])
                    out[19 + i] = (1.0 - 1.0 / TAU_HEAT) * heat[i] + share
                for i in range(26):
                    ez = EVERY[i][2]
                    post[i, z, :, cols] = out[i]
                    if ez == 1 and z == 1:
                        zs[step, 0, Z_UP.index(i), :, cols] = out[i]
                    if ez == -1 and z == 0:
                        zs[step, 1, Z_DOWN.index(i), :, cols] = out[i]
                    if EVERY[i][0] == 1:
                        r = X_UP.index(i) * 2 + z
                        xs[step, 0, r : r + 1, cols] = out[i][7:8, :]
                    if EVERY[i][0] == -1:
                        r = X_DOWN.index(i) * 2 + z
                        xs[step, 1, r : r + 1, cols] = out[i][0:1, :]

    def halo(step):
        made = []

        def put(n, src, dst, a, b):
            made.append(
                pltpu.make_async_remote_copy(
                    src_ref=src,
                    dst_ref=dst,
                    send_sem=halo_send.at[step, n],
                    recv_sem=halo_recv.at[step, n],
                    device_id=(a, b),
                    device_id_type=MESH,
                )
            )

        put(0, zs.at[step, 0, Z_UP.index(EDGES[0])], er.at[step, 0], g_up, s_up)
        put(1, zs.at[step, 0, Z_UP.index(EDGES[1])], er.at[step, 1], g_dn, s_up)
        put(2, zs.at[step, 1, Z_DOWN.index(EDGES[2])], er.at[step, 2], g_up, s_dn)
        put(3, zs.at[step, 1, Z_DOWN.index(EDGES[3])], er.at[step, 3], g_dn, s_dn)
        put(4, xs.at[step, 0], xr.at[step, 0], g_up, si)
        put(5, xs.at[step, 1], xr.at[step, 1], g_dn, si)
        put(6, zs.at[step, 0], zr.at[step, 0], gi, s_up)
        put(7, zs.at[step, 1], zr.at[step, 1], gi, s_dn)
        return made

    edge8 = iota((8, CY), 0)

    def stream(step, arrived):
        for i in range(26):
            ex, ey, ez = EVERY[i]
            for z in range(2):
                edge = None
                inside = ez == 0 or z == (1 if ez == 1 else 0)
                if arrived == (inside and ex == 0):
                    continue
                if ez == 0 or (ez == 1 and z == 1) or (ez == -1 and z == 0):
                    source = z - ez
                    piece = post[i, source]
                    if ex == 1:
                        r = X_UP.index(i) * 2 + source
                        edge = xr[step, 0, r : r + 1, :]
                    if ex == -1:
                        r = X_DOWN.index(i) * 2 + source
                        edge = xr[step, 1, r : r + 1, :]
                else:
                    if ez == 1:
                        piece = zr[step, 0, Z_UP.index(i)]
                    else:
                        piece = zr[step, 1, Z_DOWN.index(i)]
                    if ex == 1:
                        edge = er[step, EDGES.index(i), 7:8, :]
                    if ex == -1:
                        edge = er[step, EDGES.index(i), 0:1, :]
                if ex == 1:
                    piece = jnp.where(edge8 == 0, edge, pltpu.roll(piece, 1, 0))
                if ex == -1:
                    piece = jnp.where(edge8 == 7, edge, pltpu.roll(piece, 7, 0))
                if ey == 1:
                    piece = pltpu.roll(piece, 1, 1)
                if ey == -1:
                    piece = pltpu.roll(piece, CY - 1, 1)
                cur[i, z] = piece

    collide(0)
    pl.semaphore_wait(barrier, 8)
    made = halo(0)
    for c in made:
        c.start()
    tell(0)
    stream(0, False)
    slot_tables()
    hear(0)
    tell(1)
    row_tables()
    hear(1)
    tell(2)
    coupling_tables()
    hear(2)
    tell(3)
    code_tables()
    for c in made:
        c.wait_recv()
    stream(0, True)
    collide(1)
    made = halo(1)
    for c in made:
        c.start()
    stream(1, False)
    x0 = start_ref[0]
    fixed = source_ref[0] + off_diagonal(x0)
    diag = diag_ref[0]
    for c in made:
        c.wait_recv()
    stream(1, True)

    hot_rows = []
    for z in range(2):
        hot = functools.reduce(jnp.add, [cur[19 + i, z] for i in range(7)])
        temp_out[z] = hot
        hot_rows.append(hot)
        for d in range(3):
            pos = [cur[i, z] for i in range(19) if FLOW[i][d] == 1]
            neg = [cur[i, z] for i in range(19) if FLOW[i][d] == -1]
            motion_out[d, z] = functools.reduce(jnp.add, pos) - functools.reduce(jnp.add, neg)

    table = jnp.concatenate(
        [hot_rows[z][:, c * 128 : (c + 1) * 128] for c in range(3) for z in range(2)], axis=0
    )
    picked = dot(
        jnp.concatenate(parts3(table), axis=0).astype(BF16), lo_vox[...], ((1,), (0,))
    )
    picked = picked[0:48] + picked[48:96] + picked[96:144]
    seen = jnp.sum(jnp.where(iota((48, 512), 0) == vox_row, picked, 0.0), axis=0, keepdims=True)
    coeff = coeff_ref[...]
    flux = coeff * seen
    placed = place[0:16, :]
    laid = []
    for pair in zip(parts3(flux), parts3(coeff)):
        laid.append(placed * pair[0])
        laid.append(placed * pair[1])
    laid.append(jnp.zeros((32, 512), F32))
    laid = jnp.concatenate(laid, axis=0).astype(BF16)
    sent = dot(dhot[...], laid, ((1,), (1,)))
    sent = sent + pltpu.roll(sent, 96, 1) + pltpu.roll(sent, 64, 1)
    laid_out[...] = sent.reshape(64, 1, 128)

    half = subs // 4

    def landing(source):
        return landed.at[(source % 8) * groups + source // 8]

    def row_copy(src, source, to):
        return pltpu.make_async_remote_copy(
            src_ref=src,
            dst_ref=landing(source),
            send_sem=strip_send.at[0],
            recv_sem=strip_recv.at[0],
            device_id=(gi, to),
            device_id_type=MESH,
        )

    for e in range(1, half + 1):
        block_out[0, e - 1] = laid_out[lax.rem(si + half + e, subs)]
        block_out[1, e - 1] = laid_out[lax.rem(si + subs - half - e, subs)]

    def block_copy(way):
        to = lax.rem(si + (half if way == 0 else subs - half), subs)
        return pltpu.make_async_remote_copy(
            src_ref=block_out.at[way],
            dst_ref=block_in.at[way],
            send_sem=block_send.at[way],
            recv_sem=block_recv.at[way],
            device_id=(gi, to),
            device_id_type=MESH,
        )

    hear(3)
    block_copy(0).start()
    block_copy(1).start()

    def near(i, carry):
        d = (half - i // 2) * (1 - 2 * (i % 2))
        to = lax.rem(si + subs + d, subs)
        row_copy(laid_out.at[to], si, to).start()
        return carry

    lax.fori_loop(0, 2 * half, near, 0)
    landed[j * groups + g] = laid_out[si]

    early = si // (subs // 2)
    for way in (early, 1 - early):
        pltpu.make_async_copy(block_out.at[way], block_in.at[way], block_recv.at[way]).wait()
        sign = 1 - 2 * way
        source = lax.rem(si + subs - sign * half, subs)

        def forward(e, way=way, sign=sign, source=source):
            to = lax.rem(si + subs + sign * e, subs)
            row_copy(block_in.at[way, e - 1], source, to).start()

        @pl.when(way == 0)
        def _(forward=forward):
            forward(half)

        def forward_all(i, carry, forward=forward):
            forward(half - 1 - i)
            return carry

        lax.fori_loop(0, half - 1, forward_all, 0)

    def back_copy(i):
        d = subs // 2 + (1 - 2 * (i % 2)) * ((i + 1) // 2)
        to = lax.rem(si + d, subs)
        return pltpu.make_async_remote_copy(
            src_ref=returned.at[(to % 8) * groups + to // 8],
            dst_ref=received.at[si],
            send_sem=strip_send.at[1],
            recv_sem=strip_recv.at[1],
            device_id=(gi, to),
            device_id_type=MESH,
        )

    def back_go(i, carry):
        back_copy(i).start()
        return carry

    def strip_all(way, sem):
        src, dst = (laid_out, landed) if way == 0 else (returned, received)
        rest = pl.ds(0, subs - 1)
        return pltpu.make_async_copy(src.at[rest], dst.at[rest], sem.at[way])

    strip_all(0, strip_recv).wait()

    got = landed[...].reshape(64, 128)
    in_flux = jnp.where(lane < 32, got, 0.0)
    p0, p1, p2 = parts3(in_flux)
    coded = (p0 + pltpu.roll(p1, 32, 1) + pltpu.roll(p2, 64, 1)).astype(BF16)
    values = dot(coded, ecode[...], ((1,), (0,)))
    values = jnp.concatenate([values[:, k * 128 : (k + 1) * 128] for k in range(16)], axis=0)
    values = (values * mask[...]).astype(BF16)
    summed = dot(values, lohot[...], ((0,), (0,)))
    add_source = summed[0:8] + summed[32:40] + summed[64:72]
    add_diag = summed[8:16] + summed[40:48] + summed[72:80]

    diag = diag + add_diag
    r0 = fixed + add_source - diag * x0
    w1 = (diag - SHIFT) * r0 - off_diagonal(r0)
    w2 = (diag - SHIFT) * w1 - off_diagonal(w1)
    sums = [total(r0 * r0), total(r0 * w1), total(w1 * w1), total(w1 * w2)]

    held = jnp.concatenate([x0, r0, w1, jnp.zeros((8, 128), F32)], axis=0)
    held = jnp.concatenate(list(parts3(held)) + [jnp.zeros((32, 128), F32)], axis=0).astype(BF16)
    found = dot(lohot[...], held, ((1,), (1,)))
    found = (found * mask[...]).astype(BF16)
    found = jnp.concatenate([found[k * 64 : (k + 1) * 64, :] for k in range(16)], axis=1)
    found = dot(found, fcode[...], ((1,), (0,)))
    for n in range(4):
        found = jnp.where(lane == 48 + n, sums[n], found)
    returned[...] = found.reshape(64, 1, 128)
    lax.fori_loop(0, subs - 1, back_go, 0)
    received[si] = returned[j * groups + g]
    strip_all(1, strip_recv).wait()
    back = received[...].reshape(64, 128)
    tot[...] = jnp.sum(back, axis=0, keepdims=True)

    def band_copy(i):
        return pltpu.make_async_remote_copy(
            src_ref=tot,
            dst_ref=rtot.at[gi],
            send_sem=band_send,
            recv_sem=band_recv,
            device_id=(lax.rem(gi + i, bands), si),
            device_id_type=MESH,
        )

    def band_go(i, carry):
        band_copy(i).start()
        return carry

    lax.fori_loop(1, bands, band_go, 0)

    def band_all(sem):
        rest = pl.ds(0, bands - 1)
        return pltpu.make_async_copy(laid_out.at[rest], rtot.at[rest], sem)

    back = jnp.where(lane < 48, back, 0.0)
    rows = functools.reduce(
        jnp.add, [dot(p.astype(BF16), dhot[...], ((0,), (0,))) for p in parts3(back)]
    )
    rows = rows * place[...]
    row_x0 = jnp.sum(rows[0:16], axis=0, keepdims=True)
    row_r0 = jnp.sum(rows[16:32], axis=0, keepdims=True)
    row_w1 = jnp.sum(rows[32:48], axis=0, keepdims=True)

    rtot[gi] = tot[...]

    band_all(band_recv).wait()
    lane1 = iota((1, 128), 1)
    whole = functools.reduce(jnp.add, [rtot[n] for n in range(bands)])

    def lane_value(n):
        return jnp.sum(jnp.where(lane1 == 48 + n, whole, 0.0), axis=1, keepdims=True)

    n0, n1, n2, n3 = [lane_value(n) for n in range(4)]
    delta = n1 / n0
    second = n2 / n0
    spread_of = second - delta * delta
    theta = SHIFT + delta
    third = n3 / n0 - 3.0 * delta * second + 2.0 * delta * delta * delta
    wide_enough = spread_of > 1e-7 * theta * theta
    spread_of = jnp.maximum(spread_of, 0.0)
    skew = jnp.where(wide_enough, third / jnp.where(wide_enough, spread_of, 1.0), 0.0)
    step0 = 1.0 / theta
    growth = spread_of / (theta * theta)
    step1 = 1.0 / (theta + skew - spread_of / theta)
    by_r0 = step0 + step1 * (growth + step0 * delta)
    by_w1 = -step1 * step0
    solid_out[0] = x0 + by_r0 * r0 + by_w1 * w1
    rows_out[...] = row_x0 + by_r0 * row_r0 + by_w1 * row_w1

    for step in range(STEPS):
        for c in halo(step):
            c.wait_send()
    block_copy(0).wait_send()
    block_copy(1).wait_send()
    strip_all(0, strip_send).wait()
    strip_all(1, strip_send).wait()
    band_all(band_send).wait()


def publish(*refs):
    for source, target in zip(refs[:4], refs[4:]):
        target[...] = source[...]


def solution(mesh):
    bands = mesh.shape["grp"]
    subs = mesh.shape["sub"]
    groups = subs // 8

    def body(
        populations,
        heat_pops,
        solid_frac,
        coupled_grid_point,
        dest_index,
        heat_coeff,
        slot_node,
        node_diag,
        coupling,
        block_pattern,
        heat_source,
        solid_start,
    ):
        vmem = pl.BlockSpec(memory_space=pltpu.VMEM)
        smem = pl.BlockSpec(memory_space=pltpu.SMEM)
        dma = pltpu.SemaphoreType.DMA
        shapes = (
                jax.ShapeDtypeStruct((2, 8, CY), F32),
                jax.ShapeDtypeStruct((3, 2, 8, CY), F32),
                jax.ShapeDtypeStruct((1, 8, 128), F32),
                jax.ShapeDtypeStruct((1, 512), F32),
            )
        made = pl.pallas_call(
            functools.partial(kernel, groups, bands),
            out_shape=tuple(pltpu.VMEM(v.shape, v.dtype) for v in shapes),
            in_specs=[vmem] * 9 + [smem] + [vmem] * 2,
            out_specs=(vmem,) * 4,
            scratch_shapes=[
                pltpu.VMEM((26, 2, 8, CY), F32),
                pltpu.VMEM((26, 2, 8, CY), F32),
                pltpu.VMEM((STEPS, 2, 6, 8, CY), F32),
                pltpu.VMEM((STEPS, 2, 6, 8, CY), F32),
                pltpu.VMEM((STEPS, 2, 16, CY), F32),
                pltpu.VMEM((STEPS, 2, 16, CY), F32),
                pltpu.VMEM((STEPS, 4, 8, CY), F32),
                pltpu.VMEM((1024, 256), BF16),
                pltpu.VMEM((1024, 256), BF16),
                pltpu.VMEM((1024, 128), BF16),
                pltpu.VMEM((1024, 128), F32),
                pltpu.VMEM((128, 512), F32),
                pltpu.VMEM((64, 512), BF16),
                pltpu.VMEM((128, 512), BF16),
                pltpu.VMEM((128, 2048), BF16),
                pltpu.VMEM((2048, 128), BF16),
                pltpu.VMEM((64, 1, 128), F32),
                *[pltpu.VMEM((2, 16, 1, 128), F32)] * 2,
                *[pltpu.VMEM((64, 1, 128), F32)] * 3,
                pltpu.VMEM((1, 128), F32),
                pltpu.VMEM((bands, 1, 128), F32),
                dma((STEPS, 8)),
                dma((STEPS, 8)),
                dma((2,)),
                dma((2,)),
                dma,
                dma,
                dma((2,)),
                dma((2,)),
                pltpu.SemaphoreType.REGULAR((4,)),
            ],
            compiler_params=pltpu.CompilerParams(collective_id=0, has_side_effects=True),
            name="coupled_step",
        )(
            populations,
            heat_pops,
            solid_frac,
            coupled_grid_point,
            dest_index[..., 0],
            heat_coeff,
            slot_node.reshape(8, 128),
            node_diag,
            coupling,
            block_pattern,
            heat_source,
            solid_start,
        )
        return pl.pallas_call(
            publish,
            out_shape=shapes,
            in_specs=[vmem] * 4,
            out_specs=(vmem,) * 4,
            name="publish",
        )(*[pltpu.with_memory_space_constraint(v, pltpu.VMEM) for v in made])

    band = P("grp", "sub")
    block = P("grp", "sub", None)
    return jax.shard_map(
        body,
        mesh=mesh,
        in_specs=(
            P(None, "sub", "grp", None),
            P(None, "sub", "grp", None),
            P("sub", "grp", None),
            band,
            block,
            band,
            band,
            block,
            P("grp", "sub", None, None),
            band,
            block,
            block,
        ),
        out_specs=(P("sub", "grp", None), P(None, "sub", "grp", None), block, band),
        check_vma=False,
    )
```

```python
import functools

import jax
import jax.numpy as jnp
import numpy as np
from jax import lax
from jax.experimental import pallas as pl
from jax.experimental.pallas import tpu as pltpu
from jax.sharding import PartitionSpec as P

MESH = pl.DeviceIdType.MESH
F32 = jnp.float32
BF16 = jnp.bfloat16
I32 = jnp.int32

STEPS = 2
CY = 384
CAP = 16
SHIFT = 4.0

FLOW = [
    (0, 0, 0),
    (1, 0, 0),
    (-1, 0, 0),
    (0, 1, 0),
    (0, -1, 0),
    (0, 0, 1),
    (0, 0, -1),
    (1, 1, 0),
    (-1, -1, 0),
    (1, -1, 0),
    (-1, 1, 0),
    (1, 0, 1),
    (-1, 0, -1),
    (1, 0, -1),
    (-1, 0, 1),
    (0, 1, 1),
    (0, -1, -1),
    (0, 1, -1),
    (0, -1, 1),
]
EVERY = FLOW + FLOW[:7]
WEIGHT = [1.0 / 3.0] + [1.0 / 18.0] * 6 + [1.0 / 36.0] * 12
HEAT_WEIGHT = [0.25] + [0.125] * 6
TAU_FLOW = 0.8
TAU_HEAT = 0.7

X_UP = [i for i, e in enumerate(EVERY) if e[0] == 1]
X_DOWN = [i for i, e in enumerate(EVERY) if e[0] == -1]
Z_UP = [i for i, e in enumerate(EVERY) if e[2] == 1]
Z_DOWN = [i for i, e in enumerate(EVERY) if e[2] == -1]
EDGES = [
    next(i for i, e in enumerate(FLOW) if e == (1, 0, 1)),
    next(i for i, e in enumerate(FLOW) if e == (-1, 0, 1)),
    next(i for i, e in enumerate(FLOW) if e == (1, 0, -1)),
    next(i for i, e in enumerate(FLOW) if e == (-1, 0, -1)),
]


def dot(a, b, dims):
    return lax.dot_general(a, b, (dims, ((), ())), preferred_element_type=F32)


def parts3(v):
    a = v.astype(BF16).astype(F32)
    rest = v - a
    b = rest.astype(BF16).astype(F32)
    return a, b, rest - b


def iota(shape, dim):
    return lax.broadcasted_iota(I32, shape, dim)


def total(v):
    return jnp.sum(jnp.sum(v, axis=1, keepdims=True), axis=0, keepdims=True)


def kernel(
    groups,
    bands,
    pops_ref,
    heat_ref,
    solid_ref,
    voxel_ref,
    dest_ref,
    coeff_ref,
    slot_ref,
    diag_ref,
    coup_ref,
    pat_ref,
    source_ref,
    start_ref,
    temp_out,
    motion_out,
    solid_out,
    rows_out,
    cur,
    post,
    zs,
    zr,
    xs,
    xr,
    er,
    chop,
    cthop,
    lohot,
    lohot_t,
    xh_s,
    xh_r,
    vel,
    coup,
    mask,
    place,
    dhot,
    lo_vox,
    ecode,
    fcode,
    laid_out,
    block_out,
    block_in,
    landed,
    returned,
    received,
    tot,
    rtot,
    halo_send,
    halo_recv,
    strip_send,
    strip_recv,
    band_send,
    band_recv,
    block_send,
    block_recv,
    heat_send,
    heat_recv,
    coup_sem,
    ready,
):
    subs = groups * 8
    gi = lax.axis_index("grp")
    si = lax.axis_index("sub")
    g = si // 8
    j = si % 8
    g_up = lax.rem(gi + 1, bands)
    g_dn = lax.rem(gi + bands - 1, bands)
    s_up = lax.rem(si + 1, subs)
    s_dn = lax.rem(si + subs - 1, subs)

    fetch = pltpu.make_async_copy(coup_ref.at[0], coup, coup_sem)
    fetch.start()
    barrier = pltpu.get_barrier_semaphore()

    def greet(a, b):
        pl.semaphore_signal(barrier, inc=1, device_id=(a, b), device_id_type=MESH)

    for a, b in (
        (gi, s_up),
        (gi, s_dn),
        (g_up, si),
        (g_dn, si),
        (g_up, s_up),
        (g_up, s_dn),
        (g_dn, s_up),
        (g_dn, s_dn),
    ):
        greet(a, b)

    def tell(n):
        d = 1 << n
        to = [(gi, lax.rem(si + d, subs)), (gi, lax.rem(si + subs - d, subs))]
        if 2 * d < bands:
            to += [(lax.rem(gi + d, bands), si), (lax.rem(gi + bands - d, bands), si)]
        for a, b in to:
            pl.semaphore_signal(ready.at[n], inc=1, device_id=(a, b), device_id_type=MESH)

    def hear(n):
        pl.semaphore_wait(ready.at[n], 4 if 2 << n < bands else 2)

    sub8 = iota((8, 128), 0)
    lane = iota((64, 128), 1)
    xs[:, :, 8:16] = jnp.zeros((STEPS, 2, 8, CY), F32)
    xh_s[...] = jnp.zeros((2, 8, CY), F32)

    def slot_tables():
        a_of = iota((128, 2048), 0)
        spread = jnp.where(a_of == iota((128, 2048), 1) // 128, 1.0, 0.0).astype(BF16)
        slots = slot_ref[...]
        rolled = [slots] + [pltpu.roll(slots, 128 - 16 * a, 1) for a in range(1, 8)]
        slots = jnp.concatenate(rolled, axis=0)
        slot_hi = (slots // 128).astype(F32).astype(BF16)
        slot_lo = (slots % 128).astype(F32).astype(BF16)
        hi_all = dot(slot_hi, spread, ((1,), (0,)))
        lo_all = dot(slot_lo, spread, ((1,), (0,)))
        for k in range(16):
            cols = slice(k * 128, (k + 1) * 128)
            rows = pl.ds(k * 64, 64)
            lohot[rows, :] = jnp.where(lo_all[:, cols] == lane.astype(F32), 1.0, 0.0).astype(BF16)
            lohot_t[:, k * 64 : (k + 1) * 64] = (
                jnp.where(lo_all[:, cols] == lane.astype(F32), 1.0, 0.0).T.astype(BF16)
            )
            mask[rows, :] = jnp.where(hi_all[:, cols] == (lane % 8).astype(F32), 1.0, 0.0)

    def row_tables():
        dest = dest_ref[...]
        dest_hot = jnp.where(iota((64, 512), 0) == dest, 1.0, 0.0)
        dhot[...] = dest_hot.astype(BF16)
        ahead = jnp.where(iota((512, 512), 0) < iota((512, 512), 1), 1.0, 0.0).astype(BF16)
        counts = dot(dest_hot.astype(BF16), ahead, ((1,), (0,)))
        at = jnp.sum(dest_hot * counts, axis=0, keepdims=True)
        place[...] = jnp.where((iota((128, 512), 0) % 16).astype(F32) == at, 1.0, 0.0)

    def code_tables():
        wide = 16 * 128
        a_of = iota((128, wide), 0)
        c_of = iota((128, wide), 1)
        k_of = c_of // 128
        lane_of = c_of % 128
        p_of = lane_of // 32
        t_of = (lane_of // 8) % 4
        ecode[...] = jnp.where(
            (a_of == p_of * 32 + t_of * 16 + k_of) & (p_of < 3) & (t_of < 2), 1.0, 0.0
        ).astype(BF16)
        c_of = iota((wide, 128), 0)
        l_of = iota((wide, 128), 1)
        k_of = c_of // 128
        lane_of = c_of % 128
        p_of = lane_of // 32
        t_of = (lane_of // 8) % 4
        fcode[...] = jnp.where((l_of == t_of * 16 + k_of) & (p_of < 3) & (t_of < 3), 1.0, 0.0).astype(
            BF16
        )

    def coupling_tables():
        for b in range(8):
            block = coup[b]
            high = block.astype(BF16).astype(F32)
            low = block - high
            rows = pl.ds(b * 128, 128)
            chop[rows, 0:128] = high.astype(BF16)
            chop[rows, 128:256] = low.astype(BF16)
            cthop[rows, 0:128] = high.T.astype(BF16)
            cthop[rows, 128:256] = low.T.astype(BF16)

    voxel = voxel_ref[...]
    lo_vox[...] = jnp.where(iota((128, 512), 0) == voxel % 128, 1.0, 0.0).astype(BF16)
    over = voxel // 128
    layer_x = over // 3
    vox_row = (over - layer_x * 3) * 16 + layer_x

    pat = [pat_ref[0, b] for b in range(8)]
    pat_col = jnp.zeros((8, 128), I32)
    for b in range(8):
        pat_col = jnp.where(sub8 == b, pat[b], pat_col)

    def block_dot(v, table):
        high = v.astype(BF16).astype(F32)
        low = v - high
        left = jnp.concatenate([jnp.where(sub8 == b, high, 0.0) for b in range(8)], axis=1)
        right = jnp.concatenate([jnp.where(sub8 == b, low, 0.0) for b in range(8)], axis=1)
        both = jnp.concatenate([left, right], axis=0).astype(BF16)
        out = dot(both, table[...], ((1,), (0,)))
        return out[0:8, 0:128] + out[8:16, 0:128] + out[0:8, 128:256]

    def off_diagonal(v):
        partner = jnp.zeros((8, 128), F32)
        for k in range(8):
            partner = jnp.where(pat_col == k, v[k : k + 1, :], partner)
        forward = block_dot(partner, cthop)
        terms = block_dot(v, chop)
        backward = jnp.zeros((8, 128), F32)
        for b in range(8):
            backward = backward + jnp.where(sub8 == pat[b], terms[b : b + 1, :], 0.0)
        return forward + backward

    def collide(step, part):
        for z in range(2):
            for c in range(3):
                cols = slice(c * 128, (c + 1) * 128)
                if step == 0:
                    f = [pops_ref[i, z, :, cols] for i in range(19)]
                    heat = [heat_ref[i, z, :, cols] for i in range(7)]
                else:
                    f = [cur[i, z, :, cols] for i in range(19)]
                    heat = [cur[19 + i, z, :, cols] for i in range(7)]
                if part == "flow":
                    rho = vel[3, z, :, cols]
                    u = [vel[d, z, :, cols] for d in range(3)]
                else:
                    rho = functools.reduce(jnp.add, f)
                    m = []
                    for d in range(3):
                        pos = [f[i] for i in range(19) if FLOW[i][d] == 1]
                        neg = [f[i] for i in range(19) if FLOW[i][d] == -1]
                        m.append(functools.reduce(jnp.add, pos) - functools.reduce(jnp.add, neg))
                    u = [v / rho for v in m]
                if part == "heat":
                    vel[3, z, :, cols] = rho
                    for d in range(3):
                        vel[d, z, :, cols] = u[d]
                out = [None] * 26
                if part != "heat":
                    solid = solid_ref[z, :, cols]
                    flat = 1.0 - 1.5 * (u[0] * u[0] + u[1] * u[1] + u[2] * u[2])
                    fluid = 1.0 - solid
                    keep = fluid * (1.0 - 1.0 / TAU_FLOW)
                    gain = fluid * rho * (1.0 / TAU_FLOW)
                    out[0] = (keep + solid) * f[0] + gain * WEIGHT[0] * flat
                    for i in range(1, 19, 2):
                        along = None
                        for d in range(3):
                            if FLOW[i][d] == 1:
                                along = u[d] if along is None else along + u[d]
                            elif FLOW[i][d] == -1:
                                along = -u[d] if along is None else along - u[d]
                        even = flat + 4.5 * along * along
                        odd = 3.0 * along
                        scale = gain * WEIGHT[i]
                        out[i] = keep * f[i] + solid * f[i + 1] + scale * (even + odd)
                        out[i + 1] = keep * f[i + 1] + solid * f[i] + scale * (even - odd)
                if part != "flow":
                    hot = functools.reduce(jnp.add, heat)
                    for i in range(7):
                        share = hot * (HEAT_WEIGHT[i] / TAU_HEAT)
                        if i > 0:
                            d = [abs(v) for v in FLOW[i]].index(1)
                            sign = FLOW[i][d]
                            share = share * (1.0 + (4.0 * sign) * u[d])
                        out[19 + i] = (1.0 - 1.0 / TAU_HEAT) * heat[i] + share
                for i in range(26):
                    if out[i] is None:
                        continue
                    ex, ez = EVERY[i][0], EVERY[i][2]
                    post[i, z, :, cols] = out[i]
                    if ez == 1 and z == 1:
                        zs[step, 0, Z_UP.index(i), :, cols] = out[i]
                    if ez == -1 and z == 0:
                        zs[step, 1, Z_DOWN.index(i), :, cols] = out[i]
                    if ex == 0:
                        continue
                    way = 0 if ex == 1 else 1
                    row = out[i][7:8, :] if ex == 1 else out[i][0:1, :]
                    if step == 1 and i >= 19:
                        xh_s[way, z : z + 1, cols] = row
                    else:
                        r = (X_UP if ex == 1 else X_DOWN).index(i) * 2 + z
                        xs[step, way, r : r + 1, cols] = row

    def halo(step):
        made = []

        def put(n, src, dst, a, b):
            made.append(
                pltpu.make_async_remote_copy(
                    src_ref=src,
                    dst_ref=dst,
                    send_sem=halo_send.at[step, n],
                    recv_sem=halo_recv.at[step, n],
                    device_id=(a, b),
                    device_id_type=MESH,
                )
            )

        put(0, zs.at[step, 0, Z_UP.index(EDGES[0])], er.at[step, 0], g_up, s_up)
        put(1, zs.at[step, 0, Z_UP.index(EDGES[1])], er.at[step, 1], g_dn, s_up)
        put(2, zs.at[step, 1, Z_DOWN.index(EDGES[2])], er.at[step, 2], g_up, s_dn)
        put(3, zs.at[step, 1, Z_DOWN.index(EDGES[3])], er.at[step, 3], g_dn, s_dn)
        put(4, xs.at[step, 0], xr.at[step, 0], g_up, si)
        put(5, xs.at[step, 1], xr.at[step, 1], g_dn, si)
        count = 6 if step == 0 else 5
        put(6, zs.at[step, 0, 0:count], zr.at[step, 0, 0:count], gi, s_up)
        put(7, zs.at[step, 1, 0:count], zr.at[step, 1, 0:count], gi, s_dn)
        return made

    def heat_halo():
        pairs = (
            (xh_s.at[0], xh_r.at[0], g_up, si),
            (xh_s.at[1], xh_r.at[1], g_dn, si),
            (zs.at[1, 0, 5], zr.at[1, 0, 5], gi, s_up),
            (zs.at[1, 1, 5], zr.at[1, 1, 5], gi, s_dn),
        )
        return [
            pltpu.make_async_remote_copy(
                src_ref=src,
                dst_ref=dst,
                send_sem=heat_send.at[n],
                recv_sem=heat_recv.at[n],
                device_id=(a, b),
                device_id_type=MESH,
            )
            for n, (src, dst, a, b) in enumerate(pairs)
        ]

    edge8 = iota((8, CY), 0)

    def stream(step, arrived, which=range(26)):
        for i in which:
            ex, ey, ez = EVERY[i]
            for z in range(2):
                edge = None
                inside = ez == 0 or z == (1 if ez == 1 else 0)
                if arrived == (inside and ex == 0):
                    continue
                if ez == 0 or (ez == 1 and z == 1) or (ez == -1 and z == 0):
                    source = z - ez
                    piece = post[i, source]
                    if ex != 0:
                        way = 0 if ex == 1 else 1
                        if step == 1 and i >= 19:
                            edge = xh_r[way, source : source + 1, :]
                        else:
                            r = (X_UP if ex == 1 else X_DOWN).index(i) * 2 + source
                            edge = xr[step, way, r : r + 1, :]
                else:
                    if ez == 1:
                        piece = zr[step, 0, Z_UP.index(i)]
                    else:
                        piece = zr[step, 1, Z_DOWN.index(i)]
                    if ex == 1:
                        edge = er[step, EDGES.index(i), 7:8, :]
                    if ex == -1:
                        edge = er[step, EDGES.index(i), 0:1, :]
                if ex == 1:
                    piece = jnp.where(edge8 == 0, edge, pltpu.roll(piece, 1, 0))
                if ex == -1:
                    piece = jnp.where(edge8 == 7, edge, pltpu.roll(piece, 7, 0))
                if ey == 1:
                    piece = pltpu.roll(piece, 1, 1)
                if ey == -1:
                    piece = pltpu.roll(piece, CY - 1, 1)
                cur[i, z] = piece

    collide(0, "all")
    pl.semaphore_wait(barrier, 8)
    made = halo(0)
    for c in made:
        c.start()
    tell(0)
    stream(0, False)
    hear(0)
    tell(1)
    row_tables()
    hear(1)
    tell(2)
    slot_tables()
    hear(2)
    tell(3)
    fetch.wait()
    coupling_tables()
    for c in made:
        c.wait_recv()
    stream(0, True)
    collide(1, "heat")
    warm = heat_halo()
    for c in warm:
        c.start()
    collide(1, "flow")
    made = halo(1)
    for c in made:
        c.start()
    stream(1, False, range(19, 26))
    stream(1, False, range(19))
    code_tables()
    x0 = start_ref[0]
    fixed = source_ref[0] + off_diagonal(x0)
    diag = diag_ref[0]
    for c in warm:
        c.wait_recv()
    stream(1, True, range(19, 26))

    hot_rows = []
    for z in range(2):
        hot = functools.reduce(jnp.add, [cur[19 + i, z] for i in range(7)])
        temp_out[z] = hot
        hot_rows.append(hot)

    table = jnp.concatenate(
        [hot_rows[z][:, c * 128 : (c + 1) * 128] for c in range(3) for z in range(2)], axis=0
    )
    picked = dot(
        jnp.concatenate(parts3(table), axis=0).astype(BF16), lo_vox[...], ((1,), (0,))
    )
    picked = picked[0:48] + picked[48:96] + picked[96:144]
    seen = jnp.sum(jnp.where(iota((48, 512), 0) == vox_row, picked, 0.0), axis=0, keepdims=True)
    coeff = coeff_ref[...]
    flux = coeff * seen
    placed = place[0:16, :]
    laid = []
    for pair in zip(parts3(flux), parts3(coeff)):
        laid.append(placed * pair[0])
        laid.append(placed * pair[1])
    laid.append(jnp.zeros((32, 512), F32))
    laid = jnp.concatenate(laid, axis=0).astype(BF16)
    sent = dot(dhot[...], laid, ((1,), (1,)))
    sent = sent + pltpu.roll(sent, 96, 1) + pltpu.roll(sent, 64, 1)
    laid_out[...] = sent.reshape(64, 1, 128)

    half = subs // 4

    def landing(source):
        return landed.at[(source % 8) * groups + source // 8]

    def row_copy(src, source, to):
        return pltpu.make_async_remote_copy(
            src_ref=src,
            dst_ref=landing(source),
            send_sem=strip_send.at[0],
            recv_sem=strip_recv.at[0],
            device_id=(gi, to),
            device_id_type=MESH,
        )

    for e in range(1, half + 1):
        block_out[0, e - 1] = laid_out[lax.rem(si + half + e, subs)]
        block_out[1, e - 1] = laid_out[lax.rem(si + subs - half - e, subs)]

    def block_copy(way):
        to = lax.rem(si + (half if way == 0 else subs - half), subs)
        return pltpu.make_async_remote_copy(
            src_ref=block_out.at[way],
            dst_ref=block_in.at[way],
            send_sem=block_send.at[way],
            recv_sem=block_recv.at[way],
            device_id=(gi, to),
            device_id_type=MESH,
        )

    hear(3)
    block_copy(0).start()
    block_copy(1).start()

    def near(i, carry):
        d = (half - i // 2) * (1 - 2 * (i % 2))
        to = lax.rem(si + subs + d, subs)
        row_copy(laid_out.at[to], si, to).start()
        return carry

    lax.fori_loop(0, 2 * half, near, 0)
    landed[j * groups + g] = laid_out[si]

    for c in made:
        c.wait_recv()
    stream(1, True, range(19))
    for z in range(2):
        for d in range(3):
            pos = [cur[i, z] for i in range(19) if FLOW[i][d] == 1]
            neg = [cur[i, z] for i in range(19) if FLOW[i][d] == -1]
            motion_out[d, z] = functools.reduce(jnp.add, pos) - functools.reduce(jnp.add, neg)

    early = si // (subs // 2)
    for way in (early, 1 - early):
        pltpu.make_async_copy(block_out.at[way], block_in.at[way], block_recv.at[way]).wait()
        sign = 1 - 2 * way
        source = lax.rem(si + subs - sign * half, subs)

        def forward(e, way=way, sign=sign, source=source):
            to = lax.rem(si + subs + sign * e, subs)
            row_copy(block_in.at[way, e - 1], source, to).start()

        @pl.when(way == 0)
        def _(forward=forward):
            forward(half)

        def forward_all(i, carry, forward=forward):
            forward(half - 1 - i)
            return carry

        lax.fori_loop(0, half - 1, forward_all, 0)

    def back_copy(i):
        d = subs // 2 + (1 - 2 * (i % 2)) * ((i + 1) // 2)
        to = lax.rem(si + d, subs)
        return pltpu.make_async_remote_copy(
            src_ref=returned.at[(to % 8) * groups + to // 8],
            dst_ref=received.at[si],
            send_sem=strip_send.at[1],
            recv_sem=strip_recv.at[1],
            device_id=(gi, to),
            device_id_type=MESH,
        )

    def back_go(i, carry):
        back_copy(i).start()
        return carry

    def strip_all(way, sem):
        src, dst = (laid_out, landed) if way == 0 else (returned, received)
        rest = pl.ds(0, subs - 1)
        return pltpu.make_async_copy(src.at[rest], dst.at[rest], sem.at[way])

    strip_all(0, strip_recv).wait()

    got = landed[...].reshape(64, 128)
    in_flux = jnp.where(lane < 32, got, 0.0)
    p0, p1, p2 = parts3(in_flux)
    coded = (p0 + pltpu.roll(p1, 32, 1) + pltpu.roll(p2, 64, 1)).astype(BF16)
    values = dot(coded, ecode[...], ((1,), (0,)))
    values = jnp.concatenate([values[:, k * 128 : (k + 1) * 128] for k in range(16)], axis=0)
    values = (values * mask[...]).astype(BF16)
    summed = dot(lohot_t[...], values, ((1,), (0,))).T
    add_source = summed[0:8] + summed[32:40] + summed[64:72]
    add_diag = summed[8:16] + summed[40:48] + summed[72:80]

    diag = diag + add_diag
    r0 = fixed + add_source - diag * x0
    w1 = (diag - SHIFT) * r0 - off_diagonal(r0)
    w2 = (diag - SHIFT) * w1 - off_diagonal(w1)
    sums = [total(r0 * r0), total(r0 * w1), total(w1 * w1), total(w1 * w2)]

    held = jnp.concatenate([x0, r0, w1, jnp.zeros((8, 128), F32)], axis=0)
    held = jnp.concatenate(list(parts3(held)) + [jnp.zeros((32, 128), F32)], axis=0).astype(BF16)
    found = dot(lohot[...], held, ((1,), (1,)))
    found = (found * mask[...]).astype(BF16)
    found = jnp.concatenate([found[k * 64 : (k + 1) * 64, :] for k in range(16)], axis=1)
    found = dot(found, fcode[...], ((1,), (0,)))
    for n in range(4):
        found = jnp.where(lane == 48 + n, sums[n], found)
    returned[...] = found.reshape(64, 1, 128)
    lax.fori_loop(0, subs - 1, back_go, 0)
    received[si] = returned[j * groups + g]
    strip_all(1, strip_recv).wait()
    back = received[...].reshape(64, 128)
    tot[...] = jnp.sum(back, axis=0, keepdims=True)

    def band_copy(i):
        return pltpu.make_async_remote_copy(
            src_ref=tot,
            dst_ref=rtot.at[gi],
            send_sem=band_send,
            recv_sem=band_recv,
            device_id=(lax.rem(gi + i, bands), si),
            device_id_type=MESH,
        )

    def band_go(i, carry):
        band_copy(i).start()
        return carry

    lax.fori_loop(1, bands, band_go, 0)

    def band_all(sem):
        rest = pl.ds(0, bands - 1)
        return pltpu.make_async_copy(laid_out.at[rest], rtot.at[rest], sem)

    back = jnp.where(lane < 48, back, 0.0)
    rows = functools.reduce(
        jnp.add, [dot(p.astype(BF16), dhot[...], ((0,), (0,))) for p in parts3(back)]
    )
    rows = rows * place[...]
    row_x0 = jnp.sum(rows[0:16], axis=0, keepdims=True)
    row_r0 = jnp.sum(rows[16:32], axis=0, keepdims=True)
    row_w1 = jnp.sum(rows[32:48], axis=0, keepdims=True)

    rtot[gi] = tot[...]

    band_all(band_recv).wait()
    lane1 = iota((1, 128), 1)
    whole = functools.reduce(jnp.add, [rtot[n] for n in range(bands)])

    def lane_value(n):
        return jnp.sum(jnp.where(lane1 == 48 + n, whole, 0.0), axis=1, keepdims=True)

    n0, n1, n2, n3 = [lane_value(n) for n in range(4)]
    delta = n1 / n0
    second = n2 / n0
    spread_of = second - delta * delta
    theta = SHIFT + delta
    third = n3 / n0 - 3.0 * delta * second + 2.0 * delta * delta * delta
    wide_enough = spread_of > 1e-7 * theta * theta
    spread_of = jnp.maximum(spread_of, 0.0)
    skew = jnp.where(wide_enough, third / jnp.where(wide_enough, spread_of, 1.0), 0.0)
    step0 = 1.0 / theta
    growth = spread_of / (theta * theta)
    step1 = 1.0 / (theta + skew - spread_of / theta)
    by_r0 = step0 + step1 * (growth + step0 * delta)
    by_w1 = -step1 * step0
    solid_out[0] = x0 + by_r0 * r0 + by_w1 * w1
    rows_out[...] = row_x0 + by_r0 * row_r0 + by_w1 * row_w1

    for step in range(STEPS):
        for c in halo(step):
            c.wait_send()
    for c in warm:
        c.wait_send()
    block_copy(0).wait_send()
    block_copy(1).wait_send()
    strip_all(0, strip_send).wait()
    strip_all(1, strip_send).wait()
    band_all(band_send).wait()


def publish(*refs):
    for source, target in zip(refs[:4], refs[4:]):
        target[...] = source[...]


def solution(mesh):
    bands = mesh.shape["grp"]
    subs = mesh.shape["sub"]
    groups = subs // 8

    def body(
        populations,
        heat_pops,
        solid_frac,
        coupled_grid_point,
        dest_index,
        heat_coeff,
        slot_node,
        node_diag,
        coupling,
        block_pattern,
        heat_source,
        solid_start,
    ):
        vmem = pl.BlockSpec(memory_space=pltpu.VMEM)
        smem = pl.BlockSpec(memory_space=pltpu.SMEM)
        dma = pltpu.SemaphoreType.DMA
        shapes = (
                jax.ShapeDtypeStruct((2, 8, CY), F32),
                jax.ShapeDtypeStruct((3, 2, 8, CY), F32),
                jax.ShapeDtypeStruct((1, 8, 128), F32),
                jax.ShapeDtypeStruct((1, 512), F32),
            )
        made = pl.pallas_call(
            functools.partial(kernel, groups, bands),
            out_shape=tuple(pltpu.VMEM(v.shape, v.dtype) for v in shapes),
            in_specs=[vmem] * 8 + [pl.BlockSpec(memory_space=pl.ANY), smem] + [vmem] * 2,
            out_specs=(vmem,) * 4,
            scratch_shapes=[
                pltpu.VMEM((26, 2, 8, CY), F32),
                pltpu.VMEM((26, 2, 8, CY), F32),
                pltpu.VMEM((STEPS, 2, 6, 8, CY), F32),
                pltpu.VMEM((STEPS, 2, 6, 8, CY), F32),
                pltpu.VMEM((STEPS, 2, 16, CY), F32),
                pltpu.VMEM((STEPS, 2, 16, CY), F32),
                pltpu.VMEM((STEPS, 4, 8, CY), F32),
                pltpu.VMEM((1024, 256), BF16),
                pltpu.VMEM((1024, 256), BF16),
                pltpu.VMEM((1024, 128), BF16),
                pltpu.VMEM((128, 1024), BF16),
                *[pltpu.VMEM((2, 8, CY), F32)] * 2,
                pltpu.VMEM((4, 2, 8, CY), F32),
                pltpu.VMEM((8, 128, 128), F32),
                pltpu.VMEM((1024, 128), F32),
                pltpu.VMEM((128, 512), F32),
                pltpu.VMEM((64, 512), BF16),
                pltpu.VMEM((128, 512), BF16),
                pltpu.VMEM((128, 2048), BF16),
                pltpu.VMEM((2048, 128), BF16),
                pltpu.VMEM((64, 1, 128), F32),
                *[pltpu.VMEM((2, 16, 1, 128), F32)] * 2,
                *[pltpu.VMEM((64, 1, 128), F32)] * 3,
                pltpu.VMEM((1, 128), F32),
                pltpu.VMEM((bands, 1, 128), F32),
                dma((STEPS, 8)),
                dma((STEPS, 8)),
                dma((2,)),
                dma((2,)),
                dma,
                dma,
                dma((2,)),
                dma((2,)),
                dma((4,)),
                dma((4,)),
                dma,
                pltpu.SemaphoreType.REGULAR((4,)),
            ],
            compiler_params=pltpu.CompilerParams(collective_id=0, has_side_effects=True),
            name="coupled_step",
        )(
            populations,
            heat_pops,
            solid_frac,
            coupled_grid_point,
            dest_index[..., 0],
            heat_coeff,
            slot_node.reshape(8, 128),
            node_diag,
            coupling,
            block_pattern,
            heat_source,
            solid_start,
        )
        return pl.pallas_call(
            publish,
            out_shape=shapes,
            in_specs=[vmem] * 4,
            out_specs=(vmem,) * 4,
            name="publish",
        )(*[pltpu.with_memory_space_constraint(v, pltpu.VMEM) for v in made])

    band = P("grp", "sub")
    block = P("grp", "sub", None)
    return jax.shard_map(
        body,
        mesh=mesh,
        in_specs=(
            P(None, "sub", "grp", None),
            P(None, "sub", "grp", None),
            P("sub", "grp", None),
            band,
            block,
            band,
            band,
            block,
            P("grp", "sub", None, None),
            band,
            block,
            block,
        ),
        out_specs=(P("sub", "grp", None), P(None, "sub", "grp", None), block, band),
        check_vma=False,
    )
```

```python
import functools

import jax
import jax.numpy as jnp
import numpy as np
from jax import lax
from jax.experimental import pallas as pl
from jax.experimental.pallas import tpu as pltpu
from jax.sharding import PartitionSpec as P

MESH = pl.DeviceIdType.MESH
F32 = jnp.float32
BF16 = jnp.bfloat16
I32 = jnp.int32

STEPS = 2
CY = 384
CAP = 16
SHIFT = 4.0

FLOW = [
    (0, 0, 0),
    (1, 0, 0),
    (-1, 0, 0),
    (0, 1, 0),
    (0, -1, 0),
    (0, 0, 1),
    (0, 0, -1),
    (1, 1, 0),
    (-1, -1, 0),
    (1, -1, 0),
    (-1, 1, 0),
    (1, 0, 1),
    (-1, 0, -1),
    (1, 0, -1),
    (-1, 0, 1),
    (0, 1, 1),
    (0, -1, -1),
    (0, 1, -1),
    (0, -1, 1),
]
EVERY = FLOW + FLOW[:7]
WEIGHT = [1.0 / 3.0] + [1.0 / 18.0] * 6 + [1.0 / 36.0] * 12
HEAT_WEIGHT = [0.25] + [0.125] * 6
TAU_FLOW = 0.8
TAU_HEAT = 0.7

X_UP = [i for i, e in enumerate(EVERY) if e[0] == 1]
X_DOWN = [i for i, e in enumerate(EVERY) if e[0] == -1]
Z_UP = [i for i, e in enumerate(EVERY) if e[2] == 1]
Z_DOWN = [i for i, e in enumerate(EVERY) if e[2] == -1]
EDGES = [
    next(i for i, e in enumerate(FLOW) if e == (1, 0, 1)),
    next(i for i, e in enumerate(FLOW) if e == (-1, 0, 1)),
    next(i for i, e in enumerate(FLOW) if e == (1, 0, -1)),
    next(i for i, e in enumerate(FLOW) if e == (-1, 0, -1)),
]


def dot(a, b, dims):
    return lax.dot_general(a, b, (dims, ((), ())), preferred_element_type=F32)


def parts3(v):
    a = v.astype(BF16).astype(F32)
    rest = v - a
    b = rest.astype(BF16).astype(F32)
    return a, b, rest - b


def iota(shape, dim):
    return lax.broadcasted_iota(I32, shape, dim)


def total(v):
    return jnp.sum(jnp.sum(v, axis=1, keepdims=True), axis=0, keepdims=True)


def kernel(
    groups,
    bands,
    pops_ref,
    heat_ref,
    solid_ref,
    voxel_ref,
    dest_ref,
    coeff_ref,
    slot_ref,
    diag_ref,
    coup_ref,
    pat_ref,
    source_ref,
    start_ref,
    temp_out,
    motion_out,
    solid_out,
    rows_out,
    cur,
    post,
    zs,
    zr,
    xs,
    xr,
    er,
    chop,
    cthop,
    lohot,
    lohot_t,
    xh_s,
    xh_r,
    vel,
    coup,
    mask,
    place,
    dhot,
    lo_vox,
    ecode,
    fcode,
    laid_out,
    block_out,
    block_in,
    landed,
    returned,
    received,
    mom_s,
    mom_r,
    tot,
    rtot,
    halo_send,
    halo_recv,
    strip_send,
    strip_recv,
    band_send,
    band_recv,
    block_send,
    block_recv,
    heat_send,
    heat_recv,
    coup_sem,
    mom_send,
    mom_recv,
    ready,
):
    subs = groups * 8
    gi = lax.axis_index("grp")
    si = lax.axis_index("sub")
    g = si // 8
    j = si % 8
    g_up = lax.rem(gi + 1, bands)
    g_dn = lax.rem(gi + bands - 1, bands)
    s_up = lax.rem(si + 1, subs)
    s_dn = lax.rem(si + subs - 1, subs)

    fetch = pltpu.make_async_copy(coup_ref.at[0], coup, coup_sem)
    fetch.start()
    barrier = pltpu.get_barrier_semaphore()

    def greet(a, b):
        pl.semaphore_signal(barrier, inc=1, device_id=(a, b), device_id_type=MESH)

    for a, b in (
        (gi, s_up),
        (gi, s_dn),
        (g_up, si),
        (g_dn, si),
        (g_up, s_up),
        (g_up, s_dn),
        (g_dn, s_up),
        (g_dn, s_dn),
    ):
        greet(a, b)

    def tell(n):
        d = 1 << n
        to = [(gi, lax.rem(si + d, subs)), (gi, lax.rem(si + subs - d, subs))]
        if 2 * d < bands:
            to += [(lax.rem(gi + d, bands), si), (lax.rem(gi + bands - d, bands), si)]
        for a, b in to:
            pl.semaphore_signal(ready.at[n], inc=1, device_id=(a, b), device_id_type=MESH)

    def hear(n):
        pl.semaphore_wait(ready.at[n], 4 if 2 << n < bands else 2)

    sub8 = iota((8, 128), 0)
    lane = iota((64, 128), 1)
    xs[:, :, 8:16] = jnp.zeros((STEPS, 2, 8, CY), F32)
    xh_s[...] = jnp.zeros((2, 8, CY), F32)

    def slot_tables():
        a_of = iota((128, 2048), 0)
        spread = jnp.where(a_of == iota((128, 2048), 1) // 128, 1.0, 0.0).astype(BF16)
        slots = slot_ref[...]
        rolled = [slots] + [pltpu.roll(slots, 128 - 16 * a, 1) for a in range(1, 8)]
        slots = jnp.concatenate(rolled, axis=0)
        slot_hi = (slots // 128).astype(F32).astype(BF16)
        slot_lo = (slots % 128).astype(F32).astype(BF16)
        hi_all = dot(slot_hi, spread, ((1,), (0,)))
        lo_all = dot(slot_lo, spread, ((1,), (0,)))
        for k in range(16):
            cols = slice(k * 128, (k + 1) * 128)
            rows = pl.ds(k * 64, 64)
            lohot[rows, :] = jnp.where(lo_all[:, cols] == lane.astype(F32), 1.0, 0.0).astype(BF16)
            lohot_t[:, k * 64 : (k + 1) * 64] = (
                jnp.where(lo_all[:, cols] == lane.astype(F32), 1.0, 0.0).T.astype(BF16)
            )
            mask[rows, :] = jnp.where(hi_all[:, cols] == (lane % 8).astype(F32), 1.0, 0.0)

    def row_tables():
        dest = dest_ref[...]
        dest_hot = jnp.where(iota((64, 512), 0) == dest, 1.0, 0.0)
        dhot[...] = dest_hot.astype(BF16)
        ahead = jnp.where(iota((512, 512), 0) < iota((512, 512), 1), 1.0, 0.0).astype(BF16)
        counts = dot(dest_hot.astype(BF16), ahead, ((1,), (0,)))
        at = jnp.sum(dest_hot * counts, axis=0, keepdims=True)
        place[...] = jnp.where((iota((128, 512), 0) % 16).astype(F32) == at, 1.0, 0.0)

    def code_tables():
        wide = 16 * 128
        a_of = iota((128, wide), 0)
        c_of = iota((128, wide), 1)
        k_of = c_of // 128
        lane_of = c_of % 128
        p_of = lane_of // 32
        t_of = (lane_of // 8) % 4
        ecode[...] = jnp.where(
            (a_of == p_of * 32 + t_of * 16 + k_of) & (p_of < 3) & (t_of < 2), 1.0, 0.0
        ).astype(BF16)
        c_of = iota((wide, 128), 0)
        l_of = iota((wide, 128), 1)
        k_of = c_of // 128
        lane_of = c_of % 128
        p_of = lane_of // 32
        t_of = (lane_of // 8) % 4
        fcode[...] = jnp.where((l_of == t_of * 16 + k_of) & (p_of < 3) & (t_of < 3), 1.0, 0.0).astype(
            BF16
        )

    def coupling_tables():
        for b in range(8):
            block = coup[b]
            high = block.astype(BF16).astype(F32)
            low = block - high
            rows = pl.ds(b * 128, 128)
            chop[rows, 0:128] = high.astype(BF16)
            chop[rows, 128:256] = low.astype(BF16)
            cthop[rows, 0:128] = high.T.astype(BF16)
            cthop[rows, 128:256] = low.T.astype(BF16)

    voxel = voxel_ref[...]
    lo_vox[...] = jnp.where(iota((128, 512), 0) == voxel % 128, 1.0, 0.0).astype(BF16)
    over = voxel // 128
    layer_x = over // 3
    vox_row = (over - layer_x * 3) * 16 + layer_x

    pat = [pat_ref[0, b] for b in range(8)]
    pat_col = jnp.zeros((8, 128), I32)
    for b in range(8):
        pat_col = jnp.where(sub8 == b, pat[b], pat_col)

    def block_dot(v, table):
        high = v.astype(BF16).astype(F32)
        low = v - high
        left = jnp.concatenate([jnp.where(sub8 == b, high, 0.0) for b in range(8)], axis=1)
        right = jnp.concatenate([jnp.where(sub8 == b, low, 0.0) for b in range(8)], axis=1)
        both = jnp.concatenate([left, right], axis=0).astype(BF16)
        out = dot(both, table[...], ((1,), (0,)))
        return out[0:8, 0:128] + out[8:16, 0:128] + out[0:8, 128:256]

    def by_partner(v):
        partner = jnp.zeros((8, 128), F32)
        for k in range(8):
            partner = jnp.where(pat_col == k, v[k : k + 1, :], partner)
        return block_dot(partner, cthop)

    def off_diagonal(v):
        forward = by_partner(v)
        terms = block_dot(v, chop)
        backward = jnp.zeros((8, 128), F32)
        for b in range(8):
            backward = backward + jnp.where(sub8 == pat[b], terms[b : b + 1, :], 0.0)
        return forward + backward

    def collide(step, part):
        for z in range(2):
            for c in range(3):
                cols = slice(c * 128, (c + 1) * 128)
                if step == 0:
                    f = [pops_ref[i, z, :, cols] for i in range(19)]
                    heat = [heat_ref[i, z, :, cols] for i in range(7)]
                else:
                    f = [cur[i, z, :, cols] for i in range(19)]
                    heat = [cur[19 + i, z, :, cols] for i in range(7)]
                if part == "flow":
                    rho = vel[3, z, :, cols]
                    u = [vel[d, z, :, cols] for d in range(3)]
                else:
                    rho = functools.reduce(jnp.add, f)
                    m = []
                    for d in range(3):
                        pos = [f[i] for i in range(19) if FLOW[i][d] == 1]
                        neg = [f[i] for i in range(19) if FLOW[i][d] == -1]
                        m.append(functools.reduce(jnp.add, pos) - functools.reduce(jnp.add, neg))
                    u = [v / rho for v in m]
                if part == "heat":
                    vel[3, z, :, cols] = rho
                    for d in range(3):
                        vel[d, z, :, cols] = u[d]
                out = [None] * 26
                if part != "heat":
                    solid = solid_ref[z, :, cols]
                    flat = 1.0 - 1.5 * (u[0] * u[0] + u[1] * u[1] + u[2] * u[2])
                    fluid = 1.0 - solid
                    keep = fluid * (1.0 - 1.0 / TAU_FLOW)
                    gain = fluid * rho * (1.0 / TAU_FLOW)
                    out[0] = (keep + solid) * f[0] + gain * WEIGHT[0] * flat
                    for i in range(1, 19, 2):
                        along = None
                        for d in range(3):
                            if FLOW[i][d] == 1:
                                along = u[d] if along is None else along + u[d]
                            elif FLOW[i][d] == -1:
                                along = -u[d] if along is None else along - u[d]
                        even = flat + 4.5 * along * along
                        odd = 3.0 * along
                        scale = gain * WEIGHT[i]
                        out[i] = keep * f[i] + solid * f[i + 1] + scale * (even + odd)
                        out[i + 1] = keep * f[i + 1] + solid * f[i] + scale * (even - odd)
                if part != "flow":
                    hot = functools.reduce(jnp.add, heat)
                    for i in range(7):
                        share = hot * (HEAT_WEIGHT[i] / TAU_HEAT)
                        if i > 0:
                            d = [abs(v) for v in FLOW[i]].index(1)
                            sign = FLOW[i][d]
                            share = share * (1.0 + (4.0 * sign) * u[d])
                        out[19 + i] = (1.0 - 1.0 / TAU_HEAT) * heat[i] + share
                for i in range(26):
                    if out[i] is None:
                        continue
                    ex, ez = EVERY[i][0], EVERY[i][2]
                    post[i, z, :, cols] = out[i]
                    if ez == 1 and z == 1:
                        zs[step, 0, Z_UP.index(i), :, cols] = out[i]
                    if ez == -1 and z == 0:
                        zs[step, 1, Z_DOWN.index(i), :, cols] = out[i]
                    if ex == 0:
                        continue
                    way = 0 if ex == 1 else 1
                    row = out[i][7:8, :] if ex == 1 else out[i][0:1, :]
                    if step == 1 and i >= 19:
                        xh_s[way, z : z + 1, cols] = row
                    else:
                        r = (X_UP if ex == 1 else X_DOWN).index(i) * 2 + z
                        xs[step, way, r : r + 1, cols] = row

    def halo(step):
        made = []

        def put(n, src, dst, a, b):
            made.append(
                pltpu.make_async_remote_copy(
                    src_ref=src,
                    dst_ref=dst,
                    send_sem=halo_send.at[step, n],
                    recv_sem=halo_recv.at[step, n],
                    device_id=(a, b),
                    device_id_type=MESH,
                )
            )

        put(0, zs.at[step, 0, Z_UP.index(EDGES[0])], er.at[step, 0], g_up, s_up)
        put(1, zs.at[step, 0, Z_UP.index(EDGES[1])], er.at[step, 1], g_dn, s_up)
        put(2, zs.at[step, 1, Z_DOWN.index(EDGES[2])], er.at[step, 2], g_up, s_dn)
        put(3, zs.at[step, 1, Z_DOWN.index(EDGES[3])], er.at[step, 3], g_dn, s_dn)
        put(4, xs.at[step, 0], xr.at[step, 0], g_up, si)
        put(5, xs.at[step, 1], xr.at[step, 1], g_dn, si)
        count = 6 if step == 0 else 5
        put(6, zs.at[step, 0, 0:count], zr.at[step, 0, 0:count], gi, s_up)
        put(7, zs.at[step, 1, 0:count], zr.at[step, 1, 0:count], gi, s_dn)
        return made

    def heat_halo():
        pairs = (
            (xh_s.at[0], xh_r.at[0], g_up, si),
            (xh_s.at[1], xh_r.at[1], g_dn, si),
            (zs.at[1, 0, 5], zr.at[1, 0, 5], gi, s_up),
            (zs.at[1, 1, 5], zr.at[1, 1, 5], gi, s_dn),
        )
        return [
            pltpu.make_async_remote_copy(
                src_ref=src,
                dst_ref=dst,
                send_sem=heat_send.at[n],
                recv_sem=heat_recv.at[n],
                device_id=(a, b),
                device_id_type=MESH,
            )
            for n, (src, dst, a, b) in enumerate(pairs)
        ]

    edge8 = iota((8, CY), 0)

    def stream(step, arrived, which=range(26)):
        for i in which:
            ex, ey, ez = EVERY[i]
            for z in range(2):
                edge = None
                inside = ez == 0 or z == (1 if ez == 1 else 0)
                if arrived == (inside and ex == 0):
                    continue
                if ez == 0 or (ez == 1 and z == 1) or (ez == -1 and z == 0):
                    source = z - ez
                    piece = post[i, source]
                    if ex != 0:
                        way = 0 if ex == 1 else 1
                        if step == 1 and i >= 19:
                            edge = xh_r[way, source : source + 1, :]
                        else:
                            r = (X_UP if ex == 1 else X_DOWN).index(i) * 2 + source
                            edge = xr[step, way, r : r + 1, :]
                else:
                    if ez == 1:
                        piece = zr[step, 0, Z_UP.index(i)]
                    else:
                        piece = zr[step, 1, Z_DOWN.index(i)]
                    if ex == 1:
                        edge = er[step, EDGES.index(i), 7:8, :]
                    if ex == -1:
                        edge = er[step, EDGES.index(i), 0:1, :]
                if ex == 1:
                    piece = jnp.where(edge8 == 0, edge, pltpu.roll(piece, 1, 0))
                if ex == -1:
                    piece = jnp.where(edge8 == 7, edge, pltpu.roll(piece, 7, 0))
                if ey == 1:
                    piece = pltpu.roll(piece, 1, 1)
                if ey == -1:
                    piece = pltpu.roll(piece, CY - 1, 1)
                cur[i, z] = piece

    collide(0, "all")
    pl.semaphore_wait(barrier, 8)
    made = halo(0)
    for c in made:
        c.start()
    tell(0)
    stream(0, False)
    hear(0)
    tell(1)
    row_tables()
    hear(1)
    tell(2)
    slot_tables()
    hear(2)
    tell(3)
    fetch.wait()
    coupling_tables()
    for c in made:
        c.wait_recv()
    stream(0, True)
    collide(1, "heat")
    warm = heat_halo()
    for c in warm:
        c.start()
    collide(1, "flow")
    made = halo(1)
    for c in made:
        c.start()
    stream(1, False, range(19, 26))
    stream(1, False, range(19))
    code_tables()
    x0 = start_ref[0]
    fixed = source_ref[0] + off_diagonal(x0)
    diag = diag_ref[0]
    for c in warm:
        c.wait_recv()
    stream(1, True, range(19, 26))

    hot_rows = []
    for z in range(2):
        hot = functools.reduce(jnp.add, [cur[19 + i, z] for i in range(7)])
        temp_out[z] = hot
        hot_rows.append(hot)

    table = jnp.concatenate(
        [hot_rows[z][:, c * 128 : (c + 1) * 128] for c in range(3) for z in range(2)], axis=0
    )
    picked = dot(
        jnp.concatenate(parts3(table), axis=0).astype(BF16), lo_vox[...], ((1,), (0,))
    )
    picked = picked[0:48] + picked[48:96] + picked[96:144]
    seen = jnp.sum(jnp.where(iota((48, 512), 0) == vox_row, picked, 0.0), axis=0, keepdims=True)
    coeff = coeff_ref[...]
    flux = coeff * seen
    placed = place[0:16, :]
    laid = []
    for pair in zip(parts3(flux), parts3(coeff)):
        laid.append(placed * pair[0])
        laid.append(placed * pair[1])
    laid.append(jnp.zeros((32, 512), F32))
    laid = jnp.concatenate(laid, axis=0).astype(BF16)
    sent = dot(dhot[...], laid, ((1,), (1,)))
    sent = sent + pltpu.roll(sent, 96, 1) + pltpu.roll(sent, 64, 1)
    laid_out[...] = sent.reshape(64, 1, 128)

    half = subs // 4

    def landing(source):
        return landed.at[(source % 8) * groups + source // 8]

    def row_copy(src, source, to):
        return pltpu.make_async_remote_copy(
            src_ref=src,
            dst_ref=landing(source),
            send_sem=strip_send.at[0],
            recv_sem=strip_recv.at[0],
            device_id=(gi, to),
            device_id_type=MESH,
        )

    for e in range(1, half + 1):
        block_out[0, e - 1] = laid_out[lax.rem(si + half + e, subs)]
        block_out[1, e - 1] = laid_out[lax.rem(si + subs - half - e, subs)]

    def block_copy(way):
        to = lax.rem(si + (half if way == 0 else subs - half), subs)
        return pltpu.make_async_remote_copy(
            src_ref=block_out.at[way],
            dst_ref=block_in.at[way],
            send_sem=block_send.at[way],
            recv_sem=block_recv.at[way],
            device_id=(gi, to),
            device_id_type=MESH,
        )

    hear(3)
    block_copy(0).start()
    block_copy(1).start()

    def near(i, carry):
        d = (half - i // 2) * (1 - 2 * (i % 2))
        to = lax.rem(si + subs + d, subs)
        row_copy(laid_out.at[to], si, to).start()
        return carry

    lax.fori_loop(0, 2 * half, near, 0)
    landed[j * groups + g] = laid_out[si]

    for c in made:
        c.wait_recv()
    stream(1, True, range(19))
    for z in range(2):
        for d in range(3):
            pos = [cur[i, z] for i in range(19) if FLOW[i][d] == 1]
            neg = [cur[i, z] for i in range(19) if FLOW[i][d] == -1]
            motion_out[d, z] = functools.reduce(jnp.add, pos) - functools.reduce(jnp.add, neg)

    early = si // (subs // 2)
    for way in (early, 1 - early):
        pltpu.make_async_copy(block_out.at[way], block_in.at[way], block_recv.at[way]).wait()
        sign = 1 - 2 * way
        source = lax.rem(si + subs - sign * half, subs)

        def forward(e, way=way, sign=sign, source=source):
            to = lax.rem(si + subs + sign * e, subs)
            row_copy(block_in.at[way, e - 1], source, to).start()

        @pl.when(way == 0)
        def _(forward=forward):
            forward(half)

        def forward_all(i, carry, forward=forward):
            forward(half - 1 - i)
            return carry

        lax.fori_loop(0, half - 1, forward_all, 0)

    def back_copy(i):
        to = far_first(i)
        return pltpu.make_async_remote_copy(
            src_ref=returned.at[(to % 8) * groups + to // 8],
            dst_ref=received.at[si],
            send_sem=strip_send.at[1],
            recv_sem=strip_recv.at[1],
            device_id=(gi, to),
            device_id_type=MESH,
        )

    def back_go(i, carry):
        back_copy(i).start()
        return carry

    def strip_all(way, sem):
        src, dst = (laid_out, landed) if way == 0 else (returned, received)
        rest = pl.ds(0, subs - 1)
        return pltpu.make_async_copy(src.at[rest], dst.at[rest], sem.at[way])

    strip_all(0, strip_recv).wait()

    got = landed[...].reshape(64, 128)
    in_flux = jnp.where(lane < 32, got, 0.0)
    p0, p1, p2 = parts3(in_flux)
    coded = (p0 + pltpu.roll(p1, 32, 1) + pltpu.roll(p2, 64, 1)).astype(BF16)
    values = dot(coded, ecode[...], ((1,), (0,)))
    values = jnp.concatenate([values[:, k * 128 : (k + 1) * 128] for k in range(16)], axis=0)
    values = (values * mask[...]).astype(BF16)
    summed = dot(lohot_t[...], values, ((1,), (0,))).T
    add_source = summed[0:8] + summed[32:40] + summed[64:72]
    add_diag = summed[8:16] + summed[40:48] + summed[72:80]

    diag = diag + add_diag
    r0 = fixed + add_source - diag * x0
    w1 = (diag - SHIFT) * r0 - off_diagonal(r0)
    last = (diag - SHIFT) * w1 - 2.0 * by_partner(w1)
    sums = [total(r0 * r0), total(r0 * w1), total(w1 * w1), total(w1 * last)]

    lane1 = iota((1, 128), 1)
    line = jnp.zeros((1, 128), F32)
    for n in range(4):
        line = jnp.where(lane1 == 48 + n, sums[n], line)
    mom_s[...] = line

    def far_first(i):
        d = subs // 2 + (1 - 2 * (i % 2)) * ((i + 1) // 2)
        return lax.rem(si + d, subs)

    def mom_go(i, carry):
        pltpu.make_async_remote_copy(
            src_ref=mom_s,
            dst_ref=mom_r.at[si],
            send_sem=mom_send,
            recv_sem=mom_recv,
            device_id=(gi, far_first(i)),
            device_id_type=MESH,
        ).start()
        return carry

    lax.fori_loop(0, subs - 1, mom_go, 0)
    mom_r[si] = line

    def mom_all(sem):
        rest = pl.ds(0, subs - 1)
        return pltpu.make_async_copy(landed.at[rest], mom_r.at[rest], sem)

    held = jnp.concatenate([x0, r0, w1, jnp.zeros((8, 128), F32)], axis=0)
    held = jnp.concatenate(list(parts3(held)) + [jnp.zeros((32, 128), F32)], axis=0).astype(BF16)
    found = dot(lohot[...], held, ((1,), (1,)))
    found = (found * mask[...]).astype(BF16)
    found = jnp.concatenate([found[k * 64 : (k + 1) * 64, :] for k in range(16)], axis=1)
    found = dot(found, fcode[...], ((1,), (0,)))
    returned[...] = found.reshape(64, 1, 128)
    lax.fori_loop(0, subs - 1, back_go, 0)
    received[si] = returned[j * groups + g]
    mom_all(mom_recv).wait()
    tot[...] = jnp.sum(mom_r[...].reshape(64, 128), axis=0, keepdims=True)

    def band_copy(i):
        return pltpu.make_async_remote_copy(
            src_ref=tot,
            dst_ref=rtot.at[gi],
            send_sem=band_send,
            recv_sem=band_recv,
            device_id=(lax.rem(gi + i, bands), si),
            device_id_type=MESH,
        )

    def band_go(i, carry):
        band_copy(i).start()
        return carry

    lax.fori_loop(1, bands, band_go, 0)

    def band_all(sem):
        rest = pl.ds(0, bands - 1)
        return pltpu.make_async_copy(laid_out.at[rest], rtot.at[rest], sem)

    strip_all(1, strip_recv).wait()
    back = received[...].reshape(64, 128)
    rows = functools.reduce(
        jnp.add, [dot(p.astype(BF16), dhot[...], ((0,), (0,))) for p in parts3(back)]
    )
    rows = rows * place[...]
    row_x0 = jnp.sum(rows[0:16], axis=0, keepdims=True)
    row_r0 = jnp.sum(rows[16:32], axis=0, keepdims=True)
    row_w1 = jnp.sum(rows[32:48], axis=0, keepdims=True)

    rtot[gi] = tot[...]

    band_all(band_recv).wait()
    whole = functools.reduce(jnp.add, [rtot[n] for n in range(bands)])

    def lane_value(n):
        return jnp.sum(jnp.where(lane1 == 48 + n, whole, 0.0), axis=1, keepdims=True)

    n0, n1, n2, n3 = [lane_value(n) for n in range(4)]
    delta = n1 / n0
    second = n2 / n0
    spread_of = second - delta * delta
    theta = SHIFT + delta
    third = n3 / n0 - 3.0 * delta * second + 2.0 * delta * delta * delta
    wide_enough = spread_of > 1e-7 * theta * theta
    spread_of = jnp.maximum(spread_of, 0.0)
    skew = jnp.where(wide_enough, third / jnp.where(wide_enough, spread_of, 1.0), 0.0)
    step0 = 1.0 / theta
    growth = spread_of / (theta * theta)
    step1 = 1.0 / (theta + skew - spread_of / theta)
    by_r0 = step0 + step1 * (growth + step0 * delta)
    by_w1 = -step1 * step0
    solid_out[0] = x0 + by_r0 * r0 + by_w1 * w1
    rows_out[...] = row_x0 + by_r0 * row_r0 + by_w1 * row_w1

    for step in range(STEPS):
        for c in halo(step):
            c.wait_send()
    for c in warm:
        c.wait_send()
    block_copy(0).wait_send()
    block_copy(1).wait_send()
    strip_all(0, strip_send).wait()
    strip_all(1, strip_send).wait()
    band_all(band_send).wait()
    mom_all(mom_send).wait()


def publish(*refs):
    for source, target in zip(refs[:4], refs[4:]):
        target[...] = source[...]


def solution(mesh):
    bands = mesh.shape["grp"]
    subs = mesh.shape["sub"]
    groups = subs // 8

    def body(
        populations,
        heat_pops,
        solid_frac,
        coupled_grid_point,
        dest_index,
        heat_coeff,
        slot_node,
        node_diag,
        coupling,
        block_pattern,
        heat_source,
        solid_start,
    ):
        vmem = pl.BlockSpec(memory_space=pltpu.VMEM)
        smem = pl.BlockSpec(memory_space=pltpu.SMEM)
        dma = pltpu.SemaphoreType.DMA
        shapes = (
                jax.ShapeDtypeStruct((2, 8, CY), F32),
                jax.ShapeDtypeStruct((3, 2, 8, CY), F32),
                jax.ShapeDtypeStruct((1, 8, 128), F32),
                jax.ShapeDtypeStruct((1, 512), F32),
            )
        made = pl.pallas_call(
            functools.partial(kernel, groups, bands),
            out_shape=tuple(pltpu.VMEM(v.shape, v.dtype) for v in shapes),
            in_specs=[vmem] * 8 + [pl.BlockSpec(memory_space=pl.ANY), smem] + [vmem] * 2,
            out_specs=(vmem,) * 4,
            scratch_shapes=[
                pltpu.VMEM((26, 2, 8, CY), F32),
                pltpu.VMEM((26, 2, 8, CY), F32),
                pltpu.VMEM((STEPS, 2, 6, 8, CY), F32),
                pltpu.VMEM((STEPS, 2, 6, 8, CY), F32),
                pltpu.VMEM((STEPS, 2, 16, CY), F32),
                pltpu.VMEM((STEPS, 2, 16, CY), F32),
                pltpu.VMEM((STEPS, 4, 8, CY), F32),
                pltpu.VMEM((1024, 256), BF16),
                pltpu.VMEM((1024, 256), BF16),
                pltpu.VMEM((1024, 128), BF16),
                pltpu.VMEM((128, 1024), BF16),
                *[pltpu.VMEM((2, 8, CY), F32)] * 2,
                pltpu.VMEM((4, 2, 8, CY), F32),
                pltpu.VMEM((8, 128, 128), F32),
                pltpu.VMEM((1024, 128), F32),
                pltpu.VMEM((128, 512), F32),
                pltpu.VMEM((64, 512), BF16),
                pltpu.VMEM((128, 512), BF16),
                pltpu.VMEM((128, 2048), BF16),
                pltpu.VMEM((2048, 128), BF16),
                pltpu.VMEM((64, 1, 128), F32),
                *[pltpu.VMEM((2, 16, 1, 128), F32)] * 2,
                *[pltpu.VMEM((64, 1, 128), F32)] * 3,
                pltpu.VMEM((1, 128), F32),
                pltpu.VMEM((64, 1, 128), F32),
                pltpu.VMEM((1, 128), F32),
                pltpu.VMEM((bands, 1, 128), F32),
                dma((STEPS, 8)),
                dma((STEPS, 8)),
                dma((2,)),
                dma((2,)),
                dma,
                dma,
                dma((2,)),
                dma((2,)),
                dma((4,)),
                dma((4,)),
                dma,
                dma,
                dma,
                pltpu.SemaphoreType.REGULAR((4,)),
            ],
            compiler_params=pltpu.CompilerParams(collective_id=0, has_side_effects=True),
            name="coupled_step",
        )(
            populations,
            heat_pops,
            solid_frac,
            coupled_grid_point,
            dest_index[..., 0],
            heat_coeff,
            slot_node.reshape(8, 128),
            node_diag,
            coupling,
            block_pattern,
            heat_source,
            solid_start,
        )
        return pl.pallas_call(
            publish,
            out_shape=shapes,
            in_specs=[vmem] * 4,
            out_specs=(vmem,) * 4,
            name="publish",
        )(*[pltpu.with_memory_space_constraint(v, pltpu.VMEM) for v in made])

    band = P("grp", "sub")
    block = P("grp", "sub", None)
    return jax.shard_map(
        body,
        mesh=mesh,
        in_specs=(
            P(None, "sub", "grp", None),
            P(None, "sub", "grp", None),
            P("sub", "grp", None),
            band,
            block,
            band,
            band,
            block,
            P("grp", "sub", None, None),
            band,
            block,
            block,
        ),
        out_specs=(P("sub", "grp", None), P(None, "sub", "grp", None), block, band),
        check_vma=False,
    )
```

```python
import functools

import jax
import jax.numpy as jnp
import numpy as np
from jax import lax
from jax.experimental import pallas as pl
from jax.experimental.pallas import tpu as pltpu
from jax.sharding import PartitionSpec as P

MESH = pl.DeviceIdType.MESH
F32 = jnp.float32
BF16 = jnp.bfloat16
I32 = jnp.int32

STEPS = 2
CY = 384
CAP = 16
SHIFT = 4.0

FLOW = [
    (0, 0, 0),
    (1, 0, 0),
    (-1, 0, 0),
    (0, 1, 0),
    (0, -1, 0),
    (0, 0, 1),
    (0, 0, -1),
    (1, 1, 0),
    (-1, -1, 0),
    (1, -1, 0),
    (-1, 1, 0),
    (1, 0, 1),
    (-1, 0, -1),
    (1, 0, -1),
    (-1, 0, 1),
    (0, 1, 1),
    (0, -1, -1),
    (0, 1, -1),
    (0, -1, 1),
]
EVERY = FLOW + FLOW[:7]
WEIGHT = [1.0 / 3.0] + [1.0 / 18.0] * 6 + [1.0 / 36.0] * 12
HEAT_WEIGHT = [0.25] + [0.125] * 6
TAU_FLOW = 0.8
TAU_HEAT = 0.7

X_UP = [i for i, e in enumerate(EVERY) if e[0] == 1]
X_DOWN = [i for i, e in enumerate(EVERY) if e[0] == -1]
Z_UP = [i for i, e in enumerate(EVERY) if e[2] == 1]
Z_DOWN = [i for i, e in enumerate(EVERY) if e[2] == -1]
EDGES = [
    next(i for i, e in enumerate(FLOW) if e == (1, 0, 1)),
    next(i for i, e in enumerate(FLOW) if e == (-1, 0, 1)),
    next(i for i, e in enumerate(FLOW) if e == (1, 0, -1)),
    next(i for i, e in enumerate(FLOW) if e == (-1, 0, -1)),
]


def dot(a, b, dims):
    return lax.dot_general(a, b, (dims, ((), ())), preferred_element_type=F32)


def parts3(v):
    a = v.astype(BF16).astype(F32)
    rest = v - a
    b = rest.astype(BF16).astype(F32)
    return a, b, rest - b


def iota(shape, dim):
    return lax.broadcasted_iota(I32, shape, dim)


def total(v):
    return jnp.sum(jnp.sum(v, axis=1, keepdims=True), axis=0, keepdims=True)


def kernel(
    groups,
    bands,
    pops_ref,
    heat_ref,
    solid_ref,
    voxel_ref,
    dest_ref,
    coeff_ref,
    slot_ref,
    diag_ref,
    coup_ref,
    pat_ref,
    source_ref,
    start_ref,
    temp_out,
    motion_out,
    solid_out,
    rows_out,
    cur,
    post,
    zs,
    zr,
    xs,
    xr,
    er,
    chop,
    cthop,
    lohot,
    lohot_t,
    xh_s,
    xh_r,
    vel,
    coup,
    mask,
    place,
    dhot,
    lo_vox,
    ecode,
    fcode,
    laid_out,
    block_out,
    block_in,
    landed,
    returned,
    received,
    mom_s,
    mom_r,
    tot,
    rtot,
    halo_send,
    halo_recv,
    strip_send,
    strip_recv,
    band_send,
    band_recv,
    block_send,
    block_recv,
    heat_send,
    heat_recv,
    coup_sem,
    mom_send,
    mom_recv,
    ready,
):
    subs = groups * 8
    gi = lax.axis_index("grp")
    si = lax.axis_index("sub")
    g = si // 8
    j = si % 8
    g_up = lax.rem(gi + 1, bands)
    g_dn = lax.rem(gi + bands - 1, bands)
    s_up = lax.rem(si + 1, subs)
    s_dn = lax.rem(si + subs - 1, subs)

    fetch = pltpu.make_async_copy(coup_ref.at[0], coup, coup_sem)
    fetch.start()
    barrier = pltpu.get_barrier_semaphore()

    def greet(a, b):
        pl.semaphore_signal(barrier, inc=1, device_id=(a, b), device_id_type=MESH)

    for a, b in (
        (gi, s_up),
        (gi, s_dn),
        (g_up, si),
        (g_dn, si),
        (g_up, s_up),
        (g_up, s_dn),
        (g_dn, s_up),
        (g_dn, s_dn),
    ):
        greet(a, b)

    def tell(n):
        d = 1 << n
        to = [(gi, lax.rem(si + d, subs)), (gi, lax.rem(si + subs - d, subs))]
        if 2 * d < bands:
            to += [(lax.rem(gi + d, bands), si), (lax.rem(gi + bands - d, bands), si)]
        for a, b in to:
            pl.semaphore_signal(ready.at[n], inc=1, device_id=(a, b), device_id_type=MESH)

    def hear(n):
        pl.semaphore_wait(ready.at[n], 4 if 2 << n < bands else 2)

    sub8 = iota((8, 128), 0)
    lane = iota((64, 128), 1)
    xs[:, :, 8:16] = jnp.zeros((STEPS, 2, 8, CY), F32)
    xh_s[...] = jnp.zeros((2, 8, CY), F32)

    def slot_tables():
        a_of = iota((128, 2048), 0)
        spread = jnp.where(a_of == iota((128, 2048), 1) // 128, 1.0, 0.0).astype(BF16)
        slots = slot_ref[...]
        rolled = [slots] + [pltpu.roll(slots, 128 - 16 * a, 1) for a in range(1, 8)]
        slots = jnp.concatenate(rolled, axis=0)
        slot_hi = (slots // 128).astype(F32).astype(BF16)
        slot_lo = (slots % 128).astype(F32).astype(BF16)
        hi_all = dot(slot_hi, spread, ((1,), (0,)))
        lo_all = dot(slot_lo, spread, ((1,), (0,)))
        for k in range(16):
            cols = slice(k * 128, (k + 1) * 128)
            rows = pl.ds(k * 64, 64)
            lohot[rows, :] = jnp.where(lo_all[:, cols] == lane.astype(F32), 1.0, 0.0).astype(BF16)
            lohot_t[:, k * 64 : (k + 1) * 64] = (
                jnp.where(lo_all[:, cols] == lane.astype(F32), 1.0, 0.0).T.astype(BF16)
            )
            mask[rows, :] = jnp.where(hi_all[:, cols] == (lane % 8).astype(F32), 1.0, 0.0)

    def row_tables():
        dest = dest_ref[...]
        dest_hot = jnp.where(iota((64, 512), 0) == dest, 1.0, 0.0)
        dhot[...] = dest_hot.astype(BF16)
        ahead = jnp.where(iota((512, 512), 0) < iota((512, 512), 1), 1.0, 0.0).astype(BF16)
        counts = dot(dest_hot.astype(BF16), ahead, ((1,), (0,)))
        at = jnp.sum(dest_hot * counts, axis=0, keepdims=True)
        place[...] = jnp.where((iota((128, 512), 0) % 16).astype(F32) == at, 1.0, 0.0)

    def code_tables():
        wide = 16 * 128
        a_of = iota((128, wide), 0)
        c_of = iota((128, wide), 1)
        k_of = c_of // 128
        lane_of = c_of % 128
        p_of = lane_of // 32
        t_of = (lane_of // 8) % 4
        ecode[...] = jnp.where(
            (a_of == p_of * 32 + t_of * 16 + k_of) & (p_of < 3) & (t_of < 2), 1.0, 0.0
        ).astype(BF16)
        c_of = iota((wide, 128), 0)
        l_of = iota((wide, 128), 1)
        k_of = c_of // 128
        lane_of = c_of % 128
        p_of = lane_of // 32
        t_of = (lane_of // 8) % 4
        fcode[...] = jnp.where((l_of == t_of * 16 + k_of) & (p_of < 3) & (t_of < 3), 1.0, 0.0).astype(
            BF16
        )

    def coupling_tables():
        for b in range(8):
            block = coup[b]
            high = block.astype(BF16).astype(F32)
            low = block - high
            rows = pl.ds(b * 128, 128)
            chop[rows, 0:128] = high.astype(BF16)
            chop[rows, 128:256] = low.astype(BF16)
            cthop[rows, 0:128] = high.T.astype(BF16)
            cthop[rows, 128:256] = low.T.astype(BF16)

    voxel = voxel_ref[...]
    lo_vox[...] = jnp.where(iota((128, 512), 0) == voxel % 128, 1.0, 0.0).astype(BF16)
    over = voxel // 128
    layer_x = over // 3
    vox_row = (over - layer_x * 3) * 16 + layer_x

    pat = [pat_ref[0, b] for b in range(8)]
    pat_col = jnp.zeros((8, 128), I32)
    for b in range(8):
        pat_col = jnp.where(sub8 == b, pat[b], pat_col)

    def block_dot(v, table):
        high = v.astype(BF16).astype(F32)
        low = v - high
        left = jnp.concatenate([jnp.where(sub8 == b, high, 0.0) for b in range(8)], axis=1)
        right = jnp.concatenate([jnp.where(sub8 == b, low, 0.0) for b in range(8)], axis=1)
        both = jnp.concatenate([left, right], axis=0).astype(BF16)
        out = dot(both, table[...], ((1,), (0,)))
        return out[0:8, 0:128] + out[8:16, 0:128] + out[0:8, 128:256]

    def by_partner(v):
        partner = jnp.zeros((8, 128), F32)
        for k in range(8):
            partner = jnp.where(pat_col == k, v[k : k + 1, :], partner)
        return block_dot(partner, cthop)

    def off_diagonal(v):
        forward = by_partner(v)
        terms = block_dot(v, chop)
        backward = jnp.zeros((8, 128), F32)
        for b in range(8):
            backward = backward + jnp.where(sub8 == pat[b], terms[b : b + 1, :], 0.0)
        return forward + backward

    def collide(step, part):
        for z in range(2):
            for c in range(3):
                cols = slice(c * 128, (c + 1) * 128)
                if step == 0:
                    f = [pops_ref[i, z, :, cols] for i in range(19)]
                    heat = [heat_ref[i, z, :, cols] for i in range(7)]
                else:
                    f = [cur[i, z, :, cols] for i in range(19)]
                    heat = [cur[19 + i, z, :, cols] for i in range(7)]
                if part == "flow":
                    rho = vel[3, z, :, cols]
                    u = [vel[d, z, :, cols] for d in range(3)]
                else:
                    rho = functools.reduce(jnp.add, f)
                    m = []
                    for d in range(3):
                        pos = [f[i] for i in range(19) if FLOW[i][d] == 1]
                        neg = [f[i] for i in range(19) if FLOW[i][d] == -1]
                        m.append(functools.reduce(jnp.add, pos) - functools.reduce(jnp.add, neg))
                    u = [v / rho for v in m]
                if part == "heat":
                    vel[3, z, :, cols] = rho
                    for d in range(3):
                        vel[d, z, :, cols] = u[d]
                out = [None] * 26
                if part != "heat":
                    solid = solid_ref[z, :, cols]
                    flat = 1.0 - 1.5 * (u[0] * u[0] + u[1] * u[1] + u[2] * u[2])
                    fluid = 1.0 - solid
                    keep = fluid * (1.0 - 1.0 / TAU_FLOW)
                    gain = fluid * rho * (1.0 / TAU_FLOW)
                    out[0] = (keep + solid) * f[0] + gain * WEIGHT[0] * flat
                    for i in range(1, 19, 2):
                        along = None
                        for d in range(3):
                            if FLOW[i][d] == 1:
                                along = u[d] if along is None else along + u[d]
                            elif FLOW[i][d] == -1:
                                along = -u[d] if along is None else along - u[d]
                        even = flat + 4.5 * along * along
                        odd = 3.0 * along
                        scale = gain * WEIGHT[i]
                        out[i] = keep * f[i] + solid * f[i + 1] + scale * (even + odd)
                        out[i + 1] = keep * f[i + 1] + solid * f[i] + scale * (even - odd)
                if part != "flow":
                    hot = functools.reduce(jnp.add, heat)
                    for i in range(7):
                        share = hot * (HEAT_WEIGHT[i] / TAU_HEAT)
                        if i > 0:
                            d = [abs(v) for v in FLOW[i]].index(1)
                            sign = FLOW[i][d]
                            share = share * (1.0 + (4.0 * sign) * u[d])
                        out[19 + i] = (1.0 - 1.0 / TAU_HEAT) * heat[i] + share
                for i in range(26):
                    if out[i] is None:
                        continue
                    ex, ez = EVERY[i][0], EVERY[i][2]
                    post[i, z, :, cols] = out[i]
                    if ez == 1 and z == 1:
                        zs[step, 0, Z_UP.index(i), :, cols] = out[i]
                    if ez == -1 and z == 0:
                        zs[step, 1, Z_DOWN.index(i), :, cols] = out[i]
                    if ex == 0:
                        continue
                    way = 0 if ex == 1 else 1
                    row = out[i][7:8, :] if ex == 1 else out[i][0:1, :]
                    if step == 1 and i >= 19:
                        xh_s[way, z : z + 1, cols] = row
                    else:
                        r = (X_UP if ex == 1 else X_DOWN).index(i) * 2 + z
                        xs[step, way, r : r + 1, cols] = row

    def halo(step):
        made = []

        def put(n, src, dst, a, b):
            made.append(
                pltpu.make_async_remote_copy(
                    src_ref=src,
                    dst_ref=dst,
                    send_sem=halo_send.at[step, n],
                    recv_sem=halo_recv.at[step, n],
                    device_id=(a, b),
                    device_id_type=MESH,
                )
            )

        put(0, zs.at[step, 0, Z_UP.index(EDGES[0])], er.at[step, 0], g_up, s_up)
        put(1, zs.at[step, 0, Z_UP.index(EDGES[1])], er.at[step, 1], g_dn, s_up)
        put(2, zs.at[step, 1, Z_DOWN.index(EDGES[2])], er.at[step, 2], g_up, s_dn)
        put(3, zs.at[step, 1, Z_DOWN.index(EDGES[3])], er.at[step, 3], g_dn, s_dn)
        put(4, xs.at[step, 0], xr.at[step, 0], g_up, si)
        put(5, xs.at[step, 1], xr.at[step, 1], g_dn, si)
        count = 6 if step == 0 else 5
        put(6, zs.at[step, 0, 0:count], zr.at[step, 0, 0:count], gi, s_up)
        put(7, zs.at[step, 1, 0:count], zr.at[step, 1, 0:count], gi, s_dn)
        return made

    def heat_halo():
        pairs = (
            (xh_s.at[0], xh_r.at[0], g_up, si),
            (xh_s.at[1], xh_r.at[1], g_dn, si),
            (zs.at[1, 0, 5], zr.at[1, 0, 5], gi, s_up),
            (zs.at[1, 1, 5], zr.at[1, 1, 5], gi, s_dn),
        )
        return [
            pltpu.make_async_remote_copy(
                src_ref=src,
                dst_ref=dst,
                send_sem=heat_send.at[n],
                recv_sem=heat_recv.at[n],
                device_id=(a, b),
                device_id_type=MESH,
            )
            for n, (src, dst, a, b) in enumerate(pairs)
        ]

    edge8 = iota((8, CY), 0)

    def stream(step, arrived, which=range(26)):
        for i in which:
            ex, ey, ez = EVERY[i]
            for z in range(2):
                edge = None
                inside = ez == 0 or z == (1 if ez == 1 else 0)
                if arrived == (inside and ex == 0):
                    continue
                if ez == 0 or (ez == 1 and z == 1) or (ez == -1 and z == 0):
                    source = z - ez
                    piece = post[i, source]
                    if ex != 0:
                        way = 0 if ex == 1 else 1
                        if step == 1 and i >= 19:
                            edge = xh_r[way, source : source + 1, :]
                        else:
                            r = (X_UP if ex == 1 else X_DOWN).index(i) * 2 + source
                            edge = xr[step, way, r : r + 1, :]
                else:
                    if ez == 1:
                        piece = zr[step, 0, Z_UP.index(i)]
                    else:
                        piece = zr[step, 1, Z_DOWN.index(i)]
                    if ex == 1:
                        edge = er[step, EDGES.index(i), 7:8, :]
                    if ex == -1:
                        edge = er[step, EDGES.index(i), 0:1, :]
                if ex == 1:
                    piece = jnp.where(edge8 == 0, edge, pltpu.roll(piece, 1, 0))
                if ex == -1:
                    piece = jnp.where(edge8 == 7, edge, pltpu.roll(piece, 7, 0))
                if ey == 1:
                    piece = pltpu.roll(piece, 1, 1)
                if ey == -1:
                    piece = pltpu.roll(piece, CY - 1, 1)
                cur[i, z] = piece

    collide(0, "all")
    pl.semaphore_wait(barrier, 8)
    made = halo(0)
    for c in made:
        c.start()
    tell(0)
    stream(0, False)
    hear(0)
    tell(1)
    row_tables()
    hear(1)
    tell(2)
    slot_tables()
    hear(2)
    tell(3)
    fetch.wait()
    coupling_tables()
    for c in made:
        c.wait_recv()
    stream(0, True)
    collide(1, "heat")
    warm = heat_halo()
    for c in warm:
        c.start()
    collide(1, "flow")
    made = halo(1)
    for c in made:
        c.start()
    stream(1, False, range(19, 26))
    stream(1, False, range(19))
    code_tables()
    x0 = start_ref[0]
    fixed = source_ref[0] + off_diagonal(x0)
    diag = diag_ref[0]
    for c in warm:
        c.wait_recv()
    stream(1, True, range(19, 26))

    hot_rows = []
    for z in range(2):
        hot = functools.reduce(jnp.add, [cur[19 + i, z] for i in range(7)])
        temp_out[z] = hot
        hot_rows.append(hot)

    table = jnp.concatenate(
        [hot_rows[z][:, c * 128 : (c + 1) * 128] for c in range(3) for z in range(2)], axis=0
    )
    picked = dot(
        jnp.concatenate(parts3(table), axis=0).astype(BF16), lo_vox[...], ((1,), (0,))
    )
    picked = picked[0:48] + picked[48:96] + picked[96:144]
    seen = jnp.sum(jnp.where(iota((48, 512), 0) == vox_row, picked, 0.0), axis=0, keepdims=True)
    coeff = coeff_ref[...]
    flux = coeff * seen
    placed = place[0:16, :]
    laid = []
    for pair in zip(parts3(flux), parts3(coeff)):
        laid.append(placed * pair[0])
        laid.append(placed * pair[1])
    laid.append(jnp.zeros((32, 512), F32))
    laid = jnp.concatenate(laid, axis=0).astype(BF16)
    sent = dot(dhot[...], laid, ((1,), (1,)))
    sent = sent + pltpu.roll(sent, 96, 1) + pltpu.roll(sent, 64, 1)
    laid_out[...] = sent.reshape(64, 1, 128)

    half = subs // 4

    def landing(source):
        return landed.at[(source % 8) * groups + source // 8]

    def row_copy(src, source, to):
        return pltpu.make_async_remote_copy(
            src_ref=src,
            dst_ref=landing(source),
            send_sem=strip_send.at[0],
            recv_sem=strip_recv.at[0],
            device_id=(gi, to),
            device_id_type=MESH,
        )

    for e in range(1, half + 1):
        block_out[0, e - 1] = laid_out[lax.rem(si + half + e, subs)]
        block_out[1, e - 1] = laid_out[lax.rem(si + subs - half - e, subs)]

    def block_copy(way):
        to = lax.rem(si + (half if way == 0 else subs - half), subs)
        return pltpu.make_async_remote_copy(
            src_ref=block_out.at[way],
            dst_ref=block_in.at[way],
            send_sem=block_send.at[way],
            recv_sem=block_recv.at[way],
            device_id=(gi, to),
            device_id_type=MESH,
        )

    hear(3)
    block_copy(0).start()
    block_copy(1).start()

    def near(i, carry):
        d = (half - i // 2) * (1 - 2 * (i % 2))
        to = lax.rem(si + subs + d, subs)
        row_copy(laid_out.at[to], si, to).start()
        return carry

    lax.fori_loop(0, 2 * half, near, 0)
    landed[j * groups + g] = laid_out[si]

    for c in made:
        c.wait_recv()
    stream(1, True, range(19))
    for z in range(2):
        for d in range(3):
            pos = [cur[i, z] for i in range(19) if FLOW[i][d] == 1]
            neg = [cur[i, z] for i in range(19) if FLOW[i][d] == -1]
            motion_out[d, z] = functools.reduce(jnp.add, pos) - functools.reduce(jnp.add, neg)

    early = si // (subs // 2)
    for way in (early, 1 - early):
        pltpu.make_async_copy(block_out.at[way], block_in.at[way], block_recv.at[way]).wait()
        sign = 1 - 2 * way
        source = lax.rem(si + subs - sign * half, subs)

        def forward(e, way=way, sign=sign, source=source):
            to = lax.rem(si + subs + sign * e, subs)
            row_copy(block_in.at[way, e - 1], source, to).start()

        @pl.when(way == 0)
        def _(forward=forward):
            forward(half)

        def forward_all(i, carry, forward=forward):
            forward(half - 1 - i)
            return carry

        lax.fori_loop(0, half - 1, forward_all, 0)

    def back_copy(i):
        to = far_first(i)
        return pltpu.make_async_remote_copy(
            src_ref=returned.at[(to % 8) * groups + to // 8],
            dst_ref=received.at[si],
            send_sem=strip_send.at[1],
            recv_sem=strip_recv.at[1],
            device_id=(gi, to),
            device_id_type=MESH,
        )

    def back_go(i, carry):
        back_copy(i).start()
        return carry

    def strip_all(way, sem):
        src, dst = (laid_out, landed) if way == 0 else (returned, received)
        rest = pl.ds(0, subs - 1)
        return pltpu.make_async_copy(src.at[rest], dst.at[rest], sem.at[way])

    strip_all(0, strip_recv).wait()

    got = landed[...].reshape(64, 128)
    in_flux = jnp.where(lane < 32, got, 0.0)
    p0, p1, p2 = parts3(in_flux)
    coded = (p0 + pltpu.roll(p1, 32, 1) + pltpu.roll(p2, 64, 1)).astype(BF16)
    values = dot(coded, ecode[...], ((1,), (0,)))
    values = jnp.concatenate([values[:, k * 128 : (k + 1) * 128] for k in range(16)], axis=0)
    values = (values * mask[...]).astype(BF16)
    summed = dot(lohot_t[...], values, ((1,), (0,))).T
    add_source = summed[0:8] + summed[32:40] + summed[64:72]
    add_diag = summed[8:16] + summed[40:48] + summed[72:80]

    diag = diag + add_diag
    r0 = fixed + add_source - diag * x0
    w1 = (diag - SHIFT) * r0 - off_diagonal(r0)
    last = (diag - SHIFT) * w1 - 2.0 * by_partner(w1)
    sums = [total(r0 * r0), total(r0 * w1), total(w1 * w1), total(w1 * last)]

    lane1 = iota((1, 128), 1)
    line = jnp.zeros((1, 128), F32)
    for n in range(4):
        line = jnp.where(lane1 == 48 + n, sums[n], line)
    mom_s[...] = line

    def far_first(i):
        d = subs // 2 + (1 - 2 * (i % 2)) * ((i + 1) // 2)
        return lax.rem(si + d, subs)

    def mom_go(i, carry):
        pltpu.make_async_remote_copy(
            src_ref=mom_s,
            dst_ref=mom_r.at[si],
            send_sem=mom_send,
            recv_sem=mom_recv,
            device_id=(gi, far_first(i)),
            device_id_type=MESH,
        ).start()
        return carry

    lax.fori_loop(0, subs - 1, mom_go, 0)
    mom_r[si] = line

    def mom_all(sem):
        rest = pl.ds(0, subs - 1)
        return pltpu.make_async_copy(landed.at[rest], mom_r.at[rest], sem)

    held = jnp.concatenate([x0, r0, w1, jnp.zeros((8, 128), F32)], axis=0)
    held = jnp.concatenate(list(parts3(held)) + [jnp.zeros((32, 128), F32)], axis=0).astype(BF16)
    found = dot(lohot[...], held, ((1,), (1,)))
    found = (found * mask[...]).astype(BF16)
    found = jnp.concatenate([found[k * 64 : (k + 1) * 64, :] for k in range(16)], axis=1)
    found = dot(found, fcode[...], ((1,), (0,)))
    returned[...] = found.reshape(64, 1, 128)
    lax.fori_loop(0, subs - 1, back_go, 0)
    received[si] = returned[j * groups + g]
    mom_all(mom_recv).wait()
    tot[...] = jnp.sum(mom_r[...].reshape(64, 128), axis=0, keepdims=True)

    def band_copy(i):
        return pltpu.make_async_remote_copy(
            src_ref=tot,
            dst_ref=rtot.at[gi],
            send_sem=band_send,
            recv_sem=band_recv,
            device_id=(lax.rem(gi + bands // 2 + (1 - 2 * (i % 2)) * ((i + 1) // 2), bands), si),
            device_id_type=MESH,
        )

    def band_go(i, carry):
        band_copy(i).start()
        return carry

    lax.fori_loop(0, bands - 1, band_go, 0)

    def band_all(sem):
        rest = pl.ds(0, bands - 1)
        return pltpu.make_async_copy(laid_out.at[rest], rtot.at[rest], sem)

    strip_all(1, strip_recv).wait()
    back = received[...].reshape(64, 128)
    rows = functools.reduce(
        jnp.add, [dot(p.astype(BF16), dhot[...], ((0,), (0,))) for p in parts3(back)]
    )
    rows = rows * place[...]
    row_x0 = jnp.sum(rows[0:16], axis=0, keepdims=True)
    row_r0 = jnp.sum(rows[16:32], axis=0, keepdims=True)
    row_w1 = jnp.sum(rows[32:48], axis=0, keepdims=True)

    rtot[gi] = tot[...]

    band_all(band_recv).wait()
    whole = functools.reduce(jnp.add, [rtot[n] for n in range(bands)])

    def lane_value(n):
        return jnp.sum(jnp.where(lane1 == 48 + n, whole, 0.0), axis=1, keepdims=True)

    n0, n1, n2, n3 = [lane_value(n) for n in range(4)]
    delta = n1 / n0
    second = n2 / n0
    spread_of = second - delta * delta
    theta = SHIFT + delta
    third = n3 / n0 - 3.0 * delta * second + 2.0 * delta * delta * delta
    wide_enough = spread_of > 1e-7 * theta * theta
    spread_of = jnp.maximum(spread_of, 0.0)
    skew = jnp.where(wide_enough, third / jnp.where(wide_enough, spread_of, 1.0), 0.0)
    step0 = 1.0 / theta
    growth = spread_of / (theta * theta)
    step1 = 1.0 / (theta + skew - spread_of / theta)
    by_r0 = step0 + step1 * (growth + step0 * delta)
    by_w1 = -step1 * step0
    solid_out[0] = x0 + by_r0 * r0 + by_w1 * w1
    rows_out[...] = row_x0 + by_r0 * row_r0 + by_w1 * row_w1

    for step in range(STEPS):
        for c in halo(step):
            c.wait_send()
    for c in warm:
        c.wait_send()
    block_copy(0).wait_send()
    block_copy(1).wait_send()
    strip_all(0, strip_send).wait()
    strip_all(1, strip_send).wait()
    band_all(band_send).wait()
    mom_all(mom_send).wait()


def publish(*refs):
    for source, target in zip(refs[:4], refs[4:]):
        target[...] = source[...]


def solution(mesh):
    bands = mesh.shape["grp"]
    subs = mesh.shape["sub"]
    groups = subs // 8

    def body(
        populations,
        heat_pops,
        solid_frac,
        coupled_grid_point,
        dest_index,
        heat_coeff,
        slot_node,
        node_diag,
        coupling,
        block_pattern,
        heat_source,
        solid_start,
    ):
        vmem = pl.BlockSpec(memory_space=pltpu.VMEM)
        smem = pl.BlockSpec(memory_space=pltpu.SMEM)
        dma = pltpu.SemaphoreType.DMA
        shapes = (
                jax.ShapeDtypeStruct((2, 8, CY), F32),
                jax.ShapeDtypeStruct((3, 2, 8, CY), F32),
                jax.ShapeDtypeStruct((1, 8, 128), F32),
                jax.ShapeDtypeStruct((1, 512), F32),
            )
        made = pl.pallas_call(
            functools.partial(kernel, groups, bands),
            out_shape=tuple(pltpu.VMEM(v.shape, v.dtype) for v in shapes),
            in_specs=[vmem] * 8 + [pl.BlockSpec(memory_space=pl.ANY), smem] + [vmem] * 2,
            out_specs=(vmem,) * 4,
            scratch_shapes=[
                pltpu.VMEM((26, 2, 8, CY), F32),
                pltpu.VMEM((26, 2, 8, CY), F32),
                pltpu.VMEM((STEPS, 2, 6, 8, CY), F32),
                pltpu.VMEM((STEPS, 2, 6, 8, CY), F32),
                pltpu.VMEM((STEPS, 2, 16, CY), F32),
                pltpu.VMEM((STEPS, 2, 16, CY), F32),
                pltpu.VMEM((STEPS, 4, 8, CY), F32),
                pltpu.VMEM((1024, 256), BF16),
                pltpu.VMEM((1024, 256), BF16),
                pltpu.VMEM((1024, 128), BF16),
                pltpu.VMEM((128, 1024), BF16),
                *[pltpu.VMEM((2, 8, CY), F32)] * 2,
                pltpu.VMEM((4, 2, 8, CY), F32),
                pltpu.VMEM((8, 128, 128), F32),
                pltpu.VMEM((1024, 128), F32),
                pltpu.VMEM((128, 512), F32),
                pltpu.VMEM((64, 512), BF16),
                pltpu.VMEM((128, 512), BF16),
                pltpu.VMEM((128, 2048), BF16),
                pltpu.VMEM((2048, 128), BF16),
                pltpu.VMEM((64, 1, 128), F32),
                *[pltpu.VMEM((2, 16, 1, 128), F32)] * 2,
                *[pltpu.VMEM((64, 1, 128), F32)] * 3,
                pltpu.VMEM((1, 128), F32),
                pltpu.VMEM((64, 1, 128), F32),
                pltpu.VMEM((1, 128), F32),
                pltpu.VMEM((bands, 1, 128), F32),
                dma((STEPS, 8)),
                dma((STEPS, 8)),
                dma((2,)),
                dma((2,)),
                dma,
                dma,
                dma((2,)),
                dma((2,)),
                dma((4,)),
                dma((4,)),
                dma,
                dma,
                dma,
                pltpu.SemaphoreType.REGULAR((4,)),
            ],
            compiler_params=pltpu.CompilerParams(collective_id=0, has_side_effects=True),
            name="coupled_step",
        )(
            populations,
            heat_pops,
            solid_frac,
            coupled_grid_point,
            dest_index[..., 0],
            heat_coeff,
            slot_node.reshape(8, 128),
            node_diag,
            coupling,
            block_pattern,
            heat_source,
            solid_start,
        )
        return pl.pallas_call(
            publish,
            out_shape=shapes,
            in_specs=[vmem] * 4,
            out_specs=(vmem,) * 4,
            name="publish",
        )(*[pltpu.with_memory_space_constraint(v, pltpu.VMEM) for v in made])

    band = P("grp", "sub")
    block = P("grp", "sub", None)
    return jax.shard_map(
        body,
        mesh=mesh,
        in_specs=(
            P(None, "sub", "grp", None),
            P(None, "sub", "grp", None),
            P("sub", "grp", None),
            band,
            block,
            band,
            band,
            block,
            P("grp", "sub", None, None),
            band,
            block,
            block,
        ),
        out_specs=(P("sub", "grp", None), P(None, "sub", "grp", None), block, band),
        check_vma=False,
    )
```
